32 devices in a mesh: strip: 8 (over y, x, core), vec: 4 (over z).
Axes of the slice: x: 2, y: 2, z: 4, core: 2. Of those that a mesh axis runs over, the one named last changes fastest.
Arguments:
- start_vectors: float32 [64, 256, 1024], P('vec', 'strip'), may hold values from -40 to 40
- potential: int32 [256, 1024], P('strip'), may hold values from 0 to 15
- bounds: int32 [4], replicated, may hold values from -96 to 96, as said below
Outputs:
- ortho_basis: float32 [64, 256, 1024], P('vec', 'strip')
- ritz_matrix: float32 [64, 64], replicated
The draws below stay inside these ranges and needn't reach their ends.
Inputs may be any that keep to these rules, and one draw needn't show every extreme that they name: bounds[0] and bounds[1] enclose the spectrum of H: bounds[0] is at most -84 and bounds[1] at least 84; bounds[0] < bounds[2] < bounds[3] < bounds[1].
All inputs are finite; a program needn't handle non-finite values.
Results may differ from the reference program's by a relative error of at most 0.00021.
Values sent between devices are 32-bit elements; how exact they have to be, the bound alone decides.
No kernel may reach another device: no remote copies, remote signals or barrier semaphores. Data moves between devices by JAX's collectives and lax.ppermute only.
A program may use at most 64 MiB of HBM per device.

```python
import math
import jax
import jax.numpy as jnp
from jax import lax

NVEC = 64
ROWS_DEV = 32
LY = 1024
DEGREE = 32
POT_LEVELS = 16
LX = 256
SITES = 262144


def draw_start_vectors(key, part):
    first_key = jax.random.fold_in(jax.random.fold_in(key, 11), 0)
    base = jax.random.truncated_normal(first_key, -4.0, 4.0, (NVEC, LX, LY), jnp.float32)
    mixed = base + 0.5 * jnp.roll(base, -1, 0) + 0.3 * jnp.roll(base, -7, 0)
    row_scale = 3.0 ** (jnp.arange(LX).astype(jnp.float32) / max(LX - 1, 1))
    return (mixed * row_scale[None, :, None]).astype(jnp.float32)


def draw_bounds(key, part):
    base_key = jax.random.fold_in(key, 23)
    keys = jax.random.split(base_key, 4)
    enclose_lo = jax.random.randint(keys[0], (), -96, -83)
    enclose_hi = jax.random.randint(keys[1], (), 84, 97)
    window_lo = jax.random.randint(keys[2], (), -40, -8)
    window_hi = window_lo + jax.random.randint(keys[3], (), 16, 49)
    return jnp.stack([enclose_lo, enclose_hi, window_lo, window_hi]).astype(jnp.int32)


def plant(entries, rng, least, high):
    longest = entries.shape.index(max(entries.shape))
    spots = []
    for shift in (0, 1):
        where = [jax.random.randint(jax.random.fold_in(rng, axis), (), 0, length) for axis, length in enumerate(entries.shape)]
        where[longest] = (where[longest] + shift) % entries.shape[longest]
        spots.append(tuple(where))
    return entries.at[spots[0]].set(least).at[spots[1]].set(high)


def setup_inputs(seed: int = 0) -> dict:
    arg_keys = jax.random.split(jax.random.key(seed), 4)
    return {
        "start_vectors": draw_start_vectors(jax.random.fold_in(arg_keys[3], 71), 0),
        "potential": plant(jax.random.randint(arg_keys[1], (LX, LY), 0, POT_LEVELS), jax.random.fold_in(arg_keys[1], 1), 0, POT_LEVELS - 1).astype(jnp.int32),
        "bounds": draw_bounds(jax.random.fold_in(arg_keys[3], 71), 0),
    }


grid_unit = 0.0625
disorder = 2.0

def filter_terms(bounds):
    edges = bounds.astype(jnp.float32) * grid_unit
    center = (edges[0] + edges[1]) * 0.5
    spread = (edges[1] - edges[0]) * 0.5
    theta_lo = jnp.arccos((edges[2] - center) / spread)
    theta_hi = jnp.arccos((edges[3] - center) / spread)
    orders = jnp.arange(1, DEGREE + 1).astype(jnp.float32)
    others = 2.0 * (jnp.sin(orders * theta_lo) - jnp.sin(orders * theta_hi)) / (orders * math.pi)
    first = jnp.reshape((theta_lo - theta_hi) / math.pi, (1,))
    return (jnp.concatenate([first, others]), center, spread)

def hamiltonian(field, pot_field):
    beside = jnp.roll(field, 1, 1) + jnp.roll(field, -1, 1) + jnp.roll(field, 1, 2) + jnp.roll(field, -1, 2)
    return pot_field[None] * field - beside

def reference(start_vectors, potential, bounds):
    pot_field = disorder * (potential.astype(jnp.float32) / (POT_LEVELS - 1) - 0.5)
    coeffs, center, spread = filter_terms(bounds)

    def scaled(field):
        return (hamiltonian(field, pot_field) - center * field) / spread
    before = start_vectors
    current = scaled(start_vectors)
    filtered = coeffs[0] * before + coeffs[1] * current

    def advance(counter, carry):
        before, current, filtered = carry
        after = 2.0 * scaled(current) - before
        filtered = filtered + coeffs[counter + 1] * after
        return (current, after, filtered)
    before, current, filtered = lax.fori_loop(1, DEGREE, advance, (before, current, filtered))
    applied = hamiltonian(filtered, pot_field)
    y_rows = filtered.reshape(NVEC, -1)
    hy_rows = applied.reshape(NVEC, -1)
    gram_sum = jnp.dot(y_rows.astype(jnp.float32), y_rows.T.astype(jnp.float32), precision=lax.Precision.HIGHEST, preferred_element_type=jnp.float32)
    cross_sum = jnp.dot(y_rows.astype(jnp.float32), hy_rows.T.astype(jnp.float32), precision=lax.Precision.HIGHEST, preferred_element_type=jnp.float32)
    lower_factor = jnp.linalg.cholesky(gram_sum)
    ortho = jax.scipy.linalg.solve_triangular(lower_factor, y_rows, lower=True)
    ortho_basis = (math.sqrt(SITES) * ortho).reshape(NVEC, LX, LY)
    half_done = jax.scipy.linalg.solve_triangular(lower_factor, cross_sum, lower=True)
    ritz_matrix = float(ROWS_DEV) * jax.scipy.linalg.solve_triangular(lower_factor, half_done.T, lower=True)
    return (ortho_basis, ritz_matrix)
```

```python
import functools
import math

import jax
import jax.numpy as jnp
from jax import lax
from jax.experimental import pallas as pl
from jax.experimental.pallas import tpu as pltpu
from jax.sharding import PartitionSpec as P

DEGREE = 32
DEPTH = 8
POT_LEVELS = 16
LANES = 128
SUBLANES = 8

grid_unit = 0.0625
disorder = 2.0


def filter_terms(bounds):
    edges = bounds.astype(jnp.float32) * grid_unit
    center = (edges[0] + edges[1]) * 0.5
    spread = (edges[1] - edges[0]) * 0.5
    theta_lo = jnp.arccos((edges[2] - center) / spread)
    theta_hi = jnp.arccos((edges[3] - center) / spread)
    orders = jnp.arange(1, DEGREE + 1).astype(jnp.float32)
    others = 2.0 * (jnp.sin(orders * theta_lo) - jnp.sin(orders * theta_hi)) / (orders * math.pi)
    first = jnp.reshape((theta_lo - theta_hi) / math.pi, (1,))
    return (jnp.concatenate([first, others]), center, spread)


def extended(value, sides, width):
    for axis, dim in sides:
        count, length = (lax.axis_size(axis), value.shape[dim])
        up = [(i, (i + 1) % count) for i in range(count)]
        down = [(j, i) for i, j in up]
        last = lax.slice_in_dim(value, length - width, length, axis=dim)
        leading = lax.slice_in_dim(value, 0, width, axis=dim)
        before = lax.ppermute(last, axis, up)
        after = lax.ppermute(leading, axis, down)
        value = jnp.concatenate([before, value, after], axis=dim)
    return value


def stencil(padded, pot_rows, center, spread):
    middle = padded[:, 1:-1]
    beside = padded[:, 2:] + padded[:, :-2] + jnp.roll(middle, 1, 2) + jnp.roll(middle, -1, 2)
    return ((pot_rows[None] - center) * middle - beside) / spread


def deep_filter(start_vectors, pot_padded, coeffs, center, spread):
    rows = start_vectors.shape[1]

    def one_round(rounds, carry):
        before, current, filtered = carry
        stacked = jnp.stack([before, current])
        padded = extended(stacked, (("strip", 2),), DEPTH)
        old_part = padded[0]
        new_part = padded[1]
        for inner in range(DEPTH):
            counter = rounds * DEPTH + inner
            factor = jnp.where(counter == 0, 1.0, 2.0).astype(jnp.float32)
            pot_rows = pot_padded[inner + 1 : rows + 2 * DEPTH - inner - 1]
            after = factor * stencil(new_part, pot_rows, center, spread) - old_part[:, 1:-1]
            offset = DEPTH - inner - 1
            filtered = filtered + coeffs[counter + 1] * after[:, offset : offset + rows]
            old_part = new_part[:, 1:-1]
            new_part = after
        return (old_part, new_part, filtered)

    initial = (jnp.zeros_like(start_vectors), start_vectors, coeffs[0] * start_vectors)
    return lax.fori_loop(0, DEGREE // DEPTH, one_round, initial)[2]


def halo_shards(start_vectors, potential, bounds):
    vec_local, rows, columns = start_vectors.shape
    pot_field = disorder * (potential.astype(jnp.float32) / (POT_LEVELS - 1) - 0.5)
    coeffs, center, spread = filter_terms(bounds)
    pot_padded = extended(pot_field, (("strip", 0),), DEPTH)
    filtered = deep_filter(start_vectors, pot_padded, coeffs, center, spread)
    padded = extended(filtered, (("strip", 1),), 1)
    applied = stencil(padded, pot_field, 0.0, 1.0)
    slab_vecs, slab_applied = (
        lax.all_to_all(filtered, "vec", split_axis=1, concat_axis=0, tiled=True),
        lax.all_to_all(applied, "vec", split_axis=1, concat_axis=0, tiled=True),
    )
    total_vecs = slab_vecs.shape[0]
    y_rows = slab_vecs.reshape(total_vecs, -1)
    hy_rows = slab_applied.reshape(total_vecs, -1)
    gram_part = jnp.dot(
        y_rows, y_rows.T, precision=lax.Precision.HIGHEST, preferred_element_type=jnp.float32
    )
    cross_part = jnp.dot(
        y_rows, hy_rows.T, precision=lax.Precision.HIGHEST, preferred_element_type=jnp.float32
    )
    gram_sum, cross_sum = lax.psum((gram_part, cross_part), ("strip", "vec"))
    lower_factor = jnp.linalg.cholesky(gram_sum)
    site_count = lax.axis_size("strip") * rows * columns
    ortho = jax.scipy.linalg.solve_triangular(lower_factor, y_rows, lower=True)
    ortho_slab = (math.sqrt(site_count) * ortho).reshape(slab_vecs.shape)
    ortho_basis = lax.all_to_all(ortho_slab, "vec", split_axis=0, concat_axis=1, tiled=True)
    half_done = jax.scipy.linalg.solve_triangular(lower_factor, cross_sum, lower=True)
    ritz_matrix = float(rows) * jax.scipy.linalg.solve_triangular(
        lower_factor, half_done.T, lower=True
    )
    return (ortho_basis, ritz_matrix)


def filter_kernel(coef_ref, vec_ref, pot_ref, out_ref, field, site, state_a, state_b, *, vecs, slabs):
    rows = field.shape[0]
    strips = field.shape[1]
    columns = field.shape[2]
    slab_rows = rows // slabs
    center = coef_ref[DEGREE + 1]
    inverse = coef_ref[DEGREE + 2]

    def stage_pot(block, carry):
        level = jnp.swapaxes(pot_ref[:, pl.ds(block * SUBLANES, SUBLANES), :], 0, 1)
        value = disorder * (level * (1.0 / (POT_LEVELS - 1)) - 0.5)
        site[pl.ds(block * SUBLANES, SUBLANES)] = (value - center) * (2.0 * inverse)
        return carry

    lax.fori_loop(0, rows // SUBLANES, stage_pot, 0)

    def sweep(new, cur, weight, scale_site, scale_hop):
        first = cur[0]
        last = cur[rows - 1]

        def line(j, above, here, below):
            beside = (pltpu.roll(here, 1, 1) + pltpu.roll(here, columns - 1, 1)) + (above + below)
            diagonal = site[j] * here if scale_site is None else (scale_site * site[j]) * here
            value = (weight * field[j] - new[j]) + (diagonal - scale_hop * beside)
            new[j] = value

        def body(j, carry):
            above, here = carry
            below = cur[j + 1]
            line(j, above, here, below)
            return (here, below)

        above, here = lax.fori_loop(
            0, rows - 1, body, (pltpu.roll(last, 1, 0), first)
        )
        line(rows - 1, above, here, pltpu.roll(first, strips - 1, 0))

    for k in range(vecs):
        top = coef_ref[DEGREE]

        def stage(block, carry):
            here = pl.ds(block * SUBLANES, SUBLANES)
            value = jnp.swapaxes(vec_ref[:, k, here, :], 0, 1)
            field[here] = value
            state_a[here] = top * value
            state_b[here] = jnp.zeros_like(value)
            return carry

        lax.fori_loop(0, rows // SUBLANES, stage, 0)

        def two(step, carry):
            order = DEGREE - 1 - 2 * step
            sweep(state_b, state_a, coef_ref[order], None, 2.0 * inverse)
            sweep(state_a, state_b, coef_ref[order - 1], None, 2.0 * inverse)
            return carry

        lax.fori_loop(0, (DEGREE - 2) // 2, two, 0)
        sweep(state_b, state_a, coef_ref[1], None, 2.0 * inverse)

        sweep(state_a, state_b, coef_ref[0], 0.5, inverse)

        def emit(slab, carry):
            for block in range(0, slab_rows, SUBLANES):
                value = state_a[pl.ds(slab * slab_rows + block, SUBLANES)]
                out_ref[slab, :, k, pl.ds(block, SUBLANES), :] = jnp.swapaxes(value, 0, 1)
            return carry

        lax.fori_loop(0, slabs, emit, 0)


def gram_kernel(slab_ref, next_ref, pot_ref, out_ref, lines_ref):
    total, slab_rows, columns = slab_ref.shape
    acc = jnp.zeros(out_ref.shape, jnp.float32)
    for vec in range(0, total, SUBLANES):
        lines_ref[:, vec : vec + SUBLANES, :] = jnp.swapaxes(slab_ref[vec : vec + SUBLANES], 0, 1)
    for j in range(slab_rows):
        here = lines_ref[j]
        below = next_ref[...] if j == slab_rows - 1 else lines_ref[j + 1]
        level = pot_ref[j : j + 1, :]
        pot = disorder * (level * (1.0 / (POT_LEVELS - 1)) - 0.5)
        image = pot * here - (pltpu.roll(here, 1, 1) + pltpu.roll(here, columns - 1, 1)) - 2.0 * below
        both = jnp.concatenate([here, image], axis=0)
        acc = acc + lax.dot_general(
            here,
            both,
            (((1,), (1,)), ((), ())),
            precision=lax.Precision.HIGHEST,
            preferred_element_type=jnp.float32,
        )
    out_ref[...] = acc


def apply_kernel(inv_ref, lines_ref, out_ref, done_ref):
    slab_rows, total, columns = lines_ref.shape
    for j in range(slab_rows):
        done_ref[j] = jnp.dot(
            inv_ref[...],
            lines_ref[j],
            precision=lax.Precision.HIGHEST,
            preferred_element_type=jnp.float32,
        )
    for vec in range(0, total, SUBLANES):
        out_ref[vec : vec + SUBLANES] = jnp.swapaxes(done_ref[:, vec : vec + SUBLANES, :], 0, 1)


def whole_shards(start_vectors, potential, bounds):
    vec_local, rows, columns = start_vectors.shape
    strips = lax.axis_size("strip")
    groups = lax.axis_size("vec")
    both = ("vec", "strip")
    total_vecs = vec_local * groups
    vecs = vec_local // strips
    slab_rows = rows // groups
    devices = strips * groups

    coeffs, center, spread = filter_terms(bounds)
    terms = jnp.concatenate([coeffs, center[None], (1.0 / spread)[None]])
    level = potential.astype(jnp.float32)
    whole_pot = lax.all_to_all(
        jnp.broadcast_to(level[None], (strips, rows, columns)), "strip", split_axis=0, concat_axis=0, tiled=True
    )
    whole_vecs = lax.all_to_all(start_vectors, "strip", split_axis=0, concat_axis=0, tiled=True)
    lattice = (rows, strips, columns)
    vmem = pl.BlockSpec(memory_space=pltpu.VMEM)
    filtered = pl.pallas_call(
        functools.partial(filter_kernel, vecs=vecs, slabs=groups),
        in_specs=[pl.BlockSpec(memory_space=pltpu.SMEM), vmem, vmem],
        out_specs=vmem,
        out_shape=jax.ShapeDtypeStruct((groups, strips, vecs, slab_rows, columns), jnp.float32),
        scratch_shapes=[pltpu.VMEM(lattice, jnp.float32)] * 4,
        name="filter",
    )(terms, whole_vecs.reshape(strips, vecs, rows, columns), whole_pot)

    slab = lax.all_to_all(
        filtered.reshape(devices, vecs * slab_rows, columns), both, split_axis=0, concat_axis=0, tiled=True
    ).reshape(total_vecs, slab_rows, columns)

    ring = [((i + 1) % devices, i) for i in range(devices)]
    next_row = lax.ppermute(slab[:, 0], ("strip", "vec"), ring)
    place = lax.axis_index("vec")
    own_pot = lax.dynamic_slice_in_dim(level, place * slab_rows, slab_rows, axis=0)
    lines_shape = (slab_rows, total_vecs, columns)
    sums, lines = pl.pallas_call(
        gram_kernel,
        in_specs=[vmem, vmem, vmem],
        out_specs=[vmem, vmem],
        out_shape=[
            jax.ShapeDtypeStruct((total_vecs, 2 * total_vecs), jnp.float32),
            jax.ShapeDtypeStruct(lines_shape, jnp.float32),
        ],
        name="gram",
    )(slab, next_row, own_pot)
    stride = 1
    while stride < devices:
        pairs = [(i, i ^ stride) for i in range(devices)]
        sums = sums + lax.ppermute(sums, ("strip", "vec"), pairs)
        stride *= 2
    gram_sum = sums[:, :total_vecs]
    cross_half = sums[:, total_vecs:]
    cross_sum = 0.5 * (cross_half + cross_half.T)
    lower_factor = jnp.linalg.cholesky(gram_sum)
    inverse = jax.scipy.linalg.solve_triangular(
        lower_factor, jnp.eye(total_vecs, dtype=jnp.float32), lower=True
    )
    site_count = strips * rows * columns
    scaled = math.sqrt(site_count) * inverse
    ortho_slab = pl.pallas_call(
        apply_kernel,
        in_specs=[vmem, vmem],
        out_specs=vmem,
        out_shape=jax.ShapeDtypeStruct((total_vecs, slab_rows, columns), jnp.float32),
        scratch_shapes=[pltpu.VMEM(lines_shape, jnp.float32)],
        name="apply",
    )(scaled, lines)
    ortho_basis = lax.all_to_all(ortho_slab, "vec", split_axis=0, concat_axis=1, tiled=True)
    half_done = jnp.dot(inverse, cross_sum, precision=lax.Precision.HIGHEST)
    ritz_matrix = float(rows) * jnp.dot(inverse, half_done.T, precision=lax.Precision.HIGHEST)
    return (ortho_basis, ritz_matrix)


def shards(start_vectors, potential, bounds):
    vec_local, rows, columns = start_vectors.shape
    strips = lax.axis_size("strip")
    groups = lax.axis_size("vec")
    devices = strips * groups
    whole = (
        strips == SUBLANES
        and vec_local % strips == 0
        and rows % (groups * SUBLANES) == 0
        and columns % LANES == 0
        and devices & (devices - 1) == 0
        and DEGREE % 2 == 0
    )
    form = whole_shards if whole else halo_shards
    return form(start_vectors, potential, bounds)


def solution(mesh):
    in_specs = (P("vec", "strip", None), P("strip", None), P())
    out_specs = (P("vec", "strip", None), P())
    return jax.shard_map(shards, mesh=mesh, in_specs=in_specs, out_specs=out_specs, check_vma=False)
```

```python
import functools
import math

import jax
import jax.numpy as jnp
from jax import lax
from jax.experimental import pallas as pl
from jax.experimental.pallas import tpu as pltpu
from jax.sharding import PartitionSpec as P

DEGREE = 32
DEPTH = 8
POT_LEVELS = 16
LANES = 128
SUBLANES = 8

grid_unit = 0.0625
disorder = 2.0


def filter_terms(bounds):
    edges = bounds.astype(jnp.float32) * grid_unit
    center = (edges[0] + edges[1]) * 0.5
    spread = (edges[1] - edges[0]) * 0.5
    theta_lo = jnp.arccos((edges[2] - center) / spread)
    theta_hi = jnp.arccos((edges[3] - center) / spread)
    orders = jnp.arange(1, DEGREE + 1).astype(jnp.float32)
    others = 2.0 * (jnp.sin(orders * theta_lo) - jnp.sin(orders * theta_hi)) / (orders * math.pi)
    first = jnp.reshape((theta_lo - theta_hi) / math.pi, (1,))
    return (jnp.concatenate([first, others]), center, spread)


def extended(value, sides, width):
    for axis, dim in sides:
        count, length = (lax.axis_size(axis), value.shape[dim])
        up = [(i, (i + 1) % count) for i in range(count)]
        down = [(j, i) for i, j in up]
        last = lax.slice_in_dim(value, length - width, length, axis=dim)
        leading = lax.slice_in_dim(value, 0, width, axis=dim)
        before = lax.ppermute(last, axis, up)
        after = lax.ppermute(leading, axis, down)
        value = jnp.concatenate([before, value, after], axis=dim)
    return value


def stencil(padded, pot_rows, center, spread):
    middle = padded[:, 1:-1]
    beside = padded[:, 2:] + padded[:, :-2] + jnp.roll(middle, 1, 2) + jnp.roll(middle, -1, 2)
    return ((pot_rows[None] - center) * middle - beside) / spread


def deep_filter(start_vectors, pot_padded, coeffs, center, spread):
    rows = start_vectors.shape[1]

    def one_round(rounds, carry):
        before, current, filtered = carry
        stacked = jnp.stack([before, current])
        padded = extended(stacked, (("strip", 2),), DEPTH)
        old_part = padded[0]
        new_part = padded[1]
        for inner in range(DEPTH):
            counter = rounds * DEPTH + inner
            factor = jnp.where(counter == 0, 1.0, 2.0).astype(jnp.float32)
            pot_rows = pot_padded[inner + 1 : rows + 2 * DEPTH - inner - 1]
            after = factor * stencil(new_part, pot_rows, center, spread) - old_part[:, 1:-1]
            offset = DEPTH - inner - 1
            filtered = filtered + coeffs[counter + 1] * after[:, offset : offset + rows]
            old_part = new_part[:, 1:-1]
            new_part = after
        return (old_part, new_part, filtered)

    initial = (jnp.zeros_like(start_vectors), start_vectors, coeffs[0] * start_vectors)
    return lax.fori_loop(0, DEGREE // DEPTH, one_round, initial)[2]


def halo_shards(start_vectors, potential, bounds):
    vec_local, rows, columns = start_vectors.shape
    pot_field = disorder * (potential.astype(jnp.float32) / (POT_LEVELS - 1) - 0.5)
    coeffs, center, spread = filter_terms(bounds)
    pot_padded = extended(pot_field, (("strip", 0),), DEPTH)
    filtered = deep_filter(start_vectors, pot_padded, coeffs, center, spread)
    padded = extended(filtered, (("strip", 1),), 1)
    applied = stencil(padded, pot_field, 0.0, 1.0)
    slab_vecs, slab_applied = (
        lax.all_to_all(filtered, "vec", split_axis=1, concat_axis=0, tiled=True),
        lax.all_to_all(applied, "vec", split_axis=1, concat_axis=0, tiled=True),
    )
    total_vecs = slab_vecs.shape[0]
    y_rows = slab_vecs.reshape(total_vecs, -1)
    hy_rows = slab_applied.reshape(total_vecs, -1)
    gram_part = jnp.dot(
        y_rows, y_rows.T, precision=lax.Precision.HIGHEST, preferred_element_type=jnp.float32
    )
    cross_part = jnp.dot(
        y_rows, hy_rows.T, precision=lax.Precision.HIGHEST, preferred_element_type=jnp.float32
    )
    gram_sum, cross_sum = lax.psum((gram_part, cross_part), ("strip", "vec"))
    lower_factor = jnp.linalg.cholesky(gram_sum)
    site_count = lax.axis_size("strip") * rows * columns
    ortho = jax.scipy.linalg.solve_triangular(lower_factor, y_rows, lower=True)
    ortho_slab = (math.sqrt(site_count) * ortho).reshape(slab_vecs.shape)
    ortho_basis = lax.all_to_all(ortho_slab, "vec", split_axis=0, concat_axis=1, tiled=True)
    half_done = jax.scipy.linalg.solve_triangular(lower_factor, cross_sum, lower=True)
    ritz_matrix = float(rows) * jax.scipy.linalg.solve_triangular(
        lower_factor, half_done.T, lower=True
    )
    return (ortho_basis, ritz_matrix)


def filter_kernel(coef_ref, me_ref, vec_ref, pot_ref, out_ref, *rest, slabs, first):
    if first:
        site, flip, grid, field, state_a, state_b = rest
    else:
        site = pot_ref
        flip, grid, field, state_a, state_b = rest
    rows, parts, strips, lanes = field.shape
    total_rows = rows * strips
    blocks = total_rows // lanes
    per_block = lanes // rows
    slab_rows = rows // slabs
    center = coef_ref[DEGREE + 1]

    def stage(read, target, change):
        for part in range(parts):
            for block in range(blocks):
                tile = jnp.concatenate(
                    [read(block * per_block + p, part * lanes) for p in range(per_block)], axis=0
                )
                flip[block, part * lanes : (part + 1) * lanes, :] = tile.T
        for part in range(parts):
            for block in range(blocks):
                tile = flip[block, pl.ds(part, lanes, stride=parts), :]
                grid[part, block * lanes : (block + 1) * lanes, :] = tile.T

        for j in range(rows):
            for part in range(parts):
                target(j, part, change(grid[part, pl.ds(j, strips, stride=rows), :]))

    def put_site(j, part, value):
        site[j, part] = value

    if first:
        me = me_ref[0]
        places = [((p ^ me) & 1) * (strips // 2) + ((p ^ me) >> 1) for p in range(strips)]
        stage(
            lambda p, start: pot_ref[places[p], :, start : start + lanes],
            put_site,
            lambda level: disorder * (level * (1.0 / (POT_LEVELS - 1)) - 0.5) - center,
        )
    top = coef_ref[DEGREE]

    def put_field(j, part, value):
        field[j, part] = value
        state_a[j + 1, part] = top * value
        state_b[j + 1, part] = jnp.zeros_like(value)

    stage(lambda p, start: vec_ref[p, :, start : start + lanes], put_field, lambda value: value)

    def wrap(state):
        for part in range(parts):
            state[0, part] = pltpu.roll(state[rows, part], 1, 0)
            state[rows + 1, part] = pltpu.roll(state[1, part], strips - 1, 0)

    def sweep(new, cur, weight, scale):
        def next_column(line):
            return line[1:] + [pltpu.roll(line[0], lanes - 1, 1)]

        def corner(here, below):
            sums = [a + b for a, b in zip(next_column(here), below)]
            return sums, [pltpu.roll(sums[-1], 1, 1)] + sums[:-1]

        def load(j):
            return [cur[j, part] for part in range(parts)]

        here = load(1)
        _, moved = corner(load(0), here)

        for j in range(rows):
            below = load(j + 2)
            sums, moved_next = corner(here, below)
            for part in range(parts):
                image = site[j, part] * here[part] - (sums[part] + moved[part])
                if scale is not None:
                    image = scale * image
                new[j + 1, part] = image + (weight * field[j, part] - new[j + 1, part])
            here, moved = below, moved_next

    square = coef_ref[DEGREE + 2]
    wrap(state_a)

    def two(step, carry):
        order = DEGREE - 1 - 2 * step
        sweep(state_b, state_a, coef_ref[order], square)
        wrap(state_b)
        sweep(state_a, state_b, coef_ref[order - 1], None)
        wrap(state_a)
        return carry

    lax.fori_loop(0, (DEGREE - 2) // 2, two, 0)
    sweep(state_b, state_a, coef_ref[1], square)
    wrap(state_b)
    sweep(state_a, state_b, coef_ref[0], 0.5)

    for j in range(rows):
        for part in range(parts):
            grid[part, pl.ds(j, strips, stride=rows), :] = state_a[j + 1, part]
    for part in range(parts):
        for block in range(blocks):
            flip[block, pl.ds(part, lanes, stride=parts), :] = grid[part, block * lanes : (block + 1) * lanes, :].T
    for part in range(parts):
        for block in range(blocks):
            tile = flip[block, part * lanes : (part + 1) * lanes, :].T
            for p in range(per_block):
                for slab in range(slabs):
                    start = p * rows + slab * slab_rows
                    out_ref[slab, block * per_block + p, :, part * lanes : (part + 1) * lanes] = tile[
                        start : start + slab_rows
                    ]


def gram_kernel(*refs, chunks):
    slab_refs, next_refs = refs[:chunks], refs[chunks : 2 * chunks]
    pot_ref, out_ref, lines_ref, below_ref = refs[2 * chunks :]
    slab_rows, total, columns = lines_ref.shape
    acc = jnp.zeros(out_ref.shape, jnp.float32)
    for chunk in range(chunks):
        for group in range(total // (chunks * SUBLANES)):
            here = slice(group * SUBLANES, (group + 1) * SUBLANES)
            start = (group * chunks + chunk) * SUBLANES
            lines_ref[:, start : start + SUBLANES, :] = jnp.swapaxes(slab_refs[chunk][here], 0, 1)
            below_ref[start : start + SUBLANES, :] = next_refs[chunk][here]
    for j in range(slab_rows):
        here = lines_ref[j]
        below = below_ref[...] if j == slab_rows - 1 else lines_ref[j + 1]
        level = pot_ref[j : j + 1, :]
        pot = disorder * (level * (1.0 / (POT_LEVELS - 1)) - 0.5)
        image = pot * here - (pltpu.roll(here, 1, 1) + pltpu.roll(here, columns - 1, 1)) - 2.0 * below
        both = jnp.concatenate([here, image], axis=0)
        acc = acc + lax.dot_general(
            here,
            both,
            (((1,), (1,)), ((), ())),
            precision=lax.Precision.HIGHEST,
            preferred_element_type=jnp.float32,
        )
    out_ref[...] = acc


def apply_kernel(inv_ref, lines_ref, out_ref, done_ref):
    slab_rows, total, columns = lines_ref.shape
    for j in range(slab_rows):
        done_ref[j] = jnp.dot(
            inv_ref[...],
            lines_ref[j],
            precision=lax.Precision.HIGHEST,
            preferred_element_type=jnp.float32,
        )
    for vec in range(0, total, SUBLANES):
        out_ref[vec : vec + SUBLANES] = jnp.swapaxes(done_ref[:, vec : vec + SUBLANES, :], 0, 1)


def whole_shards(start_vectors, potential, bounds):
    vec_local, rows, columns = start_vectors.shape
    strips = lax.axis_size("strip")
    groups = lax.axis_size("vec")
    both = ("vec", "strip")
    total_vecs = vec_local * groups
    vecs = vec_local // strips
    slab_rows = rows // groups
    devices = strips * groups

    coeffs, center, spread = filter_terms(bounds)
    beta = 2.0 / spread
    odd = jnp.arange(DEGREE + 1) % 2 == 1
    terms = jnp.concatenate([jnp.where(odd, beta, 1.0) * coeffs, center[None], (beta * beta)[None]])
    me = lax.axis_index("strip").astype(jnp.int32)
    level = potential.astype(jnp.float32)

    def swap(value, bit):
        return lax.ppermute(value, "strip", [(i, i ^ bit) for i in range(strips)])

    inner = []
    for chunk in range(vecs):
        part = start_vectors[chunk * strips : (chunk + 1) * strips]
        inner.append(lax.all_to_all(part, "strip", split_axis=0, concat_axis=0, tiled=True))
    whole_pot = level[None]
    bit = 2
    while bit < strips:
        whole_pot = jnp.concatenate([whole_pot, swap(whole_pot, bit)], axis=0)
        bit *= 2
    whole_pot = jnp.concatenate([whole_pot, swap(whole_pot, 1)], axis=0)

    parts = columns // LANES
    lattice = (rows, parts, strips, LANES)
    padded = (rows + 2, parts, strips, LANES)
    smem = pl.BlockSpec(memory_space=pltpu.SMEM)
    vmem = pl.BlockSpec(memory_space=pltpu.VMEM)
    slab_shape = jax.ShapeDtypeStruct((groups, strips, slab_rows, columns), jnp.float32)
    site = None
    slabs, nexts = [], []
    ring = [((i + 1) % devices, i) for i in range(devices)]
    for chunk in range(vecs):
        first = chunk == 0
        done = pl.pallas_call(
            functools.partial(filter_kernel, slabs=groups, first=first),
            in_specs=[smem, smem, vmem, vmem],
            out_specs=[vmem, vmem] if first else [vmem],
            out_shape=[slab_shape] + ([jax.ShapeDtypeStruct(lattice, jnp.float32)] if first else []),
            scratch_shapes=[
                pltpu.VMEM((strips * rows // LANES, columns, LANES), jnp.float32),
                pltpu.VMEM((parts, strips * rows, LANES), jnp.float32),
                pltpu.VMEM(lattice, jnp.float32),
                pltpu.VMEM(padded, jnp.float32),
                pltpu.VMEM(padded, jnp.float32),
            ],
            name="filter",
        )(terms, me[None], inner[chunk], whole_pot if first else site)
        if first:
            site = done[1]
        slab = lax.all_to_all(
            done[0].reshape(devices, slab_rows, columns), both, split_axis=0, concat_axis=0, tiled=True
        )
        slabs.append(slab)
        nexts.append(lax.ppermute(slab[:, 0], ("strip", "vec"), ring))

    place = lax.axis_index("vec")
    own_pot = lax.dynamic_slice_in_dim(level, place * slab_rows, slab_rows, axis=0)
    lines_shape = (slab_rows, total_vecs, columns)
    sums, lines = pl.pallas_call(
        functools.partial(gram_kernel, chunks=vecs),
        in_specs=[vmem] * (2 * vecs + 1),
        out_specs=[vmem, vmem],
        out_shape=[
            jax.ShapeDtypeStruct((total_vecs, 2 * total_vecs), jnp.float32),
            jax.ShapeDtypeStruct(lines_shape, jnp.float32),
        ],
        scratch_shapes=[pltpu.VMEM((total_vecs, columns), jnp.float32)],
        name="gram",
    )(*slabs, *nexts, own_pot)
    stride = 1
    while stride < devices:
        pairs = [(i, i ^ stride) for i in range(devices)]
        sums = sums + lax.ppermute(sums, ("strip", "vec"), pairs)
        stride *= 2
    gram_sum = sums[:, :total_vecs]
    cross_half = sums[:, total_vecs:]
    cross_sum = 0.5 * (cross_half + cross_half.T)
    lower_factor = jnp.linalg.cholesky(gram_sum)
    inverse = jax.scipy.linalg.solve_triangular(
        lower_factor, jnp.eye(total_vecs, dtype=jnp.float32), lower=True
    )
    site_count = strips * rows * columns
    scaled = math.sqrt(site_count) * inverse
    ortho_slab = pl.pallas_call(
        apply_kernel,
        in_specs=[vmem, vmem],
        out_specs=vmem,
        out_shape=jax.ShapeDtypeStruct((total_vecs, slab_rows, columns), jnp.float32),
        scratch_shapes=[pltpu.VMEM(lines_shape, jnp.float32)],
        name="apply",
    )(scaled, lines)
    ortho_basis = lax.all_to_all(ortho_slab, "vec", split_axis=0, concat_axis=1, tiled=True)
    half_done = jnp.dot(inverse, cross_sum, precision=lax.Precision.HIGHEST)
    ritz_matrix = float(rows) * jnp.dot(inverse, half_done.T, precision=lax.Precision.HIGHEST)
    return (ortho_basis, ritz_matrix)


def shards(start_vectors, potential, bounds):
    vec_local, rows, columns = start_vectors.shape
    strips = lax.axis_size("strip")
    groups = lax.axis_size("vec")
    devices = strips * groups
    whole = (
        strips == SUBLANES
        and vec_local % strips == 0
        and rows % (groups * SUBLANES) == 0
        and columns % (LANES * SUBLANES) == 0
        and LANES % rows == 0
        and strips * rows % LANES == 0
        and devices & (devices - 1) == 0
        and DEGREE % 2 == 0
    )
    form = whole_shards if whole else halo_shards
    return form(start_vectors, potential, bounds)


def solution(mesh):
    in_specs = (P("vec", "strip", None), P("strip", None), P())
    out_specs = (P("vec", "strip", None), P())
    return jax.shard_map(shards, mesh=mesh, in_specs=in_specs, out_specs=out_specs, check_vma=False)
```

```python
import functools
import math

import jax
import jax.numpy as jnp
from jax import lax
from jax.experimental import pallas as pl
from jax.experimental.pallas import tpu as pltpu
from jax.sharding import PartitionSpec as P

DEGREE = 32
DEPTH = 8
POT_LEVELS = 16
LANES = 128
SUBLANES = 8

grid_unit = 0.0625
disorder = 2.0


def filter_terms(bounds):
    edges = bounds.astype(jnp.float32) * grid_unit
    center = (edges[0] + edges[1]) * 0.5
    spread = (edges[1] - edges[0]) * 0.5
    theta_lo = jnp.arccos((edges[2] - center) / spread)
    theta_hi = jnp.arccos((edges[3] - center) / spread)
    orders = jnp.arange(1, DEGREE + 1).astype(jnp.float32)
    others = 2.0 * (jnp.sin(orders * theta_lo) - jnp.sin(orders * theta_hi)) / (orders * math.pi)
    first = jnp.reshape((theta_lo - theta_hi) / math.pi, (1,))
    return (jnp.concatenate([first, others]), center, spread)


def extended(value, sides, width):
    for axis, dim in sides:
        count, length = (lax.axis_size(axis), value.shape[dim])
        up = [(i, (i + 1) % count) for i in range(count)]
        down = [(j, i) for i, j in up]
        last = lax.slice_in_dim(value, length - width, length, axis=dim)
        leading = lax.slice_in_dim(value, 0, width, axis=dim)
        before = lax.ppermute(last, axis, up)
        after = lax.ppermute(leading, axis, down)
        value = jnp.concatenate([before, value, after], axis=dim)
    return value


def stencil(padded, pot_rows, center, spread):
    middle = padded[:, 1:-1]
    beside = padded[:, 2:] + padded[:, :-2] + jnp.roll(middle, 1, 2) + jnp.roll(middle, -1, 2)
    return ((pot_rows[None] - center) * middle - beside) / spread


def deep_filter(start_vectors, pot_padded, coeffs, center, spread):
    rows = start_vectors.shape[1]

    def one_round(rounds, carry):
        before, current, filtered = carry
        stacked = jnp.stack([before, current])
        padded = extended(stacked, (("strip", 2),), DEPTH)
        old_part = padded[0]
        new_part = padded[1]
        for inner in range(DEPTH):
            counter = rounds * DEPTH + inner
            factor = jnp.where(counter == 0, 1.0, 2.0).astype(jnp.float32)
            pot_rows = pot_padded[inner + 1 : rows + 2 * DEPTH - inner - 1]
            after = factor * stencil(new_part, pot_rows, center, spread) - old_part[:, 1:-1]
            offset = DEPTH - inner - 1
            filtered = filtered + coeffs[counter + 1] * after[:, offset : offset + rows]
            old_part = new_part[:, 1:-1]
            new_part = after
        return (old_part, new_part, filtered)

    initial = (jnp.zeros_like(start_vectors), start_vectors, coeffs[0] * start_vectors)
    return lax.fori_loop(0, DEGREE // DEPTH, one_round, initial)[2]


def halo_shards(start_vectors, potential, bounds):
    _, rows, columns = start_vectors.shape
    pot_field = disorder * (potential.astype(jnp.float32) / (POT_LEVELS - 1) - 0.5)
    coeffs, center, spread = filter_terms(bounds)
    pot_padded = extended(pot_field, (("strip", 0),), DEPTH)
    filtered = deep_filter(start_vectors, pot_padded, coeffs, center, spread)
    padded = extended(filtered, (("strip", 1),), 1)
    applied = stencil(padded, pot_field, 0.0, 1.0)
    slab_vecs, slab_applied = (
        lax.all_to_all(filtered, "vec", split_axis=1, concat_axis=0, tiled=True),
        lax.all_to_all(applied, "vec", split_axis=1, concat_axis=0, tiled=True),
    )
    total_vecs = slab_vecs.shape[0]
    y_rows = slab_vecs.reshape(total_vecs, -1)
    hy_rows = slab_applied.reshape(total_vecs, -1)
    gram_part = jnp.dot(
        y_rows, y_rows.T, precision=lax.Precision.HIGHEST, preferred_element_type=jnp.float32
    )
    cross_part = jnp.dot(
        y_rows, hy_rows.T, precision=lax.Precision.HIGHEST, preferred_element_type=jnp.float32
    )
    gram_sum, cross_sum = lax.psum((gram_part, cross_part), ("strip", "vec"))
    lower_factor = jnp.linalg.cholesky(gram_sum)
    site_count = lax.axis_size("strip") * rows * columns
    ortho = jax.scipy.linalg.solve_triangular(lower_factor, y_rows, lower=True)
    ortho_slab = (math.sqrt(site_count) * ortho).reshape(slab_vecs.shape)
    ortho_basis = lax.all_to_all(ortho_slab, "vec", split_axis=0, concat_axis=1, tiled=True)
    half_done = jax.scipy.linalg.solve_triangular(lower_factor, cross_sum, lower=True)
    ritz_matrix = float(rows) * jax.scipy.linalg.solve_triangular(
        lower_factor, half_done.T, lower=True
    )
    return (ortho_basis, ritz_matrix)


def filter_kernel(coef_ref, me_ref, vec_ref, *rest, slabs, first):
    if first:
        own_ref, other_ref, out_ref, site, pot_ref, sems, flip, grid, field, state_a, state_b = rest
    else:
        site, out_ref, flip, grid, field, state_a, state_b = rest
    rows, parts, strips, lanes = field.shape
    total_rows = rows * strips
    blocks = total_rows // lanes
    per_block = lanes // rows
    slab_rows = rows // slabs
    center = coef_ref[DEGREE + 1]

    def stage(read, target, change):
        for part in range(parts):
            for block in range(blocks):
                tile = jnp.concatenate(
                    [read(block * per_block + p, part * lanes) for p in range(per_block)], axis=0
                )
                flip[block, part * lanes : (part + 1) * lanes, :] = tile.T
        for part in range(parts):
            for block in range(blocks):
                tile = flip[block, pl.ds(part, lanes, stride=parts), :]
                grid[part, block * lanes : (block + 1) * lanes, :] = tile.T

        for j in range(rows):
            for part in range(parts):
                target(j, part, change(grid[part, pl.ds(j, strips, stride=rows), :]))

    def put_site(j, part, value):
        site[j, part] = value

    if first:
        me = me_ref[0]
        copies = [
            pltpu.make_async_copy((own_ref, other_ref)[d & 1].at[d >> 1], pot_ref.at[me ^ d], sems.at[d])
            for d in range(strips)
        ]
        for copy in copies:
            copy.start()
        for copy in copies:
            copy.wait()
        stage(
            lambda p, start: pot_ref[p, :, start : start + lanes],
            put_site,
            lambda level: disorder * (level * (1.0 / (POT_LEVELS - 1)) - 0.5) - center,
        )
    top = coef_ref[DEGREE]

    def put_field(j, part, value):
        field[j, part] = value
        state_a[j + 1, part] = top * value
        state_b[j + 1, part] = jnp.zeros_like(value)

    stage(lambda p, start: vec_ref[p, :, start : start + lanes], put_field, lambda value: value)

    def wrap(state):
        for part in range(parts):
            state[0, part] = pltpu.roll(state[rows, part], 1, 0)
            state[rows + 1, part] = pltpu.roll(state[1, part], strips - 1, 0)

    def sweep(new, cur, weight, scale):
        def next_column(line):
            return line[1:] + [pltpu.roll(line[0], lanes - 1, 1)]

        def corner(here, below):
            sums = [a + b for a, b in zip(next_column(here), below)]
            return sums, [pltpu.roll(sums[-1], 1, 1)] + sums[:-1]

        def load(j):
            return [cur[j, part] for part in range(parts)]

        here = load(1)
        _, moved = corner(load(0), here)

        for j in range(rows):
            below = load(j + 2)
            sums, moved_next = corner(here, below)
            for part in range(parts):
                image = site[j, part] * here[part] - (sums[part] + moved[part])
                if scale is not None:
                    image = scale * image
                new[j + 1, part] = image + (weight * field[j, part] - new[j + 1, part])
            here, moved = below, moved_next

    square = coef_ref[DEGREE + 2]
    wrap(state_a)

    def two(step, carry):
        order = DEGREE - 1 - 2 * step
        sweep(state_b, state_a, coef_ref[order], square)
        wrap(state_b)
        sweep(state_a, state_b, coef_ref[order - 1], None)
        wrap(state_a)
        return carry

    lax.fori_loop(0, (DEGREE - 2) // 2, two, 0)
    sweep(state_b, state_a, coef_ref[1], square)
    wrap(state_b)
    sweep(state_a, state_b, coef_ref[0], 0.5)

    for j in range(rows):
        for part in range(parts):
            grid[part, pl.ds(j, strips, stride=rows), :] = state_a[j + 1, part]
    for part in range(parts):
        for block in range(blocks):
            flip[block, pl.ds(part, lanes, stride=parts), :] = grid[part, block * lanes : (block + 1) * lanes, :].T
    for part in range(parts):
        for block in range(blocks):
            tile = flip[block, part * lanes : (part + 1) * lanes, :].T
            for p in range(per_block):
                for slab in range(slabs):
                    start = p * rows + slab * slab_rows
                    out_ref[slab, block * per_block + p, :, part * lanes : (part + 1) * lanes] = tile[
                        start : start + slab_rows
                    ]


def outer(left, right):
    return lax.dot_general(
        left,
        right,
        (((1,), (1,)), ((), ())),
        precision=lax.Precision.HIGHEST,
        preferred_element_type=jnp.float32,
    )


def gram_kernel(*refs, chunks):
    slab_refs = refs[:chunks]
    pot_ref, out_ref, lines_ref = refs[chunks:]
    slab_rows, total, columns = lines_ref.shape
    acc = jnp.zeros(out_ref.shape, jnp.float32)
    for chunk in range(chunks):
        for group in range(total // (chunks * SUBLANES)):
            here = slice(group * SUBLANES, (group + 1) * SUBLANES)
            start = (group * chunks + chunk) * SUBLANES
            lines_ref[:, start : start + SUBLANES, :] = jnp.swapaxes(slab_refs[chunk][here], 0, 1)
    for j in range(slab_rows):
        here = lines_ref[j]
        level = pot_ref[j : j + 1, :]
        pot = disorder * (level * (1.0 / (POT_LEVELS - 1)) - 0.5)
        image = pot * here - (pltpu.roll(here, 1, 1) + pltpu.roll(here, columns - 1, 1))
        if j < slab_rows - 1:
            image = image - 2.0 * lines_ref[j + 1]
        acc = acc + outer(here, jnp.concatenate([here, image], axis=0))
    out_ref[...] = acc


def edge_kernel(*refs, chunks):
    next_refs = refs[:chunks]
    sums_ref, last_ref, out_ref = refs[chunks:]
    total = sums_ref.shape[0]
    parts = []
    for group in range(total // (chunks * SUBLANES)):
        for chunk in range(chunks):
            parts.append(next_refs[chunk][group * SUBLANES : (group + 1) * SUBLANES, :])
    below = jnp.concatenate(parts, axis=0)
    both = jnp.concatenate([jnp.zeros_like(below), below], axis=0)
    out_ref[...] = sums_ref[...] - 2.0 * outer(last_ref[0], both)


def eliminate(sums):
    total, width = sums.shape
    blocks = total // SUBLANES
    lane = lax.broadcasted_iota(jnp.int32, (SUBLANES, width), 1)
    sublane = lax.broadcasted_iota(jnp.int32, (SUBLANES, width), 0)
    work = []
    for block in range(blocks):
        unit = (lane == sublane + (total + block * SUBLANES)).astype(jnp.float32)
        work.append(jnp.where(lane < total, sums[block * SUBLANES : (block + 1) * SUBLANES], unit))
    for k in range(total):
        home, inside = k // SUBLANES, k % SUBLANES
        columns = [
            jnp.broadcast_to(work[block][:, k : k + 1], (SUBLANES, width)) for block in range(home, blocks)
        ]
        pivot = columns[0][inside : inside + 1, :]
        row = work[home][inside : inside + 1, :] / pivot
        row = jnp.broadcast_to(row, (SUBLANES, width))
        columns[0] = jnp.where(sublane > inside, columns[0], 0.0)
        for block in range(home, blocks):
            work[block] = work[block] - columns[block - home] * row
    result = []
    for block in range(blocks):
        pivots = jnp.sum(
            jnp.where(lane == sublane + block * SUBLANES, work[block], 0.0), axis=1, keepdims=True
        )
        result.append(work[block] / jnp.sqrt(pivots))
    return jnp.concatenate(result, axis=0)[:, total:]


def products(inv_ref, lines_ref, done_ref, out_refs, place, scale, targets, half):
    slab_rows = lines_ref.shape[0]
    vec_local = out_refs[0].shape[0]
    first = ((place ^ targets[0]) // half) * half
    weights = scale * inv_ref[pl.ds(pl.multiple_of(first * vec_local, SUBLANES), half * vec_local), :]
    for j in range(slab_rows):
        done_ref[j] = jnp.dot(
            weights, lines_ref[j], precision=lax.Precision.HIGHEST, preferred_element_type=jnp.float32
        )
    for d, out_ref in zip(targets, out_refs):
        start = ((place ^ d) - first) * vec_local
        for vec in range(0, vec_local, SUBLANES):
            rows = pl.ds(pl.multiple_of(start + vec, SUBLANES), SUBLANES)
            out_ref[vec : vec + SUBLANES] = jnp.swapaxes(done_ref[:, rows, :], 0, 1)


def solve_kernel(place_ref, mine_ref, other_ref, lines_ref, inv_ref, sums_ref, *rest, scale, targets, half):
    sums = mine_ref[...] + other_ref[...]
    sums_ref[...] = sums
    inv_ref[...] = eliminate(sums)
    products(inv_ref, lines_ref, rest[-1], rest[:-1], place_ref[0], scale, targets, half)


def near_kernel(place_ref, inv_ref, lines_ref, *rest, scale, targets, half):
    products(inv_ref, lines_ref, rest[-1], rest[:-1], place_ref[0], scale, targets, half)


def place_kernel(place_ref, *refs, targets):
    out_ref, sems = refs[-2:]
    slab_rows = refs[0].shape[1]
    copies = []
    for n, d in enumerate(targets):
        start = pl.multiple_of((place_ref[0] ^ d) * slab_rows, SUBLANES)
        copies.append(pltpu.make_async_copy(refs[n], out_ref.at[:, pl.ds(start, slab_rows), :], sems.at[n]))
    for copy in copies:
        copy.start()
    for copy in copies:
        copy.wait()


def whole_shards(start_vectors, potential, bounds):
    vec_local, rows, columns = start_vectors.shape
    strips = lax.axis_size("strip")
    groups = lax.axis_size("vec")
    both = ("vec", "strip")
    total_vecs = vec_local * groups
    vecs = vec_local // strips
    slab_rows = rows // groups
    devices = strips * groups

    coeffs, center, spread = filter_terms(bounds)
    beta = 2.0 / spread
    odd = jnp.arange(DEGREE + 1) % 2 == 1
    terms = jnp.concatenate([jnp.where(odd, beta, 1.0) * coeffs, center[None], (beta * beta)[None]])
    me = lax.axis_index("strip").astype(jnp.int32)
    level = potential.astype(jnp.float32)

    def swap(value, bit):
        return lax.ppermute(value, "strip", [(i, i ^ bit) for i in range(strips)])

    inner = []
    for chunk in range(vecs):
        part = start_vectors[chunk * strips : (chunk + 1) * strips]
        inner.append(lax.all_to_all(part, "strip", split_axis=0, concat_axis=0, tiled=True))
    own_pots = jnp.stack([level] + [swap(level, bit) for bit in range(2, strips, 2)])
    other_pots = swap(own_pots, 1)

    parts = columns // LANES
    lattice = (rows, parts, strips, LANES)
    padded = (rows + 2, parts, strips, LANES)
    smem = pl.BlockSpec(memory_space=pltpu.SMEM)
    vmem = pl.BlockSpec(memory_space=pltpu.VMEM)
    hbm = pl.BlockSpec(memory_space=pl.ANY)
    slab_shape = jax.ShapeDtypeStruct((groups, strips, slab_rows, columns), jnp.float32)
    site = None
    slabs, nexts = [], []
    ring = [((i + 1) % devices, i) for i in range(devices)]
    for chunk in range(vecs):
        first = chunk == 0
        done = pl.pallas_call(
            functools.partial(filter_kernel, slabs=groups, first=first),
            in_specs=[smem, smem, vmem] + ([hbm, hbm] if first else [vmem]),
            out_specs=[vmem, vmem] if first else [vmem],
            out_shape=[slab_shape] + ([jax.ShapeDtypeStruct(lattice, jnp.float32)] if first else []),
            scratch_shapes=(
                [pltpu.VMEM((strips, rows, columns), jnp.float32), pltpu.SemaphoreType.DMA((strips,))]
                if first
                else []
            )
            + [
                pltpu.VMEM((strips * rows // LANES, columns, LANES), jnp.float32),
                pltpu.VMEM((parts, strips * rows, LANES), jnp.float32),
                pltpu.VMEM(lattice, jnp.float32),
                pltpu.VMEM(padded, jnp.float32),
                pltpu.VMEM(padded, jnp.float32),
            ],
            name="filter",
        )(terms, me[None], inner[chunk], *((own_pots, other_pots) if first else (site,)))
        if first:
            site = done[1]
        slab = lax.all_to_all(
            done[0].reshape(devices, slab_rows, columns), both, split_axis=0, concat_axis=0, tiled=True
        )
        slabs.append(slab)
        nexts.append(lax.ppermute(slab[:, 0], ("strip", "vec"), ring))

    place = lax.axis_index("vec").astype(jnp.int32)
    own_pot = lax.dynamic_slice_in_dim(level, place * slab_rows, slab_rows, axis=0)
    lines_shape = (slab_rows, total_vecs, columns)
    sums_shape = jax.ShapeDtypeStruct((total_vecs, 2 * total_vecs), jnp.float32)
    sums, lines = pl.pallas_call(
        functools.partial(gram_kernel, chunks=vecs),
        in_specs=[vmem] * (vecs + 1),
        out_specs=[vmem, vmem],
        out_shape=[sums_shape, jax.ShapeDtypeStruct(lines_shape, jnp.float32)],
        name="gram",
    )(*slabs, own_pot)
    sums = pl.pallas_call(
        functools.partial(edge_kernel, chunks=vecs),
        grid=(1,),
        in_specs=[vmem] * (vecs + 1)
        + [pl.BlockSpec((1, total_vecs, columns), lambda i: (slab_rows - 1, 0, 0))],
        out_specs=vmem,
        out_shape=sums_shape,
        name="edge",
    )(*nexts, sums, lines)

    pending = None
    for axis, count in (("strip", strips), ("vec", groups)):
        bit = 1
        while bit < count:
            if pending is not None:
                sums = sums + pending
            pending = lax.ppermute(sums, axis, [(i, i ^ bit) for i in range(count)])
            bit *= 2

    scale = math.sqrt(strips * rows * columns)
    half = groups // 2
    far, near = tuple(range(half, groups)), tuple(range(half))
    piece = jax.ShapeDtypeStruct((vec_local, slab_rows, columns), jnp.float32)
    products_scratch = [pltpu.VMEM((slab_rows, half * vec_local, columns), jnp.float32)]
    inverse, gram_cross, *far_blocks = pl.pallas_call(
        functools.partial(solve_kernel, scale=scale, targets=far, half=half),
        in_specs=[smem, vmem, vmem, vmem],
        out_specs=[vmem] * (2 + half),
        out_shape=[jax.ShapeDtypeStruct((total_vecs, total_vecs), jnp.float32), sums_shape] + [piece] * half,
        scratch_shapes=products_scratch,
        name="solve",
    )(place[None], sums, pending, lines)
    near_blocks = pl.pallas_call(
        functools.partial(near_kernel, scale=scale, targets=near, half=half),
        in_specs=[smem, vmem, vmem],
        out_specs=[vmem] * half,
        out_shape=[piece] * half,
        scratch_shapes=products_scratch,
        name="near",
    )(place[None], inverse, lines)

    def across(block, d):
        return lax.ppermute(block, "vec", [(i, i ^ d) for i in range(groups)]) if d else block

    far_blocks = [across(block, d) for d, block in zip(far, far_blocks)]
    near_blocks = [across(block, d) for d, block in zip(near, near_blocks)]
    out_shape = jax.ShapeDtypeStruct((vec_local, rows, columns), jnp.float32)
    ortho_basis = pl.pallas_call(
        functools.partial(place_kernel, targets=near),
        in_specs=[smem] + [hbm] * half,
        out_specs=hbm,
        out_shape=out_shape,
        scratch_shapes=[pltpu.SemaphoreType.DMA((half,))],
        name="place_near",
    )(place[None], *near_blocks)
    ortho_basis = pl.pallas_call(
        functools.partial(place_kernel, targets=far),
        in_specs=[smem] + [hbm] * (half + 1),
        out_specs=hbm,
        out_shape=out_shape,
        scratch_shapes=[pltpu.SemaphoreType.DMA((half,))],
        input_output_aliases={half + 1: 0},
        name="place_far",
    )(place[None], *far_blocks, ortho_basis)

    cross_half = gram_cross[:, total_vecs:]
    cross_sum = 0.5 * (cross_half + cross_half.T)
    half_done = jnp.dot(inverse, cross_sum, precision=lax.Precision.HIGHEST)
    ritz_matrix = float(rows) * jnp.dot(inverse, half_done.T, precision=lax.Precision.HIGHEST)
    return (ortho_basis, ritz_matrix)


def is_whole(vec_local, rows, columns, strips, groups):
    devices = strips * groups
    return (
        strips == SUBLANES
        and vec_local % strips == 0
        and rows % (groups * SUBLANES) == 0
        and columns % (LANES * SUBLANES) == 0
        and LANES % rows == 0
        and strips * rows % LANES == 0
        and groups >= 2
        and devices & (devices - 1) == 0
        and vec_local % SUBLANES == 0
        and 2 * vec_local * groups == LANES
        and DEGREE % 2 == 0
    )


def solution(mesh):
    strips, groups = mesh.shape["strip"], mesh.shape["vec"]
    in_specs = (P("vec", "strip", None), P("strip", None), P())
    out_specs = (P("vec", "strip", None), P())

    def step(start_vectors, potential, bounds):
        total_vecs, total_rows, columns = start_vectors.shape
        vec_local, rows = total_vecs // groups, total_rows // strips
        whole = is_whole(vec_local, rows, columns, strips, groups)

        def form(*local):
            return (whole_shards if whole else halo_shards)(*local)

        sharded = jax.shard_map(form, mesh=mesh, in_specs=in_specs, out_specs=out_specs, check_vma=False)
        return sharded(start_vectors, potential, bounds)

    return step
```

```python
import functools
import math

import jax
import jax.numpy as jnp
from jax import lax
from jax.experimental import pallas as pl
from jax.experimental.pallas import tpu as pltpu
from jax.sharding import PartitionSpec as P

DEGREE = 32
DEPTH = 8
POT_LEVELS = 16
LANES = 128
SUBLANES = 8

grid_unit = 0.0625
disorder = 2.0


def filter_terms(bounds):
    edges = bounds.astype(jnp.float32) * grid_unit
    center = (edges[0] + edges[1]) * 0.5
    spread = (edges[1] - edges[0]) * 0.5
    theta_lo = jnp.arccos((edges[2] - center) / spread)
    theta_hi = jnp.arccos((edges[3] - center) / spread)
    orders = jnp.arange(1, DEGREE + 1).astype(jnp.float32)
    others = 2.0 * (jnp.sin(orders * theta_lo) - jnp.sin(orders * theta_hi)) / (orders * math.pi)
    first = jnp.reshape((theta_lo - theta_hi) / math.pi, (1,))
    return (jnp.concatenate([first, others]), center, spread)


def extended(value, sides, width):
    for axis, dim in sides:
        count, length = (lax.axis_size(axis), value.shape[dim])
        up = [(i, (i + 1) % count) for i in range(count)]
        down = [(j, i) for i, j in up]
        last = lax.slice_in_dim(value, length - width, length, axis=dim)
        leading = lax.slice_in_dim(value, 0, width, axis=dim)
        before = lax.ppermute(last, axis, up)
        after = lax.ppermute(leading, axis, down)
        value = jnp.concatenate([before, value, after], axis=dim)
    return value


def stencil(padded, pot_rows, center, spread):
    middle = padded[:, 1:-1]
    beside = padded[:, 2:] + padded[:, :-2] + jnp.roll(middle, 1, 2) + jnp.roll(middle, -1, 2)
    return ((pot_rows[None] - center) * middle - beside) / spread


def deep_filter(start_vectors, pot_padded, coeffs, center, spread):
    rows = start_vectors.shape[1]

    def one_round(rounds, carry):
        before, current, filtered = carry
        stacked = jnp.stack([before, current])
        padded = extended(stacked, (("strip", 2),), DEPTH)
        old_part = padded[0]
        new_part = padded[1]
        for inner in range(DEPTH):
            counter = rounds * DEPTH + inner
            factor = jnp.where(counter == 0, 1.0, 2.0).astype(jnp.float32)
            pot_rows = pot_padded[inner + 1 : rows + 2 * DEPTH - inner - 1]
            after = factor * stencil(new_part, pot_rows, center, spread) - old_part[:, 1:-1]
            offset = DEPTH - inner - 1
            filtered = filtered + coeffs[counter + 1] * after[:, offset : offset + rows]
            old_part = new_part[:, 1:-1]
            new_part = after
        return (old_part, new_part, filtered)

    initial = (jnp.zeros_like(start_vectors), start_vectors, coeffs[0] * start_vectors)
    return lax.fori_loop(0, DEGREE // DEPTH, one_round, initial)[2]


def halo_shards(start_vectors, potential, bounds):
    _, rows, columns = start_vectors.shape
    pot_field = disorder * (potential.astype(jnp.float32) / (POT_LEVELS - 1) - 0.5)
    coeffs, center, spread = filter_terms(bounds)
    pot_padded = extended(pot_field, (("strip", 0),), DEPTH)
    filtered = deep_filter(start_vectors, pot_padded, coeffs, center, spread)
    padded = extended(filtered, (("strip", 1),), 1)
    applied = stencil(padded, pot_field, 0.0, 1.0)
    slab_vecs, slab_applied = (
        lax.all_to_all(filtered, "vec", split_axis=1, concat_axis=0, tiled=True),
        lax.all_to_all(applied, "vec", split_axis=1, concat_axis=0, tiled=True),
    )
    total_vecs = slab_vecs.shape[0]
    y_rows = slab_vecs.reshape(total_vecs, -1)
    hy_rows = slab_applied.reshape(total_vecs, -1)
    gram_part = jnp.dot(
        y_rows, y_rows.T, precision=lax.Precision.HIGHEST, preferred_element_type=jnp.float32
    )
    cross_part = jnp.dot(
        y_rows, hy_rows.T, precision=lax.Precision.HIGHEST, preferred_element_type=jnp.float32
    )
    gram_sum, cross_sum = lax.psum((gram_part, cross_part), ("strip", "vec"))
    lower_factor = jnp.linalg.cholesky(gram_sum)
    site_count = lax.axis_size("strip") * rows * columns
    ortho = jax.scipy.linalg.solve_triangular(lower_factor, y_rows, lower=True)
    ortho_slab = (math.sqrt(site_count) * ortho).reshape(slab_vecs.shape)
    ortho_basis = lax.all_to_all(ortho_slab, "vec", split_axis=0, concat_axis=1, tiled=True)
    half_done = jax.scipy.linalg.solve_triangular(lower_factor, cross_sum, lower=True)
    ritz_matrix = float(rows) * jax.scipy.linalg.solve_triangular(
        lower_factor, half_done.T, lower=True
    )
    return (ortho_basis, ritz_matrix)


def filter_kernel(coef_ref, me_ref, vec_ref, *rest, slabs, first):
    if first:
        here_ref, beside_ref, own_ref, other_ref, out_ref, site, pot_ref, sems, flip, grid, field, state_a, state_b = rest
    else:
        site, out_ref, flip, grid, field, state_a, state_b = rest
    rows, parts, strips, lanes = field.shape
    total_rows = rows * strips
    blocks = total_rows // lanes
    per_block = lanes // rows
    slab_rows = rows // slabs
    center = coef_ref[DEGREE + 1]

    def stage(read, target, change):
        for part in range(parts):
            for block in range(blocks):
                tile = jnp.concatenate(
                    [read(block * per_block + p, part * lanes) for p in range(per_block)], axis=0
                )
                flip[block, part * lanes : (part + 1) * lanes, :] = tile.T
        for part in range(parts):
            for block in range(blocks):
                tile = flip[block, pl.ds(part, lanes, stride=parts), :]
                grid[part, block * lanes : (block + 1) * lanes, :] = tile.T

        for j in range(rows):
            for part in range(parts):
                target(j, part, change(grid[part, pl.ds(j, strips, stride=rows), :]))

    def put_site(j, part, value):
        site[j, part] = value

    if first:
        me = me_ref[0]
        sources = [here_ref, beside_ref]
        for d in range(2, strips):
            sources.append((own_ref, other_ref)[d & 1].at[(d >> 1) - 1])
        copies = [
            pltpu.make_async_copy(sources[d], pot_ref.at[me ^ d], sems.at[d]) for d in range(strips)
        ]
        for copy in copies:
            copy.start()
        for copy in copies:
            copy.wait()
        stage(
            lambda p, start: pot_ref[p, :, start : start + lanes],
            put_site,
            lambda level: disorder * (level * (1.0 / (POT_LEVELS - 1)) - 0.5) - center,
        )
    top = coef_ref[DEGREE]

    def put_field(j, part, value):
        field[j, part] = value
        state_a[j + 1, part] = top * value
        state_b[j + 1, part] = jnp.zeros_like(value)

    stage(lambda p, start: vec_ref[p, :, start : start + lanes], put_field, lambda value: value)

    def wrap(state):
        for part in range(parts):
            state[0, part] = pltpu.roll(state[rows, part], 1, 0)
            state[rows + 1, part] = pltpu.roll(state[1, part], strips - 1, 0)

    def sweep(new, cur, weight, scale):
        def next_column(line):
            return line[1:] + [pltpu.roll(line[0], lanes - 1, 1)]

        def corner(here, below):
            sums = [a + b for a, b in zip(next_column(here), below)]
            return sums, [pltpu.roll(sums[-1], 1, 1)] + sums[:-1]

        def load(j):
            return [cur[j, part] for part in range(parts)]

        here = load(1)
        _, moved = corner(load(0), here)

        for j in range(rows):
            below = load(j + 2)
            sums, moved_next = corner(here, below)
            for part in range(parts):
                image = site[j, part] * here[part] - (sums[part] + moved[part])
                if scale is not None:
                    image = scale * image
                new[j + 1, part] = image + (weight * field[j, part] - new[j + 1, part])
            here, moved = below, moved_next

    square = coef_ref[DEGREE + 2]
    wrap(state_a)

    def two(step, carry):
        order = DEGREE - 1 - 2 * step
        sweep(state_b, state_a, coef_ref[order], square)
        wrap(state_b)
        sweep(state_a, state_b, coef_ref[order - 1], None)
        wrap(state_a)
        return carry

    lax.fori_loop(0, (DEGREE - 2) // 2, two, 0)
    sweep(state_b, state_a, coef_ref[1], square)
    wrap(state_b)
    sweep(state_a, state_b, coef_ref[0], 0.5)

    for j in range(rows):
        for part in range(parts):
            grid[part, pl.ds(j, strips, stride=rows), :] = state_a[j + 1, part]
    for part in range(parts):
        for block in range(blocks):
            flip[block, pl.ds(part, lanes, stride=parts), :] = grid[part, block * lanes : (block + 1) * lanes, :].T
    for part in range(parts):
        for block in range(blocks):
            tile = flip[block, part * lanes : (part + 1) * lanes, :].T
            for p in range(per_block):
                for slab in range(slabs):
                    start = p * rows + slab * slab_rows
                    out_ref[slab, block * per_block + p, :, part * lanes : (part + 1) * lanes] = tile[
                        start : start + slab_rows
                    ]


def outer(left, right):
    return lax.dot_general(
        left,
        right,
        (((1,), (1,)), ((), ())),
        precision=lax.Precision.HIGHEST,
        preferred_element_type=jnp.float32,
    )


def gram_kernel(*refs, chunks):
    slab_refs = refs[:chunks]
    pot_ref, out_ref, lines_ref = refs[chunks:]
    slab_rows, total, columns = lines_ref.shape
    acc = jnp.zeros(out_ref.shape, jnp.float32)
    for chunk in range(chunks):
        for group in range(total // (chunks * SUBLANES)):
            here = slice(group * SUBLANES, (group + 1) * SUBLANES)
            start = (group * chunks + chunk) * SUBLANES
            lines_ref[:, start : start + SUBLANES, :] = jnp.swapaxes(slab_refs[chunk][here], 0, 1)
    for j in range(slab_rows):
        here = lines_ref[j]
        level = pot_ref[j : j + 1, :]
        pot = disorder * (level * (1.0 / (POT_LEVELS - 1)) - 0.5)
        image = pot * here - (pltpu.roll(here, 1, 1) + pltpu.roll(here, columns - 1, 1))
        if j < slab_rows - 1:
            image = image - 2.0 * lines_ref[j + 1]
        acc = acc + outer(here, jnp.concatenate([here, image], axis=0))
    out_ref[...] = acc


def edge_kernel(*refs, chunks):
    next_refs = refs[:chunks]
    sums_ref, last_ref, out_ref = refs[chunks:]
    total = sums_ref.shape[0]
    parts = []
    for group in range(total // (chunks * SUBLANES)):
        for chunk in range(chunks):
            parts.append(next_refs[chunk][group * SUBLANES : (group + 1) * SUBLANES, :])
    below = jnp.concatenate(parts, axis=0)
    both = jnp.concatenate([jnp.zeros_like(below), below], axis=0)
    out_ref[...] = sums_ref[...] - 2.0 * outer(last_ref[0], both)


def eliminate(sums):
    total, width = sums.shape
    blocks = total // SUBLANES
    lane = lax.broadcasted_iota(jnp.int32, (SUBLANES, width), 1)
    sublane = lax.broadcasted_iota(jnp.int32, (SUBLANES, width), 0)
    work = []
    for block in range(blocks):
        unit = (lane == sublane + (total + block * SUBLANES)).astype(jnp.float32)
        work.append(jnp.where(lane < total, sums[block * SUBLANES : (block + 1) * SUBLANES], unit))
    for k in range(total):
        home, inside = k // SUBLANES, k % SUBLANES
        columns = [
            jnp.broadcast_to(work[block][:, k : k + 1], (SUBLANES, width)) for block in range(home, blocks)
        ]
        pivot = columns[0][inside : inside + 1, :]
        row = work[home][inside : inside + 1, :] / pivot
        row = jnp.broadcast_to(row, (SUBLANES, width))
        columns[0] = jnp.where(sublane > inside, columns[0], 0.0)
        for block in range(home, blocks):
            work[block] = work[block] - columns[block - home] * row
    result = []
    for block in range(blocks):
        pivots = jnp.sum(
            jnp.where(lane == sublane + block * SUBLANES, work[block], 0.0), axis=1, keepdims=True
        )
        result.append(work[block] / jnp.sqrt(pivots))
    return jnp.concatenate(result, axis=0)[:, total:]


def products(inv_ref, lines_ref, done_ref, out_refs, place, scale, targets, half):
    slab_rows = lines_ref.shape[0]
    vec_local = out_refs[0].shape[0]
    first = ((place ^ targets[0]) // half) * half
    weights = scale * inv_ref[pl.ds(pl.multiple_of(first * vec_local, SUBLANES), half * vec_local), :]
    for j in range(slab_rows):
        done_ref[j] = jnp.dot(
            weights, lines_ref[j], precision=lax.Precision.HIGHEST, preferred_element_type=jnp.float32
        )
    for d, out_ref in zip(targets, out_refs):
        start = ((place ^ d) - first) * vec_local
        for vec in range(0, vec_local, SUBLANES):
            rows = pl.ds(pl.multiple_of(start + vec, SUBLANES), SUBLANES)
            out_ref[vec : vec + SUBLANES] = jnp.swapaxes(done_ref[:, rows, :], 0, 1)


def solve_kernel(place_ref, mine_ref, other_ref, lines_ref, inv_ref, sums_ref, *rest, scale, targets, half):
    sums = mine_ref[...] + other_ref[...]
    sums_ref[...] = sums
    inv_ref[...] = eliminate(sums)
    products(inv_ref, lines_ref, rest[-1], rest[:-1], place_ref[0], scale, targets, half)


def near_kernel(place_ref, inv_ref, lines_ref, *rest, scale, targets, half):
    products(inv_ref, lines_ref, rest[-1], rest[:-1], place_ref[0], scale, targets, half)


def place_kernel(place_ref, *refs, targets):
    out_ref, sems = refs[-2:]
    slab_rows = refs[0].shape[1]
    copies = []
    for n, d in enumerate(targets):
        start = pl.multiple_of((place_ref[0] ^ d) * slab_rows, SUBLANES)
        copies.append(pltpu.make_async_copy(refs[n], out_ref.at[:, pl.ds(start, slab_rows), :], sems.at[n]))
    for copy in copies:
        copy.start()
    for copy in copies:
        copy.wait()


def whole_shards(start_vectors, potential, bounds):
    vec_local, rows, columns = start_vectors.shape
    strips = lax.axis_size("strip")
    groups = lax.axis_size("vec")
    both = ("vec", "strip")
    total_vecs = vec_local * groups
    vecs = vec_local // strips
    slab_rows = rows // groups
    devices = strips * groups

    coeffs, center, spread = filter_terms(bounds)
    beta = 2.0 / spread
    odd = jnp.arange(DEGREE + 1) % 2 == 1
    terms = jnp.concatenate([jnp.where(odd, beta, 1.0) * coeffs, center[None], (beta * beta)[None]])
    me = lax.axis_index("strip").astype(jnp.int32)
    level = potential.astype(jnp.float32)

    def swap(value, bit):
        return lax.ppermute(value, "strip", [(i, i ^ bit) for i in range(strips)])

    inner = []
    for chunk in range(vecs):
        part = start_vectors[chunk * strips : (chunk + 1) * strips]
        inner.append(lax.all_to_all(part, "strip", split_axis=0, concat_axis=0, tiled=True))
    beside = swap(level, 1)
    pieces = [swap(level, bit) for bit in range(2, strips, 2)]
    own_pots = jnp.stack(pieces)
    other_pots = swap(own_pots, 1)

    parts = columns // LANES
    lattice = (rows, parts, strips, LANES)
    padded = (rows + 2, parts, strips, LANES)
    smem = pl.BlockSpec(memory_space=pltpu.SMEM)
    vmem = pl.BlockSpec(memory_space=pltpu.VMEM)
    hbm = pl.BlockSpec(memory_space=pl.ANY)
    slab_shape = jax.ShapeDtypeStruct((groups, strips, slab_rows, columns), jnp.float32)
    site = None
    slabs, nexts = [], []
    ring = [((i + 1) % devices, i) for i in range(devices)]
    for chunk in range(vecs):
        first = chunk == 0
        done = pl.pallas_call(
            functools.partial(filter_kernel, slabs=groups, first=first),
            in_specs=[smem, smem, vmem] + ([hbm] * 4 if first else [vmem]),
            out_specs=[vmem, vmem] if first else [vmem],
            out_shape=[slab_shape] + ([jax.ShapeDtypeStruct(lattice, jnp.float32)] if first else []),
            scratch_shapes=(
                [pltpu.VMEM((strips, rows, columns), jnp.float32), pltpu.SemaphoreType.DMA((strips,))]
                if first
                else []
            )
            + [
                pltpu.VMEM((strips * rows // LANES, columns, LANES), jnp.float32),
                pltpu.VMEM((parts, strips * rows, LANES), jnp.float32),
                pltpu.VMEM(lattice, jnp.float32),
                pltpu.VMEM(padded, jnp.float32),
                pltpu.VMEM(padded, jnp.float32),
            ],
            name="filter",
        )(terms, me[None], inner[chunk], *((level, beside, own_pots, other_pots) if first else (site,)))
        if first:
            site = done[1]
        slab = lax.all_to_all(
            done[0].reshape(devices, slab_rows, columns), both, split_axis=0, concat_axis=0, tiled=True
        )
        slabs.append(slab)
        nexts.append(lax.ppermute(slab[:, 0], ("strip", "vec"), ring))

    place = lax.axis_index("vec").astype(jnp.int32)
    own_pot = lax.dynamic_slice_in_dim(level, place * slab_rows, slab_rows, axis=0)
    lines_shape = (slab_rows, total_vecs, columns)
    sums_shape = jax.ShapeDtypeStruct((total_vecs, 2 * total_vecs), jnp.float32)
    sums, lines = pl.pallas_call(
        functools.partial(gram_kernel, chunks=vecs),
        in_specs=[vmem] * (vecs + 1),
        out_specs=[vmem, vmem],
        out_shape=[sums_shape, jax.ShapeDtypeStruct(lines_shape, jnp.float32)],
        name="gram",
    )(*slabs, own_pot)
    sums = pl.pallas_call(
        functools.partial(edge_kernel, chunks=vecs),
        grid=(1,),
        in_specs=[vmem] * (vecs + 1)
        + [pl.BlockSpec((1, total_vecs, columns), lambda i: (slab_rows - 1, 0, 0))],
        out_specs=vmem,
        out_shape=sums_shape,
        name="edge",
    )(*nexts, sums, lines)

    pending = None
    for axis, count in (("strip", strips), ("vec", groups)):
        bit = 1
        while bit < count:
            if pending is not None:
                sums = sums + pending
            pending = lax.ppermute(sums, axis, [(i, i ^ bit) for i in range(count)])
            bit *= 2

    scale = math.sqrt(strips * rows * columns)
    half = groups // 2
    far, near = tuple(range(half, groups)), tuple(range(half))
    piece = jax.ShapeDtypeStruct((vec_local, slab_rows, columns), jnp.float32)
    products_scratch = [pltpu.VMEM((slab_rows, half * vec_local, columns), jnp.float32)]
    inverse, gram_cross, *far_blocks = pl.pallas_call(
        functools.partial(solve_kernel, scale=scale, targets=far, half=half),
        in_specs=[smem, vmem, vmem, vmem],
        out_specs=[vmem] * (2 + half),
        out_shape=[jax.ShapeDtypeStruct((total_vecs, total_vecs), jnp.float32), sums_shape] + [piece] * half,
        scratch_shapes=products_scratch,
        name="solve",
    )(place[None], sums, pending, lines)
    near_blocks = pl.pallas_call(
        functools.partial(near_kernel, scale=scale, targets=near, half=half),
        in_specs=[smem, vmem, vmem],
        out_specs=[vmem] * half,
        out_shape=[piece] * half,
        scratch_shapes=products_scratch,
        name="near",
    )(place[None], inverse, lines)

    def across(block, d):
        return lax.ppermute(block, "vec", [(i, i ^ d) for i in range(groups)]) if d else block

    far_blocks = [across(block, d) for d, block in zip(far, far_blocks)]
    near_blocks = [across(block, d) for d, block in zip(near, near_blocks)]
    out_shape = jax.ShapeDtypeStruct((vec_local, rows, columns), jnp.float32)
    ortho_basis = pl.pallas_call(
        functools.partial(place_kernel, targets=near),
        in_specs=[smem] + [vmem] * half,
        out_specs=hbm,
        out_shape=out_shape,
        scratch_shapes=[pltpu.SemaphoreType.DMA((half,))],
        name="place_near",
    )(place[None], *near_blocks)
    ortho_basis = pl.pallas_call(
        functools.partial(place_kernel, targets=far),
        in_specs=[smem] + [vmem] * half + [hbm],
        out_specs=hbm,
        out_shape=out_shape,
        scratch_shapes=[pltpu.SemaphoreType.DMA((half,))],
        input_output_aliases={half + 1: 0},
        name="place_far",
    )(place[None], *far_blocks, ortho_basis)

    cross_half = gram_cross[:, total_vecs:]
    cross_sum = 0.5 * (cross_half + cross_half.T)
    half_done = jnp.dot(inverse, cross_sum, precision=lax.Precision.HIGHEST)
    ritz_matrix = float(rows) * jnp.dot(inverse, half_done.T, precision=lax.Precision.HIGHEST)
    return (ortho_basis, ritz_matrix)


def is_whole(vec_local, rows, columns, strips, groups):
    devices = strips * groups
    return (
        strips == SUBLANES
        and vec_local % strips == 0
        and rows % (groups * SUBLANES) == 0
        and columns % (LANES * SUBLANES) == 0
        and LANES % rows == 0
        and strips * rows % LANES == 0
        and groups >= 2
        and devices & (devices - 1) == 0
        and vec_local % SUBLANES == 0
        and 2 * vec_local * groups == LANES
        and DEGREE % 2 == 0
    )


def solution(mesh):
    strips, groups = mesh.shape["strip"], mesh.shape["vec"]
    in_specs = (P("vec", "strip", None), P("strip", None), P())
    out_specs = (P("vec", "strip", None), P())

    def step(start_vectors, potential, bounds):
        total_vecs, total_rows, columns = start_vectors.shape
        vec_local, rows = total_vecs // groups, total_rows // strips
        whole = is_whole(vec_local, rows, columns, strips, groups)

        def form(*local):
            return (whole_shards if whole else halo_shards)(*local)

        sharded = jax.shard_map(form, mesh=mesh, in_specs=in_specs, out_specs=out_specs, check_vma=False)
        return sharded(start_vectors, potential, bounds)

    return step
```

```python
import functools
import math

import jax
import jax.numpy as jnp
from jax import lax
from jax.experimental import pallas as pl
from jax.experimental.pallas import tpu as pltpu
from jax.sharding import PartitionSpec as P

DEGREE = 32
DEPTH = 8
POT_LEVELS = 16
LANES = 128
SUBLANES = 8

grid_unit = 0.0625
disorder = 2.0


def filter_terms(bounds):
    edges = bounds.astype(jnp.float32) * grid_unit
    center = (edges[0] + edges[1]) * 0.5
    spread = (edges[1] - edges[0]) * 0.5
    theta_lo = jnp.arccos((edges[2] - center) / spread)
    theta_hi = jnp.arccos((edges[3] - center) / spread)
    orders = jnp.arange(1, DEGREE + 1).astype(jnp.float32)
    others = 2.0 * (jnp.sin(orders * theta_lo) - jnp.sin(orders * theta_hi)) / (orders * math.pi)
    first = jnp.reshape((theta_lo - theta_hi) / math.pi, (1,))
    return (jnp.concatenate([first, others]), center, spread)


def extended(value, sides, width):
    for axis, dim in sides:
        count, length = (lax.axis_size(axis), value.shape[dim])
        up = [(i, (i + 1) % count) for i in range(count)]
        down = [(j, i) for i, j in up]
        last = lax.slice_in_dim(value, length - width, length, axis=dim)
        leading = lax.slice_in_dim(value, 0, width, axis=dim)
        before = lax.ppermute(last, axis, up)
        after = lax.ppermute(leading, axis, down)
        value = jnp.concatenate([before, value, after], axis=dim)
    return value


def stencil(padded, pot_rows, center, spread):
    middle = padded[:, 1:-1]
    beside = padded[:, 2:] + padded[:, :-2] + jnp.roll(middle, 1, 2) + jnp.roll(middle, -1, 2)
    return ((pot_rows[None] - center) * middle - beside) / spread


def deep_filter(start_vectors, pot_padded, coeffs, center, spread):
    rows = start_vectors.shape[1]

    def one_round(rounds, carry):
        before, current, filtered = carry
        stacked = jnp.stack([before, current])
        padded = extended(stacked, (("strip", 2),), DEPTH)
        old_part = padded[0]
        new_part = padded[1]
        for inner in range(DEPTH):
            counter = rounds * DEPTH + inner
            factor = jnp.where(counter == 0, 1.0, 2.0).astype(jnp.float32)
            pot_rows = pot_padded[inner + 1 : rows + 2 * DEPTH - inner - 1]
            after = factor * stencil(new_part, pot_rows, center, spread) - old_part[:, 1:-1]
            offset = DEPTH - inner - 1
            filtered = filtered + coeffs[counter + 1] * after[:, offset : offset + rows]
            old_part = new_part[:, 1:-1]
            new_part = after
        return (old_part, new_part, filtered)

    initial = (jnp.zeros_like(start_vectors), start_vectors, coeffs[0] * start_vectors)
    return lax.fori_loop(0, DEGREE // DEPTH, one_round, initial)[2]


def halo_shards(start_vectors, potential, bounds):
    _, rows, columns = start_vectors.shape
    pot_field = disorder * (potential.astype(jnp.float32) / (POT_LEVELS - 1) - 0.5)
    coeffs, center, spread = filter_terms(bounds)
    pot_padded = extended(pot_field, (("strip", 0),), DEPTH)
    filtered = deep_filter(start_vectors, pot_padded, coeffs, center, spread)
    padded = extended(filtered, (("strip", 1),), 1)
    applied = stencil(padded, pot_field, 0.0, 1.0)
    slab_vecs, slab_applied = (
        lax.all_to_all(filtered, "vec", split_axis=1, concat_axis=0, tiled=True),
        lax.all_to_all(applied, "vec", split_axis=1, concat_axis=0, tiled=True),
    )
    total_vecs = slab_vecs.shape[0]
    y_rows = slab_vecs.reshape(total_vecs, -1)
    hy_rows = slab_applied.reshape(total_vecs, -1)
    gram_part = jnp.dot(
        y_rows, y_rows.T, precision=lax.Precision.HIGHEST, preferred_element_type=jnp.float32
    )
    cross_part = jnp.dot(
        y_rows, hy_rows.T, precision=lax.Precision.HIGHEST, preferred_element_type=jnp.float32
    )
    gram_sum, cross_sum = lax.psum((gram_part, cross_part), ("strip", "vec"))
    lower_factor = jnp.linalg.cholesky(gram_sum)
    site_count = lax.axis_size("strip") * rows * columns
    ortho = jax.scipy.linalg.solve_triangular(lower_factor, y_rows, lower=True)
    ortho_slab = (math.sqrt(site_count) * ortho).reshape(slab_vecs.shape)
    ortho_basis = lax.all_to_all(ortho_slab, "vec", split_axis=0, concat_axis=1, tiled=True)
    half_done = jax.scipy.linalg.solve_triangular(lower_factor, cross_sum, lower=True)
    ritz_matrix = float(rows) * jax.scipy.linalg.solve_triangular(
        lower_factor, half_done.T, lower=True
    )
    return (ortho_basis, ritz_matrix)


def stage(read, flip, grid, target, change, rows, strips):
    parts, total_rows, lanes = grid.shape
    blocks = total_rows // lanes
    per_block = lanes // rows
    for part in range(parts):
        for block in range(blocks):
            tile = jnp.concatenate(
                [read(block * per_block + p, part * lanes) for p in range(per_block)], axis=0
            )
            flip[block, part * lanes : (part + 1) * lanes, :] = tile.T
    for part in range(parts):
        for block in range(blocks):
            tile = flip[block, pl.ds(part, lanes, stride=parts), :]
            grid[part, block * lanes : (block + 1) * lanes, :] = tile.T
    for j in range(rows):
        for part in range(parts):
            target(j, part, change(grid[part, pl.ds(j, strips, stride=rows), :]))


def site_kernel(coef_ref, me_ref, here_ref, beside_ref, own_ref, other_ref, site, pot_ref, sems, flip, grid):
    rows, _, strips, lanes = site.shape
    center = coef_ref[DEGREE + 1]
    me = me_ref[0]
    sources = [here_ref, beside_ref]
    for d in range(2, strips):
        sources.append((own_ref, other_ref)[d & 1].at[(d >> 1) - 1])
    copies = [pltpu.make_async_copy(sources[d], pot_ref.at[me ^ d], sems.at[d]) for d in range(strips)]
    for copy in copies:
        copy.start()
    for copy in copies:
        copy.wait()

    def put_site(j, part, value):
        site[j, part] = value

    stage(
        lambda p, start: pot_ref[p, :, start : start + lanes],
        flip,
        grid,
        put_site,
        lambda level: disorder * (level * (1.0 / (POT_LEVELS - 1)) - 0.5) - center,
        rows,
        strips,
    )


def filter_kernel(coef_ref, vec_ref, site, out_ref, flip, grid, field, state_a, state_b, *, slabs):
    rows, parts, strips, lanes = field.shape
    total_rows = rows * strips
    blocks = total_rows // lanes
    per_block = lanes // rows
    slab_rows = rows // slabs
    top = coef_ref[DEGREE]

    def put_field(j, part, value):
        field[j, part] = value
        state_a[j + 1, part] = top * value
        state_b[j + 1, part] = jnp.zeros_like(value)

    stage(
        lambda p, start: vec_ref[p, :, start : start + lanes],
        flip,
        grid,
        put_field,
        lambda value: value,
        rows,
        strips,
    )

    def wrap(state):
        for part in range(parts):
            state[0, part] = pltpu.roll(state[rows, part], 1, 0)
            state[rows + 1, part] = pltpu.roll(state[1, part], strips - 1, 0)

    def sweep(new, cur, weight, scale):
        def next_column(line):
            return line[1:] + [pltpu.roll(line[0], lanes - 1, 1)]

        def corner(here, below):
            sums = [a + b for a, b in zip(next_column(here), below)]
            return sums, [pltpu.roll(sums[-1], 1, 1)] + sums[:-1]

        def load(j):
            return [cur[j, part] for part in range(parts)]

        here = load(1)
        _, moved = corner(load(0), here)

        for j in range(rows):
            below = load(j + 2)
            sums, moved_next = corner(here, below)
            for part in range(parts):
                image = site[j, part] * here[part] - (sums[part] + moved[part])
                if scale is not None:
                    image = scale * image
                new[j + 1, part] = image + (weight * field[j, part] - new[j + 1, part])
            here, moved = below, moved_next

    square = coef_ref[DEGREE + 2]
    wrap(state_a)

    def two(step, carry):
        order = DEGREE - 1 - 2 * step
        sweep(state_b, state_a, coef_ref[order], square)
        wrap(state_b)
        sweep(state_a, state_b, coef_ref[order - 1], None)
        wrap(state_a)
        return carry

    lax.fori_loop(0, (DEGREE - 2) // 2, two, 0)
    sweep(state_b, state_a, coef_ref[1], square)
    wrap(state_b)
    sweep(state_a, state_b, coef_ref[0], 0.5)

    for j in range(rows):
        for part in range(parts):
            grid[part, pl.ds(j, strips, stride=rows), :] = state_a[j + 1, part]
    for part in range(parts):
        for block in range(blocks):
            flip[block, pl.ds(part, lanes, stride=parts), :] = grid[part, block * lanes : (block + 1) * lanes, :].T
    for part in range(parts):
        for block in range(blocks):
            tile = flip[block, part * lanes : (part + 1) * lanes, :].T
            for p in range(per_block):
                for slab in range(slabs):
                    start = p * rows + slab * slab_rows
                    out_ref[slab, block * per_block + p, :, part * lanes : (part + 1) * lanes] = tile[
                        start : start + slab_rows
                    ]


def outer(left, right):
    return lax.dot_general(
        left,
        right,
        (((1,), (1,)), ((), ())),
        precision=lax.Precision.HIGHEST,
        preferred_element_type=jnp.float32,
    )


def gram_kernel(*refs, chunks):
    slab_refs = refs[:chunks]
    place_ref, pot_ref, out_ref, lines_ref = refs[chunks:]
    slab_rows, total, columns = lines_ref.shape
    acc = jnp.zeros(out_ref.shape, jnp.float32)
    for chunk in range(chunks):
        for group in range(total // (chunks * SUBLANES)):
            here = slice(group * SUBLANES, (group + 1) * SUBLANES)
            start = (group * chunks + chunk) * SUBLANES
            lines_ref[:, start : start + SUBLANES, :] = jnp.swapaxes(slab_refs[chunk][here], 0, 1)
    levels = pot_ref[pl.ds(pl.multiple_of(place_ref[0] * slab_rows, SUBLANES), slab_rows), :]
    for j in range(slab_rows):
        here = lines_ref[j]
        level = levels[j : j + 1, :]
        pot = disorder * (level * (1.0 / (POT_LEVELS - 1)) - 0.5)
        image = pot * here - (pltpu.roll(here, 1, 1) + pltpu.roll(here, columns - 1, 1))
        if j < slab_rows - 1:
            image = image - 2.0 * lines_ref[j + 1]
        acc = acc + outer(here, jnp.concatenate([here, image], axis=0))
    out_ref[...] = acc


def edge_kernel(*refs, chunks):
    next_refs = refs[:chunks]
    last_ref, out_ref = refs[chunks:]
    total = out_ref.shape[0]
    parts = []
    for group in range(total // (chunks * SUBLANES)):
        for chunk in range(chunks):
            parts.append(next_refs[chunk][group * SUBLANES : (group + 1) * SUBLANES, :])
    out_ref[...] = -2.0 * outer(last_ref[0], jnp.concatenate(parts, axis=0))


def eliminate(sums):
    total, width = sums.shape
    blocks = total // SUBLANES
    lane = lax.broadcasted_iota(jnp.int32, (SUBLANES, width), 1)
    sublane = lax.broadcasted_iota(jnp.int32, (SUBLANES, width), 0)
    work = []
    for block in range(blocks):
        unit = (lane == sublane + (total + block * SUBLANES)).astype(jnp.float32)
        work.append(jnp.where(lane < total, sums[block * SUBLANES : (block + 1) * SUBLANES], unit))
    for k in range(total):
        home, inside = k // SUBLANES, k % SUBLANES
        columns = [
            jnp.broadcast_to(work[block][:, k : k + 1], (SUBLANES, width)) for block in range(home, blocks)
        ]
        pivot = columns[0][inside : inside + 1, :]
        row = work[home][inside : inside + 1, :] / pivot
        row = jnp.broadcast_to(row, (SUBLANES, width))
        columns[0] = jnp.where(sublane > inside, columns[0], 0.0)
        for block in range(home, blocks):
            work[block] = work[block] - columns[block - home] * row
    result = []
    for block in range(blocks):
        pivots = jnp.sum(
            jnp.where(lane == sublane + block * SUBLANES, work[block], 0.0), axis=1, keepdims=True
        )
        result.append(work[block] / jnp.sqrt(pivots))
    return jnp.concatenate(result, axis=0)[:, total:]


def products(inv_ref, lines_ref, done_ref, out_refs, place, scale, targets, half):
    slab_rows = lines_ref.shape[0]
    vec_local = out_refs[0].shape[0]
    first = ((place ^ targets[0]) // half) * half
    weights = scale * inv_ref[pl.ds(pl.multiple_of(first * vec_local, SUBLANES), half * vec_local), :]
    for j in range(slab_rows):
        done_ref[j] = jnp.dot(
            weights, lines_ref[j], precision=lax.Precision.HIGHEST, preferred_element_type=jnp.float32
        )
    for d, out_ref in zip(targets, out_refs):
        start = ((place ^ d) - first) * vec_local
        for vec in range(0, vec_local, SUBLANES):
            rows = pl.ds(pl.multiple_of(start + vec, SUBLANES), SUBLANES)
            out_ref[vec : vec + SUBLANES] = jnp.swapaxes(done_ref[:, rows, :], 0, 1)


def solve_kernel(place_ref, mine_ref, other_ref, lines_ref, inv_ref, sums_ref, *rest, scale, targets, half):
    sums = mine_ref[...] + other_ref[...]
    sums_ref[...] = sums
    inv_ref[...] = eliminate(sums)
    products(inv_ref, lines_ref, rest[-1], rest[:-1], place_ref[0], scale, targets, half)


def near_kernel(place_ref, inv_ref, lines_ref, *rest, scale, targets, half):
    products(inv_ref, lines_ref, rest[-1], rest[:-1], place_ref[0], scale, targets, half)


def whole_shards(start_vectors, potential, bounds):
    vec_local, rows, columns = start_vectors.shape
    strips = lax.axis_size("strip")
    groups = lax.axis_size("vec")
    both = ("vec", "strip")
    total_vecs = vec_local * groups
    vecs = vec_local // strips
    slab_rows = rows // groups
    devices = strips * groups

    coeffs, center, spread = filter_terms(bounds)
    beta = 2.0 / spread
    odd = jnp.arange(DEGREE + 1) % 2 == 1
    terms = jnp.concatenate([jnp.where(odd, beta, 1.0) * coeffs, center[None], (beta * beta)[None]])
    me = lax.axis_index("strip").astype(jnp.int32)
    level = potential.astype(jnp.float32)

    def swap(value, bit):
        return lax.ppermute(value, "strip", [(i, i ^ bit) for i in range(strips)])

    inner = []

    def spread(vectors, chunk):
        part = vectors[chunk * strips : (chunk + 1) * strips]
        inner.append(lax.all_to_all(part, "strip", split_axis=0, concat_axis=0, tiled=True))

    spread(start_vectors, 0)
    beside = swap(level, 1)
    pieces = [swap(level, bit) for bit in range(2, strips, 2)]
    own_pots = jnp.stack(pieces)
    other_pots = swap(own_pots, 1)
    later, _ = lax.optimization_barrier((start_vectors, own_pots))
    for chunk in range(1, vecs):
        spread(later, chunk)

    parts = columns // LANES
    lattice = (rows, parts, strips, LANES)
    padded = (rows + 2, parts, strips, LANES)
    smem = pl.BlockSpec(memory_space=pltpu.SMEM)
    vmem = pl.BlockSpec(memory_space=pltpu.VMEM)
    hbm = pl.BlockSpec(memory_space=pl.ANY)
    slab_shape = jax.ShapeDtypeStruct((groups, strips, slab_rows, columns), jnp.float32)
    staging = [
        pltpu.VMEM((strips * rows // LANES, columns, LANES), jnp.float32),
        pltpu.VMEM((parts, strips * rows, LANES), jnp.float32),
    ]
    site = pl.pallas_call(
        site_kernel,
        in_specs=[smem, smem] + [hbm] * 4,
        out_specs=vmem,
        out_shape=jax.ShapeDtypeStruct(lattice, jnp.float32),
        scratch_shapes=[
            pltpu.VMEM((strips, rows, columns), jnp.float32),
            pltpu.SemaphoreType.DMA((strips,)),
        ]
        + staging,
        name="site",
    )(terms, me[None], level, beside, own_pots, other_pots)
    slabs, nexts = [], []
    ring = [((i + 1) % devices, i) for i in range(devices)]
    for chunk in range(vecs):
        done = pl.pallas_call(
            functools.partial(filter_kernel, slabs=groups),
            in_specs=[smem, vmem, vmem],
            out_specs=vmem,
            out_shape=slab_shape,
            scratch_shapes=staging
            + [
                pltpu.VMEM(lattice, jnp.float32),
                pltpu.VMEM(padded, jnp.float32),
                pltpu.VMEM(padded, jnp.float32),
            ],
            name="filter",
        )(terms, inner[chunk], site)
        slab = lax.all_to_all(done.reshape(devices, slab_rows, columns), both, split_axis=0, concat_axis=0, tiled=True)
        slabs.append(slab)
        nexts.append(lax.ppermute(slab[:, 0], ("strip", "vec"), ring))

    place = lax.axis_index("vec").astype(jnp.int32)
    lines_shape = (slab_rows, total_vecs, columns)
    sums_shape = jax.ShapeDtypeStruct((total_vecs, 2 * total_vecs), jnp.float32)
    sums, lines = pl.pallas_call(
        functools.partial(gram_kernel, chunks=vecs),
        in_specs=[vmem] * vecs + [smem, vmem],
        out_specs=[vmem, vmem],
        out_shape=[sums_shape, jax.ShapeDtypeStruct(lines_shape, jnp.float32)],
        name="gram",
    )(*slabs, place[None], level)
    edge = pl.pallas_call(
        functools.partial(edge_kernel, chunks=vecs),
        grid=(1,),
        in_specs=[vmem] * vecs + [pl.BlockSpec((1, total_vecs, columns), lambda i: (slab_rows - 1, 0, 0))],
        out_specs=vmem,
        out_shape=jax.ShapeDtypeStruct((total_vecs, total_vecs), jnp.float32),
        name="edge",
    )(*nexts, lines)

    def pairwise(value, order):
        rounds = [(axis, count, 1 << n) for axis, count in order for n in range(count.bit_length() - 1)]
        for number, (axis, count, bit) in enumerate(rounds):
            other = lax.ppermute(value, axis, [(i, i ^ bit) for i in range(count)])
            if number < len(rounds) - 1:
                value = value + other
        return value, other

    sums, pending = pairwise(sums, (("strip", strips), ("vec", groups)))
    edge = sum(pairwise(edge, (("vec", groups), ("strip", strips))))

    scale = math.sqrt(strips * rows * columns)
    half = groups // 2
    far, near = tuple(range(half, groups)), tuple(range(half))
    piece = jax.ShapeDtypeStruct((vec_local, slab_rows, columns), jnp.float32)
    products_scratch = [pltpu.VMEM((slab_rows, half * vec_local, columns), jnp.float32)]
    inverse, gram_cross, *far_blocks = pl.pallas_call(
        functools.partial(solve_kernel, scale=scale, targets=far, half=half),
        in_specs=[smem, vmem, vmem, vmem],
        out_specs=[vmem] * (2 + half),
        out_shape=[jax.ShapeDtypeStruct((total_vecs, total_vecs), jnp.float32), sums_shape] + [piece] * half,
        scratch_shapes=products_scratch,
        name="solve",
    )(place[None], sums, pending, lines)
    near_blocks = pl.pallas_call(
        functools.partial(near_kernel, scale=scale, targets=near, half=half),
        in_specs=[smem, vmem, vmem],
        out_specs=[vmem] * half,
        out_shape=[piece] * half,
        scratch_shapes=products_scratch,
        name="near",
    )(place[None], inverse, lines)

    def across(block, d):
        return lax.ppermute(block, "vec", [(i, i ^ d) for i in range(groups)]) if d else block

    far_blocks = [across(block, d) for d, block in zip(far, far_blocks)]
    near_blocks = [across(block, d) for d, block in zip(near, near_blocks)]
    ortho_basis = jnp.zeros((vec_local, rows, columns), jnp.float32)
    for d, block in zip(near + far, near_blocks + far_blocks):
        start = (place ^ d) * slab_rows
        ortho_basis = lax.dynamic_update_slice(ortho_basis, block, (0, start, 0))

    cross_half = gram_cross[:, total_vecs:] + edge
    cross_sum = 0.5 * (cross_half + cross_half.T)
    half_done = jnp.dot(inverse, cross_sum, precision=lax.Precision.HIGHEST)
    ritz_matrix = float(rows) * jnp.dot(inverse, half_done.T, precision=lax.Precision.HIGHEST)
    return (ortho_basis, ritz_matrix)


def is_whole(vec_local, rows, columns, strips, groups):
    devices = strips * groups
    return (
        strips == SUBLANES
        and vec_local % strips == 0
        and rows % (groups * SUBLANES) == 0
        and columns % (LANES * SUBLANES) == 0
        and LANES % rows == 0
        and strips * rows % LANES == 0
        and groups >= 2
        and devices & (devices - 1) == 0
        and vec_local % SUBLANES == 0
        and 2 * vec_local * groups == LANES
        and DEGREE % 2 == 0
    )


def solution(mesh):
    strips, groups = mesh.shape["strip"], mesh.shape["vec"]
    in_specs = (P("vec", "strip", None), P("strip", None), P())
    out_specs = (P("vec", "strip", None), P())

    def step(start_vectors, potential, bounds):
        total_vecs, total_rows, columns = start_vectors.shape
        vec_local, rows = total_vecs // groups, total_rows // strips
        whole = is_whole(vec_local, rows, columns, strips, groups)

        def form(*local):
            return (whole_shards if whole else halo_shards)(*local)

        sharded = jax.shard_map(form, mesh=mesh, in_specs=in_specs, out_specs=out_specs, check_vma=False)
        return sharded(start_vectors, potential, bounds)

    return step
```

```python
import functools
import math

import jax
import jax.numpy as jnp
from jax import lax
from jax.experimental import pallas as pl
from jax.experimental.pallas import tpu as pltpu
from jax.sharding import PartitionSpec as P

DEGREE = 32
DEPTH = 8
POT_LEVELS = 16
LANES = 128
SUBLANES = 8

grid_unit = 0.0625
disorder = 2.0


def filter_terms(bounds):
    edges = bounds.astype(jnp.float32) * grid_unit
    center = (edges[0] + edges[1]) * 0.5
    spread = (edges[1] - edges[0]) * 0.5
    theta_lo = jnp.arccos((edges[2] - center) / spread)
    theta_hi = jnp.arccos((edges[3] - center) / spread)
    orders = jnp.arange(1, DEGREE + 1).astype(jnp.float32)
    others = 2.0 * (jnp.sin(orders * theta_lo) - jnp.sin(orders * theta_hi)) / (orders * math.pi)
    first = jnp.reshape((theta_lo - theta_hi) / math.pi, (1,))
    return (jnp.concatenate([first, others]), center, spread)


def extended(value, sides, width):
    for axis, dim in sides:
        count, length = (lax.axis_size(axis), value.shape[dim])
        up = [(i, (i + 1) % count) for i in range(count)]
        down = [(j, i) for i, j in up]
        last = lax.slice_in_dim(value, length - width, length, axis=dim)
        leading = lax.slice_in_dim(value, 0, width, axis=dim)
        before = lax.ppermute(last, axis, up)
        after = lax.ppermute(leading, axis, down)
        value = jnp.concatenate([before, value, after], axis=dim)
    return value


def stencil(padded, pot_rows, center, spread):
    middle = padded[:, 1:-1]
    beside = padded[:, 2:] + padded[:, :-2] + jnp.roll(middle, 1, 2) + jnp.roll(middle, -1, 2)
    return ((pot_rows[None] - center) * middle - beside) / spread


def deep_filter(start_vectors, pot_padded, coeffs, center, spread):
    rows = start_vectors.shape[1]

    def one_round(rounds, carry):
        before, current, filtered = carry
        stacked = jnp.stack([before, current])
        padded = extended(stacked, (("strip", 2),), DEPTH)
        old_part = padded[0]
        new_part = padded[1]
        for inner in range(DEPTH):
            counter = rounds * DEPTH + inner
            factor = jnp.where(counter == 0, 1.0, 2.0).astype(jnp.float32)
            pot_rows = pot_padded[inner + 1 : rows + 2 * DEPTH - inner - 1]
            after = factor * stencil(new_part, pot_rows, center, spread) - old_part[:, 1:-1]
            offset = DEPTH - inner - 1
            filtered = filtered + coeffs[counter + 1] * after[:, offset : offset + rows]
            old_part = new_part[:, 1:-1]
            new_part = after
        return (old_part, new_part, filtered)

    initial = (jnp.zeros_like(start_vectors), start_vectors, coeffs[0] * start_vectors)
    return lax.fori_loop(0, DEGREE // DEPTH, one_round, initial)[2]


def halo_shards(start_vectors, potential, bounds):
    _, rows, columns = start_vectors.shape
    pot_field = disorder * (potential.astype(jnp.float32) / (POT_LEVELS - 1) - 0.5)
    coeffs, center, spread = filter_terms(bounds)
    pot_padded = extended(pot_field, (("strip", 0),), DEPTH)
    filtered = deep_filter(start_vectors, pot_padded, coeffs, center, spread)
    padded = extended(filtered, (("strip", 1),), 1)
    applied = stencil(padded, pot_field, 0.0, 1.0)
    slab_vecs, slab_applied = (
        lax.all_to_all(filtered, "vec", split_axis=1, concat_axis=0, tiled=True),
        lax.all_to_all(applied, "vec", split_axis=1, concat_axis=0, tiled=True),
    )
    total_vecs = slab_vecs.shape[0]
    y_rows = slab_vecs.reshape(total_vecs, -1)
    hy_rows = slab_applied.reshape(total_vecs, -1)
    gram_part = jnp.dot(
        y_rows, y_rows.T, precision=lax.Precision.HIGHEST, preferred_element_type=jnp.float32
    )
    cross_part = jnp.dot(
        y_rows, hy_rows.T, precision=lax.Precision.HIGHEST, preferred_element_type=jnp.float32
    )
    gram_sum, cross_sum = lax.psum((gram_part, cross_part), ("strip", "vec"))
    lower_factor = jnp.linalg.cholesky(gram_sum)
    site_count = lax.axis_size("strip") * rows * columns
    ortho = jax.scipy.linalg.solve_triangular(lower_factor, y_rows, lower=True)
    ortho_slab = (math.sqrt(site_count) * ortho).reshape(slab_vecs.shape)
    ortho_basis = lax.all_to_all(ortho_slab, "vec", split_axis=0, concat_axis=1, tiled=True)
    half_done = jax.scipy.linalg.solve_triangular(lower_factor, cross_sum, lower=True)
    ritz_matrix = float(rows) * jax.scipy.linalg.solve_triangular(
        lower_factor, half_done.T, lower=True
    )
    return (ortho_basis, ritz_matrix)


def turned(group, strip, groups):
    odd = strip % 2
    return group + odd * (groups - 1 - 2 * group)


def stage(read, flip, grid, target, change, rows, strips):
    parts, total_rows, lanes = grid.shape
    blocks = total_rows // lanes
    per_block = lanes // rows
    for part in range(parts):
        for block in range(blocks):
            tile = jnp.concatenate(
                [read(block * per_block + p, part * lanes) for p in range(per_block)], axis=0
            )
            flip[block, part * lanes : (part + 1) * lanes, :] = tile.T
    for part in range(parts):
        for block in range(blocks):
            tile = flip[block, pl.ds(part, lanes, stride=parts), :]
            grid[part, block * lanes : (block + 1) * lanes, :] = tile.T
    for j in range(rows):
        for part in range(parts):
            target(j, part, change(grid[part, pl.ds(j, strips, stride=rows), :]))


def site_kernel(coef_ref, me_ref, here_ref, beside_ref, own_ref, other_ref, site, pot_ref, sems, flip, grid):
    rows, _, strips, lanes = site.shape
    center = coef_ref[DEGREE + 1]
    me = me_ref[0]
    sources = [here_ref, beside_ref]
    for d in range(2, strips):
        sources.append((own_ref, other_ref)[d & 1].at[(d >> 1) - 1])
    copies = [pltpu.make_async_copy(sources[d], pot_ref.at[me ^ d], sems.at[d]) for d in range(strips)]
    for copy in copies:
        copy.start()
    for copy in copies:
        copy.wait()

    def put_site(j, part, value):
        site[j, part] = value

    stage(
        lambda p, start: pot_ref[p, :, start : start + lanes],
        flip,
        grid,
        put_site,
        lambda level: disorder * (level * (1.0 / (POT_LEVELS - 1)) - 0.5) - center,
        rows,
        strips,
    )


def filter_kernel(coef_ref, vec_ref, site, out_ref, flip, grid, field, state_a, state_b, *, slabs):
    rows, parts, strips, lanes = field.shape
    total_rows = rows * strips
    blocks = total_rows // lanes
    per_block = lanes // rows
    slab_rows = rows // slabs
    top = coef_ref[DEGREE]

    def put_field(j, part, value):
        field[j, part] = value
        state_a[j + 1, part] = top * value
        state_b[j + 1, part] = jnp.zeros_like(value)

    stage(
        lambda p, start: vec_ref[p, :, start : start + lanes],
        flip,
        grid,
        put_field,
        lambda value: value,
        rows,
        strips,
    )

    def wrap(state):
        for part in range(parts):
            state[0, part] = pltpu.roll(state[rows, part], 1, 0)
            state[rows + 1, part] = pltpu.roll(state[1, part], strips - 1, 0)

    def sweep(new, cur, weight, scale):
        def next_column(line):
            return line[1:] + [pltpu.roll(line[0], lanes - 1, 1)]

        def corner(here, below):
            sums = [a + b for a, b in zip(next_column(here), below)]
            return sums, [pltpu.roll(sums[-1], 1, 1)] + sums[:-1]

        def load(j):
            return [cur[j, part] for part in range(parts)]

        here = load(1)
        _, moved = corner(load(0), here)

        for j in range(rows):
            below = load(j + 2)
            sums, moved_next = corner(here, below)
            for part in range(parts):
                image = site[j, part] * here[part] - (sums[part] + moved[part])
                if scale is not None:
                    image = scale * image
                new[j + 1, part] = image + (weight * field[j, part] - new[j + 1, part])
            here, moved = below, moved_next

    square = coef_ref[DEGREE + 2]
    wrap(state_a)

    def two(step, carry):
        order = DEGREE - 1 - 2 * step
        sweep(state_b, state_a, coef_ref[order], square)
        wrap(state_b)
        sweep(state_a, state_b, coef_ref[order - 1], None)
        wrap(state_a)
        return carry

    lax.fori_loop(0, (DEGREE - 2) // 2, two, 0)
    sweep(state_b, state_a, coef_ref[1], square)
    wrap(state_b)
    sweep(state_a, state_b, coef_ref[0], 0.5)

    for j in range(rows):
        for part in range(parts):
            grid[part, pl.ds(j, strips, stride=rows), :] = state_a[j + 1, part]
    for part in range(parts):
        for block in range(blocks):
            flip[block, pl.ds(part, lanes, stride=parts), :] = grid[part, block * lanes : (block + 1) * lanes, :].T
    for part in range(parts):
        for block in range(blocks):
            tile = flip[block, part * lanes : (part + 1) * lanes, :].T
            for p in range(per_block):
                strip = block * per_block + p
                for slab in range(slabs):
                    start = p * rows + slab * slab_rows
                    group = turned(slab, strip, slabs)
                    out_ref[group, strip, :, part * lanes : (part + 1) * lanes] = tile[start : start + slab_rows]


def outer(left, right):
    return lax.dot_general(
        left,
        right,
        (((1,), (1,)), ((), ())),
        precision=lax.Precision.HIGHEST,
        preferred_element_type=jnp.float32,
    )


def gram_kernel(*refs, chunks):
    slab_refs = refs[:chunks]
    place_ref, pot_ref, out_ref, lines_ref = refs[chunks:]
    slab_rows, total, columns = lines_ref.shape
    acc = jnp.zeros(out_ref.shape, jnp.float32)
    for chunk in range(chunks):
        for group in range(total // (chunks * SUBLANES)):
            here = slice(group * SUBLANES, (group + 1) * SUBLANES)
            start = (group * chunks + chunk) * SUBLANES
            lines_ref[:, start : start + SUBLANES, :] = jnp.swapaxes(slab_refs[chunk][here], 0, 1)
    levels = pot_ref[pl.ds(pl.multiple_of(place_ref[0] * slab_rows, SUBLANES), slab_rows), :]
    for j in range(slab_rows):
        here = lines_ref[j]
        level = levels[j : j + 1, :]
        pot = disorder * (level * (1.0 / (POT_LEVELS - 1)) - 0.5)
        image = pot * here - (pltpu.roll(here, 1, 1) + pltpu.roll(here, columns - 1, 1))
        if j < slab_rows - 1:
            image = image - 2.0 * lines_ref[j + 1]
        acc = acc + outer(here, jnp.concatenate([here, image], axis=0))
    out_ref[...] = acc


def edge_kernel(*refs, chunks):
    next_refs = refs[:chunks]
    last_ref, out_ref = refs[chunks:]
    total = out_ref.shape[0]
    parts = []
    for group in range(total // (chunks * SUBLANES)):
        for chunk in range(chunks):
            parts.append(next_refs[chunk][group * SUBLANES : (group + 1) * SUBLANES, :])
    out_ref[...] = -2.0 * outer(last_ref[0], jnp.concatenate(parts, axis=0))


def eliminate(sums):
    total, width = sums.shape
    blocks = total // SUBLANES
    lane = lax.broadcasted_iota(jnp.int32, (SUBLANES, width), 1)
    sublane = lax.broadcasted_iota(jnp.int32, (SUBLANES, width), 0)
    work = []
    for block in range(blocks):
        unit = (lane == sublane + (total + block * SUBLANES)).astype(jnp.float32)
        work.append(jnp.where(lane < total, sums[block * SUBLANES : (block + 1) * SUBLANES], unit))
    for k in range(total):
        home, inside = k // SUBLANES, k % SUBLANES
        columns = [
            jnp.broadcast_to(work[block][:, k : k + 1], (SUBLANES, width)) for block in range(home, blocks)
        ]
        pivot = columns[0][inside : inside + 1, :]
        row = work[home][inside : inside + 1, :] / pivot
        row = jnp.broadcast_to(row, (SUBLANES, width))
        columns[0] = jnp.where(sublane > inside, columns[0], 0.0)
        for block in range(home, blocks):
            work[block] = work[block] - columns[block - home] * row
    result = []
    for block in range(blocks):
        pivots = jnp.sum(
            jnp.where(lane == sublane + block * SUBLANES, work[block], 0.0), axis=1, keepdims=True
        )
        result.append(work[block] / jnp.sqrt(pivots))
    return jnp.concatenate(result, axis=0)[:, total:]


def products(inv_ref, lines_ref, done_ref, out_refs, place, scale, targets, half):
    slab_rows = lines_ref.shape[0]
    vec_local = out_refs[0].shape[0]
    first = ((place ^ targets[0]) // half) * half
    weights = scale * inv_ref[pl.ds(pl.multiple_of(first * vec_local, SUBLANES), half * vec_local), :]
    for j in range(slab_rows):
        done_ref[j] = jnp.dot(
            weights, lines_ref[j], precision=lax.Precision.HIGHEST, preferred_element_type=jnp.float32
        )
    for d, out_ref in zip(targets, out_refs):
        start = ((place ^ d) - first) * vec_local
        for vec in range(0, vec_local, SUBLANES):
            rows = pl.ds(pl.multiple_of(start + vec, SUBLANES), SUBLANES)
            out_ref[vec : vec + SUBLANES] = jnp.swapaxes(done_ref[:, rows, :], 0, 1)


def solve_kernel(place_ref, mine_ref, other_ref, lines_ref, inv_ref, sums_ref, *rest, scale, targets, half):
    sums = mine_ref[...] + other_ref[...]
    sums_ref[...] = sums
    inv_ref[...] = eliminate(sums)
    products(inv_ref, lines_ref, rest[-1], rest[:-1], place_ref[0], scale, targets, half)


def near_kernel(place_ref, inv_ref, lines_ref, *rest, scale, targets, half):
    products(inv_ref, lines_ref, rest[-1], rest[:-1], place_ref[0], scale, targets, half)


def whole_shards(start_vectors, potential, bounds):
    vec_local, rows, columns = start_vectors.shape
    strips = lax.axis_size("strip")
    groups = lax.axis_size("vec")
    both = ("vec", "strip")
    total_vecs = vec_local * groups
    vecs = vec_local // strips
    slab_rows = rows // groups
    devices = strips * groups

    coeffs, center, spread = filter_terms(bounds)
    beta = 2.0 / spread
    odd = jnp.arange(DEGREE + 1) % 2 == 1
    terms = jnp.concatenate([jnp.where(odd, beta, 1.0) * coeffs, center[None], (beta * beta)[None]])
    me = lax.axis_index("strip").astype(jnp.int32)
    level = potential.astype(jnp.float32)

    def swap(value, bit):
        return lax.ppermute(value, "strip", [(i, i ^ bit) for i in range(strips)])

    inner = []

    def spread(vectors, chunk):
        part = vectors[chunk * strips : (chunk + 1) * strips]
        inner.append(lax.all_to_all(part, "strip", split_axis=0, concat_axis=0, tiled=True))

    spread(start_vectors, 0)
    beside = swap(level, 1)
    pieces = [swap(level, bit) for bit in range(2, strips, 2)]
    own_pots = jnp.stack(pieces)
    other_pots = swap(own_pots, 1)
    later, _ = lax.optimization_barrier((start_vectors, own_pots))
    for chunk in range(1, vecs):
        spread(later, chunk)

    parts = columns // LANES
    lattice = (rows, parts, strips, LANES)
    padded = (rows + 2, parts, strips, LANES)
    smem = pl.BlockSpec(memory_space=pltpu.SMEM)
    vmem = pl.BlockSpec(memory_space=pltpu.VMEM)
    hbm = pl.BlockSpec(memory_space=pl.ANY)
    slab_shape = jax.ShapeDtypeStruct((groups, strips, slab_rows, columns), jnp.float32)
    staging = [
        pltpu.VMEM((strips * rows // LANES, columns, LANES), jnp.float32),
        pltpu.VMEM((parts, strips * rows, LANES), jnp.float32),
    ]
    site = pl.pallas_call(
        site_kernel,
        in_specs=[smem, smem] + [hbm] * 4,
        out_specs=vmem,
        out_shape=jax.ShapeDtypeStruct(lattice, jnp.float32),
        scratch_shapes=[
            pltpu.VMEM((strips, rows, columns), jnp.float32),
            pltpu.SemaphoreType.DMA((strips,)),
        ]
        + staging,
        name="site",
    )(terms, me[None], level, beside, own_pots, other_pots)
    slabs, nexts = [], []
    holders = [p * groups + turned(s, p, groups) for p in range(strips) for s in range(groups)]
    ring = [(holders[(g + 1) % devices], holders[g]) for g in range(devices)]
    for chunk in range(vecs):
        done = pl.pallas_call(
            functools.partial(filter_kernel, slabs=groups),
            in_specs=[smem, vmem, vmem],
            out_specs=vmem,
            out_shape=slab_shape,
            scratch_shapes=staging
            + [
                pltpu.VMEM(lattice, jnp.float32),
                pltpu.VMEM(padded, jnp.float32),
                pltpu.VMEM(padded, jnp.float32),
            ],
            name="filter",
        )(terms, inner[chunk], site)
        slab = lax.all_to_all(done.reshape(devices, slab_rows, columns), both, split_axis=0, concat_axis=0, tiled=True)
        slabs.append(slab)
        nexts.append(lax.ppermute(slab[:, 0], ("strip", "vec"), ring))

    place = lax.axis_index("vec").astype(jnp.int32)
    lines_shape = (slab_rows, total_vecs, columns)
    sums_shape = jax.ShapeDtypeStruct((total_vecs, 2 * total_vecs), jnp.float32)
    sums, lines = pl.pallas_call(
        functools.partial(gram_kernel, chunks=vecs),
        in_specs=[vmem] * vecs + [smem, vmem],
        out_specs=[vmem, vmem],
        out_shape=[sums_shape, jax.ShapeDtypeStruct(lines_shape, jnp.float32)],
        name="gram",
    )(*slabs, turned(place, me, groups)[None], level)
    edge = pl.pallas_call(
        functools.partial(edge_kernel, chunks=vecs),
        grid=(1,),
        in_specs=[vmem] * vecs + [pl.BlockSpec((1, total_vecs, columns), lambda i: (slab_rows - 1, 0, 0))],
        out_specs=vmem,
        out_shape=jax.ShapeDtypeStruct((total_vecs, total_vecs), jnp.float32),
        name="edge",
    )(*nexts, lines)

    def pairwise(value, order):
        rounds = [(axis, count, 1 << n) for axis, count in order for n in range(count.bit_length() - 1)]
        for number, (axis, count, bit) in enumerate(rounds):
            other = lax.ppermute(value, axis, [(i, i ^ bit) for i in range(count)])
            if number < len(rounds) - 1:
                value = value + other
        return value, other

    sums, pending = pairwise(sums, (("strip", strips), ("vec", groups)))
    edge = sum(pairwise(edge, (("strip", strips),)))
    others = []
    for d in range(1, groups):
        others.append(lax.ppermute(edge, "vec", [(i, i ^ d) for i in range(groups)]))
    edge = edge + sum(others)

    scale = math.sqrt(strips * rows * columns)
    half = groups // 2
    far, near = tuple(range(half, groups)), tuple(range(half))
    piece = jax.ShapeDtypeStruct((vec_local, slab_rows, columns), jnp.float32)
    products_scratch = [pltpu.VMEM((slab_rows, half * vec_local, columns), jnp.float32)]
    inverse, gram_cross, *far_blocks = pl.pallas_call(
        functools.partial(solve_kernel, scale=scale, targets=far, half=half),
        in_specs=[smem, vmem, vmem, vmem],
        out_specs=[vmem] * (2 + half),
        out_shape=[jax.ShapeDtypeStruct((total_vecs, total_vecs), jnp.float32), sums_shape] + [piece] * half,
        scratch_shapes=products_scratch,
        name="solve",
    )(place[None], sums, pending, lines)
    near_blocks = pl.pallas_call(
        functools.partial(near_kernel, scale=scale, targets=near, half=half),
        in_specs=[smem, vmem, vmem],
        out_specs=[vmem] * half,
        out_shape=[piece] * half,
        scratch_shapes=products_scratch,
        name="near",
    )(place[None], inverse, lines)

    def across(block, d):
        return lax.ppermute(block, "vec", [(i, i ^ d) for i in range(groups)]) if d else block

    far_blocks = [across(block, d) for d, block in zip(far, far_blocks)]
    near_blocks = [across(block, d) for d, block in zip(near, near_blocks)]
    ortho_basis = jnp.zeros((vec_local, rows, columns), jnp.float32)
    for d, block in zip(near + far, near_blocks + far_blocks):
        start = turned(place ^ d, me, groups) * slab_rows
        ortho_basis = lax.dynamic_update_slice(ortho_basis, block, (0, start, 0))

    cross_half = gram_cross[:, total_vecs:] + edge
    cross_sum = 0.5 * (cross_half + cross_half.T)
    half_done = jnp.dot(inverse, cross_sum, precision=lax.Precision.HIGHEST)
    ritz_matrix = float(rows) * jnp.dot(inverse, half_done.T, precision=lax.Precision.HIGHEST)
    return (ortho_basis, ritz_matrix)


def is_whole(vec_local, rows, columns, strips, groups):
    devices = strips * groups
    return (
        strips == SUBLANES
        and vec_local % strips == 0
        and rows % (groups * SUBLANES) == 0
        and columns % (LANES * SUBLANES) == 0
        and LANES % rows == 0
        and strips * rows % LANES == 0
        and groups >= 2
        and devices & (devices - 1) == 0
        and vec_local % SUBLANES == 0
        and 2 * vec_local * groups == LANES
        and DEGREE % 2 == 0
    )


def solution(mesh):
    strips, groups = mesh.shape["strip"], mesh.shape["vec"]
    in_specs = (P("vec", "strip", None), P("strip", None), P())
    out_specs = (P("vec", "strip", None), P())

    def step(start_vectors, potential, bounds):
        total_vecs, total_rows, columns = start_vectors.shape
        vec_local, rows = total_vecs // groups, total_rows // strips
        whole = is_whole(vec_local, rows, columns, strips, groups)

        def form(*local):
            return (whole_shards if whole else halo_shards)(*local)

        sharded = jax.shard_map(form, mesh=mesh, in_specs=in_specs, out_specs=out_specs, check_vma=False)
        return sharded(start_vectors, potential, bounds)

    return step
```

```python
import functools
import math

import jax
import jax.numpy as jnp
from jax import lax
from jax.experimental import pallas as pl
from jax.experimental.pallas import tpu as pltpu
from jax.sharding import PartitionSpec as P

DEGREE = 32
DEPTH = 8
POT_LEVELS = 16
LANES = 128
SUBLANES = 8

grid_unit = 0.0625
disorder = 2.0


def filter_terms(bounds):
    edges = bounds.astype(jnp.float32) * grid_unit
    center = (edges[0] + edges[1]) * 0.5
    spread = (edges[1] - edges[0]) * 0.5
    theta_lo = jnp.arccos((edges[2] - center) / spread)
    theta_hi = jnp.arccos((edges[3] - center) / spread)
    orders = jnp.arange(1, DEGREE + 1).astype(jnp.float32)
    others = 2.0 * (jnp.sin(orders * theta_lo) - jnp.sin(orders * theta_hi)) / (orders * math.pi)
    first = jnp.reshape((theta_lo - theta_hi) / math.pi, (1,))
    return (jnp.concatenate([first, others]), center, spread)


def extended(value, sides, width):
    for axis, dim in sides:
        count, length = (lax.axis_size(axis), value.shape[dim])
        up = [(i, (i + 1) % count) for i in range(count)]
        down = [(j, i) for i, j in up]
        last = lax.slice_in_dim(value, length - width, length, axis=dim)
        leading = lax.slice_in_dim(value, 0, width, axis=dim)
        before = lax.ppermute(last, axis, up)
        after = lax.ppermute(leading, axis, down)
        value = jnp.concatenate([before, value, after], axis=dim)
    return value


def stencil(padded, pot_rows, center, spread):
    middle = padded[:, 1:-1]
    beside = padded[:, 2:] + padded[:, :-2] + jnp.roll(middle, 1, 2) + jnp.roll(middle, -1, 2)
    return ((pot_rows[None] - center) * middle - beside) / spread


def deep_filter(start_vectors, pot_padded, coeffs, center, spread):
    rows = start_vectors.shape[1]

    def one_round(rounds, carry):
        before, current, filtered = carry
        stacked = jnp.stack([before, current])
        padded = extended(stacked, (("strip", 2),), DEPTH)
        old_part = padded[0]
        new_part = padded[1]
        for inner in range(DEPTH):
            counter = rounds * DEPTH + inner
            factor = jnp.where(counter == 0, 1.0, 2.0).astype(jnp.float32)
            pot_rows = pot_padded[inner + 1 : rows + 2 * DEPTH - inner - 1]
            after = factor * stencil(new_part, pot_rows, center, spread) - old_part[:, 1:-1]
            offset = DEPTH - inner - 1
            filtered = filtered + coeffs[counter + 1] * after[:, offset : offset + rows]
            old_part = new_part[:, 1:-1]
            new_part = after
        return (old_part, new_part, filtered)

    initial = (jnp.zeros_like(start_vectors), start_vectors, coeffs[0] * start_vectors)
    return lax.fori_loop(0, DEGREE // DEPTH, one_round, initial)[2]


def halo_shards(start_vectors, potential, bounds):
    _, rows, columns = start_vectors.shape
    pot_field = disorder * (potential.astype(jnp.float32) / (POT_LEVELS - 1) - 0.5)
    coeffs, center, spread = filter_terms(bounds)
    pot_padded = extended(pot_field, (("strip", 0),), DEPTH)
    filtered = deep_filter(start_vectors, pot_padded, coeffs, center, spread)
    padded = extended(filtered, (("strip", 1),), 1)
    applied = stencil(padded, pot_field, 0.0, 1.0)
    slab_vecs, slab_applied = (
        lax.all_to_all(filtered, "vec", split_axis=1, concat_axis=0, tiled=True),
        lax.all_to_all(applied, "vec", split_axis=1, concat_axis=0, tiled=True),
    )
    total_vecs = slab_vecs.shape[0]
    y_rows = slab_vecs.reshape(total_vecs, -1)
    hy_rows = slab_applied.reshape(total_vecs, -1)
    gram_part = jnp.dot(
        y_rows, y_rows.T, precision=lax.Precision.HIGHEST, preferred_element_type=jnp.float32
    )
    cross_part = jnp.dot(
        y_rows, hy_rows.T, precision=lax.Precision.HIGHEST, preferred_element_type=jnp.float32
    )
    gram_sum, cross_sum = lax.psum((gram_part, cross_part), ("strip", "vec"))
    lower_factor = jnp.linalg.cholesky(gram_sum)
    site_count = lax.axis_size("strip") * rows * columns
    ortho = jax.scipy.linalg.solve_triangular(lower_factor, y_rows, lower=True)
    ortho_slab = (math.sqrt(site_count) * ortho).reshape(slab_vecs.shape)
    ortho_basis = lax.all_to_all(ortho_slab, "vec", split_axis=0, concat_axis=1, tiled=True)
    half_done = jax.scipy.linalg.solve_triangular(lower_factor, cross_sum, lower=True)
    ritz_matrix = float(rows) * jax.scipy.linalg.solve_triangular(
        lower_factor, half_done.T, lower=True
    )
    return (ortho_basis, ritz_matrix)


def turned(group, strip, groups):
    odd = strip % 2
    return group + odd * (groups - 1 - 2 * group)


def stage(read, flip, grid, target, change, rows, strips):
    parts, total_rows, lanes = grid.shape
    blocks = total_rows // lanes
    per_block = lanes // rows
    for part in range(parts):
        for block in range(blocks):
            tile = jnp.concatenate(
                [read(block * per_block + p, part * lanes) for p in range(per_block)], axis=0
            )
            flip[block, part * lanes : (part + 1) * lanes, :] = tile.T
    for part in range(parts):
        for block in range(blocks):
            tile = flip[block, pl.ds(part, lanes, stride=parts), :]
            grid[part, block * lanes : (block + 1) * lanes, :] = tile.T
    for j in range(rows):
        for part in range(parts):
            target(j, part, change(grid[part, pl.ds(j, strips, stride=rows), :]))


def site_kernel(coef_ref, me_ref, here_ref, beside_ref, own_ref, other_ref, site, pot_ref, sems, flip, grid):
    rows, _, strips, lanes = site.shape
    center = coef_ref[DEGREE + 1]
    me = me_ref[0]
    sources = [here_ref, beside_ref]
    for d in range(2, strips):
        sources.append((own_ref, other_ref)[d & 1].at[(d >> 1) - 1])
    copies = [pltpu.make_async_copy(sources[d], pot_ref.at[me ^ d], sems.at[d]) for d in range(strips)]
    for copy in copies:
        copy.start()
    for copy in copies:
        copy.wait()

    def put_site(j, part, value):
        site[j, part] = value

    stage(
        lambda p, start: pot_ref[p, :, start : start + lanes],
        flip,
        grid,
        put_site,
        lambda level: disorder * (level * (1.0 / (POT_LEVELS - 1)) - 0.5) - center,
        rows,
        strips,
    )


def filter_kernel(coef_ref, vec_ref, site, out_ref, flip, grid, field, state_a, state_b, *, slabs):
    rows, parts, strips, lanes = field.shape
    total_rows = rows * strips
    blocks = total_rows // lanes
    per_block = lanes // rows
    slab_rows = rows // slabs
    top = coef_ref[DEGREE]

    def put_field(j, part, value):
        field[j, part] = value
        state_a[j + 1, part] = top * value
        state_b[j + 1, part] = jnp.zeros_like(value)

    stage(
        lambda p, start: vec_ref[p, :, start : start + lanes],
        flip,
        grid,
        put_field,
        lambda value: value,
        rows,
        strips,
    )

    def wrap(state):
        for part in range(parts):
            state[0, part] = pltpu.roll(state[rows, part], 1, 0)
            state[rows + 1, part] = pltpu.roll(state[1, part], strips - 1, 0)

    def sweep(new, cur, weight, scale):
        def next_column(line):
            return line[1:] + [pltpu.roll(line[0], lanes - 1, 1)]

        def corner(here, below):
            sums = [a + b for a, b in zip(next_column(here), below)]
            return sums, [pltpu.roll(sums[-1], 1, 1)] + sums[:-1]

        def load(j):
            return [cur[j, part] for part in range(parts)]

        here = load(1)
        _, moved = corner(load(0), here)

        for j in range(rows):
            below = load(j + 2)
            sums, moved_next = corner(here, below)
            for part in range(parts):
                image = site[j, part] * here[part] - (sums[part] + moved[part])
                if scale is not None:
                    image = scale * image
                new[j + 1, part] = image + (weight * field[j, part] - new[j + 1, part])
            here, moved = below, moved_next

    square = coef_ref[DEGREE + 2]
    wrap(state_a)

    def two(step, carry):
        order = DEGREE - 1 - 2 * step
        sweep(state_b, state_a, coef_ref[order], square)
        wrap(state_b)
        sweep(state_a, state_b, coef_ref[order - 1], None)
        wrap(state_a)
        return carry

    lax.fori_loop(0, (DEGREE - 2) // 2, two, 0)
    sweep(state_b, state_a, coef_ref[1], square)
    wrap(state_b)
    sweep(state_a, state_b, coef_ref[0], 0.5)

    for j in range(rows):
        for part in range(parts):
            grid[part, pl.ds(j, strips, stride=rows), :] = state_a[j + 1, part]
    for part in range(parts):
        for block in range(blocks):
            flip[block, pl.ds(part, lanes, stride=parts), :] = grid[part, block * lanes : (block + 1) * lanes, :].T
    for part in range(parts):
        for block in range(blocks):
            tile = flip[block, part * lanes : (part + 1) * lanes, :].T
            for p in range(per_block):
                strip = block * per_block + p
                for slab in range(slabs):
                    start = p * rows + slab * slab_rows
                    group = turned(slab, strip, slabs)
                    out_ref[group, strip, :, part * lanes : (part + 1) * lanes] = tile[start : start + slab_rows]


def outer(left, right):
    return lax.dot_general(
        left,
        right,
        (((1,), (1,)), ((), ())),
        precision=lax.Precision.HIGHEST,
        preferred_element_type=jnp.float32,
    )


def gram_kernel(*refs, chunks):
    slab_refs = refs[:chunks]
    place_ref, pot_ref, out_ref, first_ref, low_ref, high_ref = refs[chunks:]
    slab_rows, total, width = low_ref.shape
    columns = slab_refs[0].shape[2]
    acc = jnp.zeros(out_ref.shape, jnp.float32)
    for chunk in range(chunks):
        for group in range(total // (chunks * SUBLANES)):
            here = slice(group * SUBLANES, (group + 1) * SUBLANES)
            start = (group * chunks + chunk) * SUBLANES
            there = slice(start, start + SUBLANES)
            value = jnp.swapaxes(slab_refs[chunk][here], 0, 1)
            low_ref[:, there, :] = value[:, :, :width]
            high_ref[:, there, :] = value[:, :, width:]
            first_ref[there, :] = value[0]

    def line(j):
        return jnp.concatenate([low_ref[j], high_ref[j]], axis=1)

    levels = pot_ref[pl.ds(pl.multiple_of(place_ref[0] * slab_rows, SUBLANES), slab_rows), :]
    for j in range(slab_rows):
        here = line(j)
        level = levels[j : j + 1, :]
        pot = disorder * (level * (1.0 / (POT_LEVELS - 1)) - 0.5)
        image = pot * here - (pltpu.roll(here, 1, 1) + pltpu.roll(here, columns - 1, 1))
        if j < slab_rows - 1:
            image = image - 2.0 * line(j + 1)
        acc = acc + outer(here, jnp.concatenate([here, image], axis=0))
    out_ref[...] = acc


def edge_kernel(next_ref, low_ref, high_ref, out_ref):
    last = jnp.concatenate([low_ref[0], high_ref[0]], axis=1)
    out_ref[...] = -2.0 * outer(last, next_ref[...])


def eliminate(sums):
    total, width = sums.shape
    blocks = total // SUBLANES
    lane = lax.broadcasted_iota(jnp.int32, (SUBLANES, width), 1)
    sublane = lax.broadcasted_iota(jnp.int32, (SUBLANES, width), 0)
    work = []
    for block in range(blocks):
        unit = (lane == sublane + (total + block * SUBLANES)).astype(jnp.float32)
        work.append(jnp.where(lane < total, sums[block * SUBLANES : (block + 1) * SUBLANES], unit))
    for k in range(total):
        home, inside = k // SUBLANES, k % SUBLANES
        columns = [
            jnp.broadcast_to(work[block][:, k : k + 1], (SUBLANES, width)) for block in range(home, blocks)
        ]
        pivot = columns[0][inside : inside + 1, :]
        row = work[home][inside : inside + 1, :] / pivot
        row = jnp.broadcast_to(row, (SUBLANES, width))
        columns[0] = jnp.where(sublane > inside, columns[0], 0.0)
        for block in range(home, blocks):
            work[block] = work[block] - columns[block - home] * row
    result = []
    for block in range(blocks):
        pivots = jnp.sum(
            jnp.where(lane == sublane + block * SUBLANES, work[block], 0.0), axis=1, keepdims=True
        )
        result.append(work[block] / jnp.sqrt(pivots))
    return jnp.concatenate(result, axis=0)[:, total:]


def products(inv_ref, sources, done_ref, place, scale, targets, half, vec_local):
    first = ((place ^ targets[0]) // half) * half
    weights = scale * inv_ref[pl.ds(pl.multiple_of(first * vec_local, SUBLANES), half * vec_local), :]
    for lines_ref, out_refs, at in sources:
        slab_rows, _, width = lines_ref.shape
        for j in range(slab_rows):
            done_ref[j] = jnp.dot(
                weights, lines_ref[j], precision=lax.Precision.HIGHEST, preferred_element_type=jnp.float32
            )
        for d, out_ref in zip(targets, out_refs):
            start = ((place ^ d) - first) * vec_local
            for vec in range(0, vec_local, SUBLANES):
                rows = pl.ds(pl.multiple_of(start + vec, SUBLANES), SUBLANES)
                out_ref[vec : vec + SUBLANES, :, at : at + width] = jnp.swapaxes(done_ref[:, rows, :], 0, 1)


def solve_kernel(place_ref, mine_ref, other_ref, low_ref, high_ref, inv_ref, sums_ref, *rest, **static):
    sums = mine_ref[...] + other_ref[...]
    sums_ref[...] = sums
    inv_ref[...] = eliminate(sums)
    half = static["half"]
    sources = [(low_ref, rest[:half], 0), (high_ref, rest[half : 2 * half], 0)]
    products(inv_ref, sources, rest[-1], place_ref[0], **static)


def near_kernel(place_ref, inv_ref, low_ref, high_ref, *rest, **static):
    sources = [(low_ref, rest[:-1], 0), (high_ref, rest[:-1], low_ref.shape[2])]
    products(inv_ref, sources, rest[-1], place_ref[0], **static)


def extra_kernel(place_ref, inv_ref, lines_ref, *rest, **static):
    products(inv_ref, [(lines_ref, rest[:-1], 0)], rest[-1], place_ref[0], **static)


def whole_shards(start_vectors, potential, bounds):
    vec_local, rows, columns = start_vectors.shape
    strips = lax.axis_size("strip")
    groups = lax.axis_size("vec")
    both = ("vec", "strip")
    total_vecs = vec_local * groups
    vecs = vec_local // strips
    slab_rows = rows // groups
    devices = strips * groups

    coeffs, center, spread = filter_terms(bounds)
    beta = 2.0 / spread
    odd = jnp.arange(DEGREE + 1) % 2 == 1
    terms = jnp.concatenate([jnp.where(odd, beta, 1.0) * coeffs, center[None], (beta * beta)[None]])
    me = lax.axis_index("strip").astype(jnp.int32)
    level = potential.astype(jnp.float32)

    def swap(value, bit):
        return lax.ppermute(value, "strip", [(i, i ^ bit) for i in range(strips)])

    inner = []

    def spread(vectors, chunk):
        part = vectors[chunk * strips : (chunk + 1) * strips]
        inner.append(lax.all_to_all(part, "strip", split_axis=0, concat_axis=0, tiled=True))

    spread(start_vectors, 0)
    beside = swap(level, 1)
    pieces = [swap(level, bit) for bit in range(2, strips, 2)]
    own_pots = jnp.stack(pieces)
    other_pots = swap(own_pots, 1)
    later, _ = lax.optimization_barrier((start_vectors, own_pots))
    for chunk in range(1, vecs):
        spread(later, chunk)

    parts = columns // LANES
    lattice = (rows, parts, strips, LANES)
    padded = (rows + 2, parts, strips, LANES)
    smem = pl.BlockSpec(memory_space=pltpu.SMEM)
    vmem = pl.BlockSpec(memory_space=pltpu.VMEM)
    hbm = pl.BlockSpec(memory_space=pl.ANY)
    slab_shape = jax.ShapeDtypeStruct((groups, strips, slab_rows, columns), jnp.float32)
    staging = [
        pltpu.VMEM((strips * rows // LANES, columns, LANES), jnp.float32),
        pltpu.VMEM((parts, strips * rows, LANES), jnp.float32),
    ]
    site = pl.pallas_call(
        site_kernel,
        in_specs=[smem, smem] + [hbm] * 4,
        out_specs=vmem,
        out_shape=jax.ShapeDtypeStruct(lattice, jnp.float32),
        scratch_shapes=[
            pltpu.VMEM((strips, rows, columns), jnp.float32),
            pltpu.SemaphoreType.DMA((strips,)),
        ]
        + staging,
        name="site",
    )(terms, me[None], level, beside, own_pots, other_pots)
    slabs = []
    holders = [p * groups + turned(s, p, groups) for p in range(strips) for s in range(groups)]
    ring = [(holders[(g + 1) % devices], holders[g]) for g in range(devices)]
    for chunk in range(vecs):
        done = pl.pallas_call(
            functools.partial(filter_kernel, slabs=groups),
            in_specs=[smem, vmem, vmem],
            out_specs=vmem,
            out_shape=slab_shape,
            scratch_shapes=staging
            + [
                pltpu.VMEM(lattice, jnp.float32),
                pltpu.VMEM(padded, jnp.float32),
                pltpu.VMEM(padded, jnp.float32),
            ],
            name="filter",
        )(terms, inner[chunk], site)
        slab = lax.all_to_all(done.reshape(devices, slab_rows, columns), both, split_axis=0, concat_axis=0, tiled=True)
        slabs.append(slab)

    place = lax.axis_index("vec").astype(jnp.int32)
    width = columns // 2
    lines_shape = jax.ShapeDtypeStruct((slab_rows, total_vecs, width), jnp.float32)
    sums_shape = jax.ShapeDtypeStruct((total_vecs, 2 * total_vecs), jnp.float32)
    sums, first_row, low, high = pl.pallas_call(
        functools.partial(gram_kernel, chunks=vecs),
        in_specs=[vmem] * vecs + [smem, vmem],
        out_specs=[vmem] * 4,
        out_shape=[
            sums_shape,
            jax.ShapeDtypeStruct((total_vecs, columns), jnp.float32),
            lines_shape,
            lines_shape,
        ],
        name="gram",
    )(*slabs, turned(place, me, groups)[None], level)
    next_row = lax.ppermute(first_row, ("strip", "vec"), ring)
    half = groups // 2
    middle = (half - 1, half)
    raw = lax.ppermute(high, "vec", [middle, middle[::-1]])
    last_row = pl.BlockSpec((1, total_vecs, width), lambda i: (slab_rows - 1, 0, 0))
    edge = pl.pallas_call(
        edge_kernel,
        grid=(1,),
        in_specs=[vmem, last_row, last_row],
        out_specs=vmem,
        out_shape=jax.ShapeDtypeStruct((total_vecs, total_vecs), jnp.float32),
        name="edge",
    )(next_row, low, high)

    def pairwise(value, order):
        rounds = [(axis, count, 1 << n) for axis, count in order for n in range(count.bit_length() - 1)]
        for number, (axis, count, bit) in enumerate(rounds):
            other = lax.ppermute(value, axis, [(i, i ^ bit) for i in range(count)])
            if number < len(rounds) - 1:
                value = value + other
        return value, other

    sums, pending = pairwise(sums, (("vec", groups), ("strip", strips)))
    mine, other = pairwise(edge, (("strip", strips),))
    edge = mine + other
    others = []
    for d in range(1, groups):
        others.append(lax.ppermute(edge, "vec", [(i, i ^ d) for i in range(groups)]))
    edge = edge + sum(others)

    static = dict(scale=math.sqrt(strips * rows * columns), half=half, vec_local=vec_local)
    far, near = tuple(range(half, groups)), tuple(range(half))
    piece = jax.ShapeDtypeStruct((vec_local, slab_rows, columns), jnp.float32)
    part_piece = jax.ShapeDtypeStruct((vec_local, slab_rows, width), jnp.float32)
    products_scratch = [pltpu.VMEM((slab_rows, half * vec_local, width), jnp.float32)]
    inverse, gram_cross, *blocks = pl.pallas_call(
        functools.partial(solve_kernel, targets=far, **static),
        in_specs=[smem] + [vmem] * 4,
        out_specs=[vmem] * (2 + 2 * half),
        out_shape=[jax.ShapeDtypeStruct((total_vecs, total_vecs), jnp.float32), sums_shape]
        + [part_piece] * (2 * half),
        scratch_shapes=products_scratch,
        name="solve",
    )(place[None], sums, pending, low, high)
    own_block, beside_block = pl.pallas_call(
        functools.partial(near_kernel, targets=near, **static),
        in_specs=[smem] + [vmem] * 3,
        out_specs=[vmem] * half,
        out_shape=[piece] * half,
        scratch_shapes=products_scratch,
        name="near",
    )(place[None], inverse, low, high)
    own_extra, beside_extra = pl.pallas_call(
        functools.partial(extra_kernel, targets=near, **static),
        in_specs=[smem] + [vmem] * 2,
        out_specs=[vmem] * half,
        out_shape=[part_piece] * half,
        scratch_shapes=products_scratch,
        name="extra",
    )(place[None], inverse, raw)

    def across(block, d, sources=range(groups)):
        return lax.ppermute(block, "vec", [(i, i ^ d) for i in sources])

    outer_groups = [i for i in range(groups) if i not in middle]
    far_high = [across(block, d, outer_groups) for d, block in zip(far, blocks[half:])]
    far_low = [across(block, d) for d, block in zip(far, blocks[:half])]
    beside_block = across(beside_block, 1)
    beside_extra = across(beside_extra, 1, middle)
    far_high = [far_high[0] + beside_extra, far_high[1] + own_extra]

    ortho_basis = jnp.zeros((vec_local, rows, columns), jnp.float32)
    for d, block, at in (
        (0, own_block, 0),
        (1, beside_block, 0),
        (2, far_low[0], 0),
        (3, far_low[1], 0),
        (2, far_high[0], width),
        (3, far_high[1], width),
    ):
        start = turned(place ^ d, me, groups) * slab_rows
        ortho_basis = lax.dynamic_update_slice(ortho_basis, block, (0, start, at))

    cross_half = gram_cross[:, total_vecs:] + edge
    cross_sum = 0.5 * (cross_half + cross_half.T)
    half_done = jnp.dot(inverse, cross_sum, precision=lax.Precision.HIGHEST)
    ritz_matrix = float(rows) * jnp.dot(inverse, half_done.T, precision=lax.Precision.HIGHEST)
    return (ortho_basis, ritz_matrix)


def is_whole(vec_local, rows, columns, strips, groups):
    devices = strips * groups
    return (
        strips == SUBLANES
        and vec_local % strips == 0
        and rows % (groups * SUBLANES) == 0
        and columns % (LANES * SUBLANES) == 0
        and LANES % rows == 0
        and strips * rows % LANES == 0
        and groups == 4
        and devices & (devices - 1) == 0
        and vec_local % SUBLANES == 0
        and 2 * vec_local * groups == LANES
        and DEGREE % 2 == 0
    )


def solution(mesh):
    strips, groups = mesh.shape["strip"], mesh.shape["vec"]
    in_specs = (P("vec", "strip", None), P("strip", None), P())
    out_specs = (P("vec", "strip", None), P())

    def step(start_vectors, potential, bounds):
        total_vecs, total_rows, columns = start_vectors.shape
        vec_local, rows = total_vecs // groups, total_rows // strips
        whole = is_whole(vec_local, rows, columns, strips, groups)

        def form(*local):
            return (whole_shards if whole else halo_shards)(*local)

        sharded = jax.shard_map(form, mesh=mesh, in_specs=in_specs, out_specs=out_specs, check_vma=False)
        return sharded(start_vectors, potential, bounds)

    return step
```

```python
import functools
import math

import jax
import jax.numpy as jnp
from jax import lax
from jax.experimental import pallas as pl
from jax.experimental.pallas import tpu as pltpu
from jax.sharding import PartitionSpec as P

DEGREE = 32
DEPTH = 8
POT_LEVELS = 16
LANES = 128
SUBLANES = 8

grid_unit = 0.0625
disorder = 2.0


def filter_terms(bounds):
    edges = bounds.astype(jnp.float32) * grid_unit
    center = (edges[0] + edges[1]) * 0.5
    spread = (edges[1] - edges[0]) * 0.5
    theta_lo = jnp.arccos((edges[2] - center) / spread)
    theta_hi = jnp.arccos((edges[3] - center) / spread)
    orders = jnp.arange(1, DEGREE + 1).astype(jnp.float32)
    others = 2.0 * (jnp.sin(orders * theta_lo) - jnp.sin(orders * theta_hi)) / (orders * math.pi)
    first = jnp.reshape((theta_lo - theta_hi) / math.pi, (1,))
    return (jnp.concatenate([first, others]), center, spread)


def extended(value, sides, width):
    for axis, dim in sides:
        count, length = (lax.axis_size(axis), value.shape[dim])
        up = [(i, (i + 1) % count) for i in range(count)]
        down = [(j, i) for i, j in up]
        last = lax.slice_in_dim(value, length - width, length, axis=dim)
        leading = lax.slice_in_dim(value, 0, width, axis=dim)
        before = lax.ppermute(last, axis, up)
        after = lax.ppermute(leading, axis, down)
        value = jnp.concatenate([before, value, after], axis=dim)
    return value


def stencil(padded, pot_rows, center, spread):
    middle = padded[:, 1:-1]
    beside = padded[:, 2:] + padded[:, :-2] + jnp.roll(middle, 1, 2) + jnp.roll(middle, -1, 2)
    return ((pot_rows[None] - center) * middle - beside) / spread


def deep_filter(start_vectors, pot_padded, coeffs, center, spread):
    rows = start_vectors.shape[1]

    def one_round(rounds, carry):
        before, current, filtered = carry
        stacked = jnp.stack([before, current])
        padded = extended(stacked, (("strip", 2),), DEPTH)
        old_part = padded[0]
        new_part = padded[1]
        for inner in range(DEPTH):
            counter = rounds * DEPTH + inner
            factor = jnp.where(counter == 0, 1.0, 2.0).astype(jnp.float32)
            pot_rows = pot_padded[inner + 1 : rows + 2 * DEPTH - inner - 1]
            after = factor * stencil(new_part, pot_rows, center, spread) - old_part[:, 1:-1]
            offset = DEPTH - inner - 1
            filtered = filtered + coeffs[counter + 1] * after[:, offset : offset + rows]
            old_part = new_part[:, 1:-1]
            new_part = after
        return (old_part, new_part, filtered)

    initial = (jnp.zeros_like(start_vectors), start_vectors, coeffs[0] * start_vectors)
    return lax.fori_loop(0, DEGREE // DEPTH, one_round, initial)[2]


def halo_shards(start_vectors, potential, bounds):
    _, rows, columns = start_vectors.shape
    pot_field = disorder * (potential.astype(jnp.float32) / (POT_LEVELS - 1) - 0.5)
    coeffs, center, spread = filter_terms(bounds)
    pot_padded = extended(pot_field, (("strip", 0),), DEPTH)
    filtered = deep_filter(start_vectors, pot_padded, coeffs, center, spread)
    padded = extended(filtered, (("strip", 1),), 1)
    applied = stencil(padded, pot_field, 0.0, 1.0)
    slab_vecs, slab_applied = (
        lax.all_to_all(filtered, "vec", split_axis=1, concat_axis=0, tiled=True),
        lax.all_to_all(applied, "vec", split_axis=1, concat_axis=0, tiled=True),
    )
    total_vecs = slab_vecs.shape[0]
    y_rows = slab_vecs.reshape(total_vecs, -1)
    hy_rows = slab_applied.reshape(total_vecs, -1)
    gram_part = jnp.dot(
        y_rows, y_rows.T, precision=lax.Precision.HIGHEST, preferred_element_type=jnp.float32
    )
    cross_part = jnp.dot(
        y_rows, hy_rows.T, precision=lax.Precision.HIGHEST, preferred_element_type=jnp.float32
    )
    gram_sum, cross_sum = lax.psum((gram_part, cross_part), ("strip", "vec"))
    lower_factor = jnp.linalg.cholesky(gram_sum)
    site_count = lax.axis_size("strip") * rows * columns
    ortho = jax.scipy.linalg.solve_triangular(lower_factor, y_rows, lower=True)
    ortho_slab = (math.sqrt(site_count) * ortho).reshape(slab_vecs.shape)
    ortho_basis = lax.all_to_all(ortho_slab, "vec", split_axis=0, concat_axis=1, tiled=True)
    half_done = jax.scipy.linalg.solve_triangular(lower_factor, cross_sum, lower=True)
    ritz_matrix = float(rows) * jax.scipy.linalg.solve_triangular(
        lower_factor, half_done.T, lower=True
    )
    return (ortho_basis, ritz_matrix)


def turned(group, strip, groups):
    odd = strip % 2
    return group + odd * (groups - 1 - 2 * group)


def stage(read, flip, grid, target, change, rows, strips):
    parts, total_rows, lanes = grid.shape
    blocks = total_rows // lanes
    per_block = lanes // rows
    for part in range(parts):
        for block in range(blocks):
            tile = jnp.concatenate(
                [read(block * per_block + p, part * lanes) for p in range(per_block)], axis=0
            )
            flip[block, part * lanes : (part + 1) * lanes, :] = tile.T
    for part in range(parts):
        for block in range(blocks):
            tile = flip[block, pl.ds(part, lanes, stride=parts), :]
            grid[part, block * lanes : (block + 1) * lanes, :] = tile.T
    for j in range(rows):
        for part in range(parts):
            target(j, part, change(grid[part, pl.ds(j, strips, stride=rows), :]))


def site_kernel(coef_ref, me_ref, here_ref, beside_ref, own_ref, other_ref, site, pot_ref, sems, flip, grid):
    rows, _, strips, lanes = site.shape
    center = coef_ref[DEGREE + 1]
    me = me_ref[0]
    sources = [here_ref, beside_ref]
    for d in range(2, strips):
        sources.append((own_ref, other_ref)[d & 1].at[(d >> 1) - 1])
    copies = [pltpu.make_async_copy(sources[d], pot_ref.at[me ^ d], sems.at[d]) for d in range(strips)]
    for copy in copies:
        copy.start()
    for copy in copies:
        copy.wait()

    def put_site(j, part, value):
        site[j, part] = value

    stage(
        lambda p, start: pot_ref[p, :, start : start + lanes],
        flip,
        grid,
        put_site,
        lambda level: disorder * (level * (1.0 / (POT_LEVELS - 1)) - 0.5) - center,
        rows,
        strips,
    )


def filter_kernel(coef_ref, vec_ref, site, out_ref, flip, grid, field, state_a, state_b, *, slabs):
    rows, parts, strips, lanes = field.shape
    total_rows = rows * strips
    blocks = total_rows // lanes
    per_block = lanes // rows
    slab_rows = rows // slabs
    top = coef_ref[DEGREE]

    def put_field(j, part, value):
        field[j, part] = value
        state_a[j + 1, part] = top * value
        state_b[j + 1, part] = jnp.zeros_like(value)

    stage(
        lambda p, start: vec_ref[p, :, start : start + lanes],
        flip,
        grid,
        put_field,
        lambda value: value,
        rows,
        strips,
    )

    def wrap(state):
        for part in range(parts):
            state[0, part] = pltpu.roll(state[rows, part], 1, 0)
            state[rows + 1, part] = pltpu.roll(state[1, part], strips - 1, 0)

    def sweep(new, cur, weight, scale):
        def next_column(line):
            return line[1:] + [pltpu.roll(line[0], lanes - 1, 1)]

        def corner(here, below):
            sums = [a + b for a, b in zip(next_column(here), below)]
            return sums, [pltpu.roll(sums[-1], 1, 1)] + sums[:-1]

        def load(j):
            return [cur[j, part] for part in range(parts)]

        here = load(1)
        _, moved = corner(load(0), here)

        for j in range(rows):
            below = load(j + 2)
            sums, moved_next = corner(here, below)
            for part in range(parts):
                image = site[j, part] * here[part] - (sums[part] + moved[part])
                if scale is not None:
                    image = scale * image
                new[j + 1, part] = image + (weight * field[j, part] - new[j + 1, part])
            here, moved = below, moved_next

    square = coef_ref[DEGREE + 2]
    wrap(state_a)

    def two(step, carry):
        order = DEGREE - 1 - 2 * step
        sweep(state_b, state_a, coef_ref[order], square)
        wrap(state_b)
        sweep(state_a, state_b, coef_ref[order - 1], None)
        wrap(state_a)
        return carry

    lax.fori_loop(0, (DEGREE - 2) // 2, two, 0)
    sweep(state_b, state_a, coef_ref[1], square)
    wrap(state_b)
    sweep(state_a, state_b, coef_ref[0], 0.5)

    for j in range(rows):
        for part in range(parts):
            grid[part, pl.ds(j, strips, stride=rows), :] = state_a[j + 1, part]
    for part in range(parts):
        for block in range(blocks):
            flip[block, pl.ds(part, lanes, stride=parts), :] = grid[part, block * lanes : (block + 1) * lanes, :].T
    for part in range(parts):
        for block in range(blocks):
            tile = flip[block, part * lanes : (part + 1) * lanes, :].T
            for p in range(per_block):
                strip = block * per_block + p
                for slab in range(slabs):
                    start = p * rows + slab * slab_rows
                    group = turned(slab, strip, slabs)
                    out_ref[group, strip, :, part * lanes : (part + 1) * lanes] = tile[start : start + slab_rows]


def outer(left, right):
    return lax.dot_general(
        left,
        right,
        (((1,), (1,)), ((), ())),
        precision=lax.Precision.HIGHEST,
        preferred_element_type=jnp.float32,
    )


def gram_kernel(*refs, chunks):
    slab_refs = refs[:chunks]
    place_ref, pot_ref, out_ref, first_ref, low_ref, high_ref = refs[chunks:]
    slab_rows, total, width = low_ref.shape
    columns = slab_refs[0].shape[2]
    acc = jnp.zeros(out_ref.shape, jnp.float32)
    for chunk in range(chunks):
        for group in range(total // (chunks * SUBLANES)):
            here = slice(group * SUBLANES, (group + 1) * SUBLANES)
            start = (group * chunks + chunk) * SUBLANES
            there = slice(start, start + SUBLANES)
            value = jnp.swapaxes(slab_refs[chunk][here], 0, 1)
            low_ref[:, there, :] = value[:, :, :width]
            high_ref[:, there, :] = value[:, :, width:]
            first_ref[there, :] = value[0]

    def line(j):
        return jnp.concatenate([low_ref[j], high_ref[j]], axis=1)

    levels = pot_ref[pl.ds(pl.multiple_of(place_ref[0] * slab_rows, SUBLANES), slab_rows), :]
    for j in range(slab_rows):
        here = line(j)
        level = levels[j : j + 1, :]
        pot = disorder * (level * (1.0 / (POT_LEVELS - 1)) - 0.5)
        image = pot * here - (pltpu.roll(here, 1, 1) + pltpu.roll(here, columns - 1, 1))
        if j < slab_rows - 1:
            image = image - 2.0 * line(j + 1)
        acc = acc + outer(here, jnp.concatenate([here, image], axis=0))
    out_ref[...] = acc


def edge_kernel(next_ref, low_ref, high_ref, out_ref):
    last = jnp.concatenate([low_ref[0], high_ref[0]], axis=1)
    out_ref[...] = -2.0 * outer(last, next_ref[...])


def eliminate(sums):
    total, width = sums.shape
    blocks = total // SUBLANES
    lane = lax.broadcasted_iota(jnp.int32, (SUBLANES, width), 1)
    sublane = lax.broadcasted_iota(jnp.int32, (SUBLANES, width), 0)
    work = []
    for block in range(blocks):
        unit = (lane == sublane + (total + block * SUBLANES)).astype(jnp.float32)
        work.append(jnp.where(lane < total, sums[block * SUBLANES : (block + 1) * SUBLANES], unit))
    for k in range(total):
        home, inside = k // SUBLANES, k % SUBLANES
        columns = [
            jnp.broadcast_to(work[block][:, k : k + 1], (SUBLANES, width)) for block in range(home, blocks)
        ]
        pivot = columns[0][inside : inside + 1, :]
        row = work[home][inside : inside + 1, :] / pivot
        row = jnp.broadcast_to(row, (SUBLANES, width))
        columns[0] = jnp.where(sublane > inside, columns[0], 0.0)
        for block in range(home, blocks):
            work[block] = work[block] - columns[block - home] * row
    result = []
    for block in range(blocks):
        pivots = jnp.sum(
            jnp.where(lane == sublane + block * SUBLANES, work[block], 0.0), axis=1, keepdims=True
        )
        result.append(work[block] / jnp.sqrt(pivots))
    return jnp.concatenate(result, axis=0)[:, total:]


def products(inv_ref, sources, done_ref, place, scale, targets, half, vec_local):
    first = ((place ^ targets[0]) // half) * half
    weights = scale * inv_ref[pl.ds(pl.multiple_of(first * vec_local, SUBLANES), half * vec_local), :]
    for lines_ref, out_refs, at in sources:
        slab_rows, _, width = lines_ref.shape
        for j in range(slab_rows):
            done_ref[j, :, :width] = jnp.dot(
                weights, lines_ref[j], precision=lax.Precision.HIGHEST, preferred_element_type=jnp.float32
            )
        for d, out_ref in zip(targets, out_refs):
            start = ((place ^ d) - first) * vec_local
            for vec in range(0, vec_local, SUBLANES):
                rows = pl.ds(pl.multiple_of(start + vec, SUBLANES), SUBLANES)
                out_ref[vec : vec + SUBLANES, :, at : at + width] = jnp.swapaxes(
                    done_ref[:, rows, :width], 0, 1
                )


def solve_kernel(place_ref, mine_ref, other_ref, low_ref, high_ref, inv_ref, sums_ref, *rest, **static):
    sums = mine_ref[...] + other_ref[...]
    sums_ref[...] = sums
    inv_ref[...] = eliminate(sums)
    half = static["half"]
    sources = [(low_ref, rest[:half], 0), (high_ref, rest[half : 2 * half], 0)]
    products(inv_ref, sources, rest[-1], place_ref[0], **static)


def near_kernel(place_ref, inv_ref, low_ref, high_ref, *rest, **static):
    sources = [(low_ref, rest[:-1], 0), (high_ref, rest[:-1], low_ref.shape[2])]
    products(inv_ref, sources, rest[-1], place_ref[0], **static)


def extra_kernel(place_ref, inv_ref, lines_ref, *rest, **static):
    products(inv_ref, [(lines_ref, rest[:-1], 0)], rest[-1], place_ref[0], **static)


def whole_shards(start_vectors, potential, bounds):
    vec_local, rows, columns = start_vectors.shape
    strips = lax.axis_size("strip")
    groups = lax.axis_size("vec")
    both = ("vec", "strip")
    total_vecs = vec_local * groups
    vecs = vec_local // strips
    slab_rows = rows // groups
    devices = strips * groups

    coeffs, center, spread = filter_terms(bounds)
    beta = 2.0 / spread
    odd = jnp.arange(DEGREE + 1) % 2 == 1
    terms = jnp.concatenate([jnp.where(odd, beta, 1.0) * coeffs, center[None], (beta * beta)[None]])
    me = lax.axis_index("strip").astype(jnp.int32)
    level = potential.astype(jnp.float32)

    def swap(value, bit):
        return lax.ppermute(value, "strip", [(i, i ^ bit) for i in range(strips)])

    inner = []

    def spread(vectors, chunk):
        part = vectors[chunk * strips : (chunk + 1) * strips]
        inner.append(lax.all_to_all(part, "strip", split_axis=0, concat_axis=0, tiled=True))

    spread(start_vectors, 0)
    beside = swap(level, 1)
    pieces = [swap(level, bit) for bit in range(2, strips, 2)]
    own_pots = jnp.stack(pieces)
    other_pots = swap(own_pots, 1)
    later, _ = lax.optimization_barrier((start_vectors, own_pots))
    for chunk in range(1, vecs):
        spread(later, chunk)

    parts = columns // LANES
    lattice = (rows, parts, strips, LANES)
    padded = (rows + 2, parts, strips, LANES)
    smem = pl.BlockSpec(memory_space=pltpu.SMEM)
    vmem = pl.BlockSpec(memory_space=pltpu.VMEM)
    hbm = pl.BlockSpec(memory_space=pl.ANY)
    slab_shape = jax.ShapeDtypeStruct((groups, strips, slab_rows, columns), jnp.float32)
    staging = [
        pltpu.VMEM((strips * rows // LANES, columns, LANES), jnp.float32),
        pltpu.VMEM((parts, strips * rows, LANES), jnp.float32),
    ]
    site = pl.pallas_call(
        site_kernel,
        in_specs=[smem, smem] + [hbm] * 4,
        out_specs=vmem,
        out_shape=jax.ShapeDtypeStruct(lattice, jnp.float32),
        scratch_shapes=[
            pltpu.VMEM((strips, rows, columns), jnp.float32),
            pltpu.SemaphoreType.DMA((strips,)),
        ]
        + staging,
        name="site",
    )(terms, me[None], level, beside, own_pots, other_pots)
    slabs = []
    holders = [p * groups + turned(s, p, groups) for p in range(strips) for s in range(groups)]
    ring = [(holders[(g + 1) % devices], holders[g]) for g in range(devices)]
    for chunk in range(vecs):
        done = pl.pallas_call(
            functools.partial(filter_kernel, slabs=groups),
            in_specs=[smem, vmem, vmem],
            out_specs=vmem,
            out_shape=slab_shape,
            scratch_shapes=staging
            + [
                pltpu.VMEM(lattice, jnp.float32),
                pltpu.VMEM(padded, jnp.float32),
                pltpu.VMEM(padded, jnp.float32),
            ],
            name="filter",
        )(terms, inner[chunk], site)
        slab = lax.all_to_all(done.reshape(devices, slab_rows, columns), both, split_axis=0, concat_axis=0, tiled=True)
        slabs.append(slab)

    place = lax.axis_index("vec").astype(jnp.int32)
    width = columns - columns // 4
    low_shape = jax.ShapeDtypeStruct((slab_rows, total_vecs, width), jnp.float32)
    high_shape = jax.ShapeDtypeStruct((slab_rows, total_vecs, columns - width), jnp.float32)
    sums_shape = jax.ShapeDtypeStruct((total_vecs, 2 * total_vecs), jnp.float32)
    sums, first_row, low, high = pl.pallas_call(
        functools.partial(gram_kernel, chunks=vecs),
        in_specs=[vmem] * vecs + [smem, vmem],
        out_specs=[vmem] * 4,
        out_shape=[
            sums_shape,
            jax.ShapeDtypeStruct((total_vecs, columns), jnp.float32),
            low_shape,
            high_shape,
        ],
        name="gram",
    )(*slabs, turned(place, me, groups)[None], level)
    next_row = lax.ppermute(first_row, ("strip", "vec"), ring)
    half = groups // 2
    middle = (half - 1, half)
    raw = lax.ppermute(high, "vec", [middle, middle[::-1]])
    last_low, last_high = (
        pl.BlockSpec((1, total_vecs, part.shape[2]), lambda i: (slab_rows - 1, 0, 0))
        for part in (low_shape, high_shape)
    )
    edge = pl.pallas_call(
        edge_kernel,
        grid=(1,),
        in_specs=[vmem, last_low, last_high],
        out_specs=vmem,
        out_shape=jax.ShapeDtypeStruct((total_vecs, total_vecs), jnp.float32),
        name="edge",
    )(next_row, low, high)

    def pairwise(value, order):
        rounds = [(axis, count, 1 << n) for axis, count in order for n in range(count.bit_length() - 1)]
        for number, (axis, count, bit) in enumerate(rounds):
            other = lax.ppermute(value, axis, [(i, i ^ bit) for i in range(count)])
            if number < len(rounds) - 1:
                value = value + other
        return value, other

    sums, pending = pairwise(sums, (("vec", groups), ("strip", strips)))
    mine, other = pairwise(edge, (("strip", strips),))
    edge = mine + other
    others = []
    for d in range(1, groups):
        others.append(lax.ppermute(edge, "vec", [(i, i ^ d) for i in range(groups)]))
    edge = edge + sum(others)

    static = dict(scale=math.sqrt(strips * rows * columns), half=half, vec_local=vec_local)
    far, near = tuple(range(half, groups)), tuple(range(half))
    piece = jax.ShapeDtypeStruct((vec_local, slab_rows, columns), jnp.float32)
    low_piece = jax.ShapeDtypeStruct((vec_local, slab_rows, width), jnp.float32)
    high_piece = jax.ShapeDtypeStruct((vec_local, slab_rows, columns - width), jnp.float32)
    products_scratch = [pltpu.VMEM((slab_rows, half * vec_local, width), jnp.float32)]
    inverse, gram_cross, *blocks = pl.pallas_call(
        functools.partial(solve_kernel, targets=far, **static),
        in_specs=[smem] + [vmem] * 4,
        out_specs=[vmem] * (2 + 2 * half),
        out_shape=[jax.ShapeDtypeStruct((total_vecs, total_vecs), jnp.float32), sums_shape]
        + [low_piece] * half
        + [high_piece] * half,
        scratch_shapes=products_scratch,
        name="solve",
    )(place[None], sums, pending, low, high)
    own_block, beside_block = pl.pallas_call(
        functools.partial(near_kernel, targets=near, **static),
        in_specs=[smem] + [vmem] * 3,
        out_specs=[vmem] * half,
        out_shape=[piece] * half,
        scratch_shapes=products_scratch,
        name="near",
    )(place[None], inverse, low, high)
    own_extra, beside_extra = pl.pallas_call(
        functools.partial(extra_kernel, targets=near, **static),
        in_specs=[smem] + [vmem] * 2,
        out_specs=[vmem] * half,
        out_shape=[high_piece] * half,
        scratch_shapes=products_scratch,
        name="extra",
    )(place[None], inverse, raw)

    def across(block, d, sources=range(groups)):
        return lax.ppermute(block, "vec", [(i, i ^ d) for i in sources])

    outer_groups = [i for i in range(groups) if i not in middle]
    far_high = [across(block, d, outer_groups) for d, block in zip(far, blocks[half:])]
    far_low = [across(block, d) for d, block in zip(far, blocks[:half])]
    beside_block = across(beside_block, 1)
    beside_extra = across(beside_extra, 1, middle)
    far_high = [far_high[0] + beside_extra, far_high[1] + own_extra]

    ortho_basis = jnp.zeros((vec_local, rows, columns), jnp.float32)
    for d, block, at in (
        (0, own_block, 0),
        (1, beside_block, 0),
        (2, far_low[0], 0),
        (3, far_low[1], 0),
        (2, far_high[0], width),
        (3, far_high[1], width),
    ):
        start = turned(place ^ d, me, groups) * slab_rows
        ortho_basis = lax.dynamic_update_slice(ortho_basis, block, (0, start, at))

    cross_half = gram_cross[:, total_vecs:] + edge
    cross_sum = 0.5 * (cross_half + cross_half.T)
    half_done = jnp.dot(inverse, cross_sum, precision=lax.Precision.HIGHEST)
    ritz_matrix = float(rows) * jnp.dot(inverse, half_done.T, precision=lax.Precision.HIGHEST)
    return (ortho_basis, ritz_matrix)


def is_whole(vec_local, rows, columns, strips, groups):
    devices = strips * groups
    return (
        strips == SUBLANES
        and vec_local % strips == 0
        and rows % (groups * SUBLANES) == 0
        and columns % (LANES * SUBLANES) == 0
        and LANES % rows == 0
        and strips * rows % LANES == 0
        and groups == 4
        and devices & (devices - 1) == 0
        and vec_local % SUBLANES == 0
        and 2 * vec_local * groups == LANES
        and DEGREE % 2 == 0
    )


def solution(mesh):
    strips, groups = mesh.shape["strip"], mesh.shape["vec"]
    in_specs = (P("vec", "strip", None), P("strip", None), P())
    out_specs = (P("vec", "strip", None), P())

    def step(start_vectors, potential, bounds):
        total_vecs, total_rows, columns = start_vectors.shape
        vec_local, rows = total_vecs // groups, total_rows // strips
        whole = is_whole(vec_local, rows, columns, strips, groups)

        def form(*local):
            return (whole_shards if whole else halo_shards)(*local)

        sharded = jax.shard_map(form, mesh=mesh, in_specs=in_specs, out_specs=out_specs, check_vma=False)
        return sharded(start_vectors, potential, bounds)

    return step
```

```python
import functools
import math

import jax
import jax.numpy as jnp
from jax import lax
from jax.experimental import pallas as pl
from jax.experimental.pallas import tpu as pltpu
from jax.sharding import PartitionSpec as P

DEGREE = 32
DEPTH = 8
POT_LEVELS = 16
LANES = 128
SUBLANES = 8

grid_unit = 0.0625
disorder = 2.0


def filter_terms(bounds):
    edges = bounds.astype(jnp.float32) * grid_unit
    center = (edges[0] + edges[1]) * 0.5
    spread = (edges[1] - edges[0]) * 0.5
    theta_lo = jnp.arccos((edges[2] - center) / spread)
    theta_hi = jnp.arccos((edges[3] - center) / spread)
    orders = jnp.arange(1, DEGREE + 1).astype(jnp.float32)
    others = 2.0 * (jnp.sin(orders * theta_lo) - jnp.sin(orders * theta_hi)) / (orders * math.pi)
    first = jnp.reshape((theta_lo - theta_hi) / math.pi, (1,))
    return (jnp.concatenate([first, others]), center, spread)


def extended(value, sides, width):
    for axis, dim in sides:
        count, length = (lax.axis_size(axis), value.shape[dim])
        up = [(i, (i + 1) % count) for i in range(count)]
        down = [(j, i) for i, j in up]
        last = lax.slice_in_dim(value, length - width, length, axis=dim)
        leading = lax.slice_in_dim(value, 0, width, axis=dim)
        before = lax.ppermute(last, axis, up)
        after = lax.ppermute(leading, axis, down)
        value = jnp.concatenate([before, value, after], axis=dim)
    return value


def stencil(padded, pot_rows, center, spread):
    middle = padded[:, 1:-1]
    beside = padded[:, 2:] + padded[:, :-2] + jnp.roll(middle, 1, 2) + jnp.roll(middle, -1, 2)
    return ((pot_rows[None] - center) * middle - beside) / spread


def deep_filter(start_vectors, pot_padded, coeffs, center, spread):
    rows = start_vectors.shape[1]

    def one_round(rounds, carry):
        before, current, filtered = carry
        stacked = jnp.stack([before, current])
        padded = extended(stacked, (("strip", 2),), DEPTH)
        old_part = padded[0]
        new_part = padded[1]
        for inner in range(DEPTH):
            counter = rounds * DEPTH + inner
            factor = jnp.where(counter == 0, 1.0, 2.0).astype(jnp.float32)
            pot_rows = pot_padded[inner + 1 : rows + 2 * DEPTH - inner - 1]
            after = factor * stencil(new_part, pot_rows, center, spread) - old_part[:, 1:-1]
            offset = DEPTH - inner - 1
            filtered = filtered + coeffs[counter + 1] * after[:, offset : offset + rows]
            old_part = new_part[:, 1:-1]
            new_part = after
        return (old_part, new_part, filtered)

    initial = (jnp.zeros_like(start_vectors), start_vectors, coeffs[0] * start_vectors)
    return lax.fori_loop(0, DEGREE // DEPTH, one_round, initial)[2]


def halo_shards(start_vectors, potential, bounds):
    _, rows, columns = start_vectors.shape
    pot_field = disorder * (potential.astype(jnp.float32) / (POT_LEVELS - 1) - 0.5)
    coeffs, center, spread = filter_terms(bounds)
    pot_padded = extended(pot_field, (("strip", 0),), DEPTH)
    filtered = deep_filter(start_vectors, pot_padded, coeffs, center, spread)
    padded = extended(filtered, (("strip", 1),), 1)
    applied = stencil(padded, pot_field, 0.0, 1.0)
    slab_vecs, slab_applied = (
        lax.all_to_all(filtered, "vec", split_axis=1, concat_axis=0, tiled=True),
        lax.all_to_all(applied, "vec", split_axis=1, concat_axis=0, tiled=True),
    )
    total_vecs = slab_vecs.shape[0]
    y_rows = slab_vecs.reshape(total_vecs, -1)
    hy_rows = slab_applied.reshape(total_vecs, -1)
    gram_part = jnp.dot(
        y_rows, y_rows.T, precision=lax.Precision.HIGHEST, preferred_element_type=jnp.float32
    )
    cross_part = jnp.dot(
        y_rows, hy_rows.T, precision=lax.Precision.HIGHEST, preferred_element_type=jnp.float32
    )
    gram_sum, cross_sum = lax.psum((gram_part, cross_part), ("strip", "vec"))
    lower_factor = jnp.linalg.cholesky(gram_sum)
    site_count = lax.axis_size("strip") * rows * columns
    ortho = jax.scipy.linalg.solve_triangular(lower_factor, y_rows, lower=True)
    ortho_slab = (math.sqrt(site_count) * ortho).reshape(slab_vecs.shape)
    ortho_basis = lax.all_to_all(ortho_slab, "vec", split_axis=0, concat_axis=1, tiled=True)
    half_done = jax.scipy.linalg.solve_triangular(lower_factor, cross_sum, lower=True)
    ritz_matrix = float(rows) * jax.scipy.linalg.solve_triangular(
        lower_factor, half_done.T, lower=True
    )
    return (ortho_basis, ritz_matrix)


def turned(group, strip, groups):
    odd = strip % 2
    return group + odd * (groups - 1 - 2 * group)


def stage(read, flip, grid, target, change, rows, strips):
    parts, total_rows, lanes = grid.shape
    blocks = total_rows // lanes
    per_block = lanes // rows
    for part in range(parts):
        for block in range(blocks):
            tile = jnp.concatenate(
                [read(block * per_block + p, part * lanes) for p in range(per_block)], axis=0
            )
            flip[block, part * lanes : (part + 1) * lanes, :] = tile.T
    for part in range(parts):
        for block in range(blocks):
            tile = flip[block, pl.ds(part, lanes, stride=parts), :]
            grid[part, block * lanes : (block + 1) * lanes, :] = tile.T
    for j in range(rows):
        for part in range(parts):
            target(j, part, change(grid[part, pl.ds(j, strips, stride=rows), :]))


def site_kernel(coef_ref, me_ref, here_ref, beside_ref, own_ref, other_ref, site, pot_ref, sems, flip, grid):
    rows, _, strips, lanes = site.shape
    center = coef_ref[DEGREE + 1]
    me = me_ref[0]
    sources = [here_ref, beside_ref]
    for d in range(2, strips):
        sources.append((own_ref, other_ref)[d & 1].at[(d >> 1) - 1])
    copies = [pltpu.make_async_copy(sources[d], pot_ref.at[me ^ d], sems.at[d]) for d in range(strips)]
    for copy in copies:
        copy.start()
    for copy in copies:
        copy.wait()

    def put_site(j, part, value):
        site[j, part] = value

    stage(
        lambda p, start: pot_ref[p, :, start : start + lanes],
        flip,
        grid,
        put_site,
        lambda level: disorder * (level * (1.0 / (POT_LEVELS - 1)) - 0.5) - center,
        rows,
        strips,
    )


def filter_kernel(coef_ref, vec_ref, site, out_ref, flip, grid, field, state_a, state_b, *, slabs):
    rows, parts, strips, lanes = field.shape
    total_rows = rows * strips
    blocks = total_rows // lanes
    per_block = lanes // rows
    slab_rows = rows // slabs
    top = coef_ref[DEGREE]

    def put_field(j, part, value):
        field[j, part] = value
        state_a[j + 1, part] = top * value
        state_b[j + 1, part] = jnp.zeros_like(value)

    stage(
        lambda p, start: vec_ref[p, :, start : start + lanes],
        flip,
        grid,
        put_field,
        lambda value: value,
        rows,
        strips,
    )

    def wrap(state):
        for part in range(parts):
            state[0, part] = pltpu.roll(state[rows, part], 1, 0)
            state[rows + 1, part] = pltpu.roll(state[1, part], strips - 1, 0)

    def sweep(new, cur, weight, scale):
        def next_column(line):
            return line[1:] + [pltpu.roll(line[0], lanes - 1, 1)]

        def corner(here, below):
            sums = [a + b for a, b in zip(next_column(here), below)]
            return sums, [pltpu.roll(sums[-1], 1, 1)] + sums[:-1]

        def load(j):
            return [cur[j, part] for part in range(parts)]

        here = load(1)
        _, moved = corner(load(0), here)

        for j in range(rows):
            below = load(j + 2)
            sums, moved_next = corner(here, below)
            for part in range(parts):
                image = site[j, part] * here[part] - (sums[part] + moved[part])
                if scale is not None:
                    image = scale * image
                new[j + 1, part] = image + (weight * field[j, part] - new[j + 1, part])
            here, moved = below, moved_next

    square = coef_ref[DEGREE + 2]
    wrap(state_a)

    def two(step, carry):
        order = DEGREE - 1 - 2 * step
        sweep(state_b, state_a, coef_ref[order], square)
        wrap(state_b)
        sweep(state_a, state_b, coef_ref[order - 1], None)
        wrap(state_a)
        return carry

    lax.fori_loop(0, (DEGREE - 2) // 2, two, 0)
    sweep(state_b, state_a, coef_ref[1], square)
    wrap(state_b)
    sweep(state_a, state_b, coef_ref[0], 0.5)

    for j in range(rows):
        for part in range(parts):
            grid[part, pl.ds(j, strips, stride=rows), :] = state_a[j + 1, part]
    for part in range(parts):
        for block in range(blocks):
            flip[block, pl.ds(part, lanes, stride=parts), :] = grid[part, block * lanes : (block + 1) * lanes, :].T
    for part in range(parts):
        for block in range(blocks):
            tile = flip[block, part * lanes : (part + 1) * lanes, :].T
            for p in range(per_block):
                strip = block * per_block + p
                for slab in range(slabs):
                    start = p * rows + slab * slab_rows
                    group = turned(slab, strip, slabs)
                    out_ref[group, strip, :, part * lanes : (part + 1) * lanes] = tile[start : start + slab_rows]


def outer(left, right):
    return lax.dot_general(
        left,
        right,
        (((1,), (1,)), ((), ())),
        precision=lax.Precision.HIGHEST,
        preferred_element_type=jnp.float32,
    )


def gram_kernel(*refs, chunks):
    slab_refs = refs[:chunks]
    place_ref, pot_ref, out_ref, first_ref, low_ref, high_ref = refs[chunks:]
    slab_rows, total, width = low_ref.shape
    columns = slab_refs[0].shape[2]
    acc = jnp.zeros(out_ref.shape, jnp.float32)
    for chunk in range(chunks):
        for group in range(total // (chunks * SUBLANES)):
            here = slice(group * SUBLANES, (group + 1) * SUBLANES)
            start = (group * chunks + chunk) * SUBLANES
            there = slice(start, start + SUBLANES)
            value = jnp.swapaxes(slab_refs[chunk][here], 0, 1)
            low_ref[:, there, :] = value[:, :, :width]
            high_ref[:, there, :] = value[:, :, width:]
            first_ref[there, :] = value[0]

    def line(j):
        return jnp.concatenate([low_ref[j], high_ref[j]], axis=1)

    levels = pot_ref[pl.ds(pl.multiple_of(place_ref[0] * slab_rows, SUBLANES), slab_rows), :]
    for j in range(slab_rows):
        here = line(j)
        level = levels[j : j + 1, :]
        pot = disorder * (level * (1.0 / (POT_LEVELS - 1)) - 0.5)
        image = pot * here - (pltpu.roll(here, 1, 1) + pltpu.roll(here, columns - 1, 1))
        if j < slab_rows - 1:
            image = image - 2.0 * line(j + 1)
        acc = acc + outer(here, jnp.concatenate([here, image], axis=0))
    out_ref[...] = acc


def edge_kernel(next_ref, low_ref, high_ref, out_ref):
    last = jnp.concatenate([low_ref[0], high_ref[0]], axis=1)
    out_ref[...] = -2.0 * outer(last, next_ref[...])


def eliminate(sums):
    total, width = sums.shape
    blocks = total // SUBLANES
    lane = lax.broadcasted_iota(jnp.int32, (SUBLANES, width), 1)
    sublane = lax.broadcasted_iota(jnp.int32, (SUBLANES, width), 0)
    work = []
    for block in range(blocks):
        unit = (lane == sublane + (total + block * SUBLANES)).astype(jnp.float32)
        work.append(jnp.where(lane < total, sums[block * SUBLANES : (block + 1) * SUBLANES], unit))
    for k in range(0, total, 2):
        home, inside = k // SUBLANES, k % SUBLANES

        def column(k):
            return [
                jnp.broadcast_to(work[block][:, k : k + 1], (SUBLANES, width)) for block in range(home, blocks)
            ]

        one, two = column(k), column(k + 1)
        upper, lower = slice(inside, inside + 1), slice(inside + 1, inside + 2)
        inverse = 1.0 / one[0][upper]
        shared = two[0][upper] * inverse
        ratio = one[0][lower] * inverse
        row_one = work[home][upper]
        row_two = work[home][lower] - ratio * row_one
        row_two = row_two * (1.0 / (two[0][lower] - ratio * two[0][upper]))
        row_one = jnp.broadcast_to(row_one * inverse, (SUBLANES, width))
        row_two = jnp.broadcast_to(row_two, (SUBLANES, width))
        for block in range(home, blocks):
            first = one[block - home]
            second = two[block - home] - first * shared
            if block == home:
                first = jnp.where(sublane > inside, first, 0.0)
                second = jnp.where(sublane > inside + 1, second, 0.0)
            work[block] = work[block] - (first * row_one + second * row_two)
    result = []
    for block in range(blocks):
        pivots = jnp.sum(
            jnp.where(lane == sublane + block * SUBLANES, work[block], 0.0), axis=1, keepdims=True
        )
        result.append(work[block] / jnp.sqrt(pivots))
    return jnp.concatenate(result, axis=0)[:, total:]


def products(inv_ref, sources, done_ref, place, scale, targets, half, vec_local):
    first = ((place ^ targets[0]) // half) * half
    weights = scale * inv_ref[pl.ds(pl.multiple_of(first * vec_local, SUBLANES), half * vec_local), :]
    for lines_ref, begin, width, out_refs, at in sources:
        for j in range(lines_ref.shape[0]):
            done_ref[j, :, :width] = jnp.dot(
                weights,
                lines_ref[j, :, begin : begin + width],
                precision=lax.Precision.HIGHEST,
                preferred_element_type=jnp.float32,
            )
        for d, out_ref in zip(targets, out_refs):
            start = ((place ^ d) - first) * vec_local
            for vec in range(0, vec_local, SUBLANES):
                rows = pl.ds(pl.multiple_of(start + vec, SUBLANES), SUBLANES)
                out_ref[vec : vec + SUBLANES, :, at : at + width] = jnp.swapaxes(
                    done_ref[:, rows, :width], 0, 1
                )


def solve_kernel(place_ref, mine_ref, other_ref, low_ref, inv_ref, sums_ref, *rest, **static):
    sums = mine_ref[...] + other_ref[...]
    sums_ref[...] = sums
    inv_ref[...] = eliminate(sums)
    head = rest[0].shape[2]
    products(inv_ref, [(low_ref, 0, head, rest[:-1], 0)], rest[-1], place_ref[0], **static)


def rest_kernel(place_ref, inv_ref, low_ref, high_ref, *rest, **static):
    half, tail = static["half"], rest[0].shape[2]
    sources = [
        (low_ref, low_ref.shape[2] - tail, tail, rest[:half], 0),
        (high_ref, 0, high_ref.shape[2], rest[half : 2 * half], 0),
    ]
    products(inv_ref, sources, rest[-1], place_ref[0], **static)


def near_kernel(place_ref, inv_ref, low_ref, high_ref, *rest, **static):
    low, high = low_ref.shape[2], high_ref.shape[2]
    sources = [(low_ref, 0, low, rest[:-1], 0), (high_ref, 0, high, rest[:-1], low)]
    products(inv_ref, sources, rest[-1], place_ref[0], **static)


def extra_kernel(place_ref, inv_ref, lines_ref, *rest, **static):
    products(inv_ref, [(lines_ref, 0, lines_ref.shape[2], rest[:-1], 0)], rest[-1], place_ref[0], **static)


def whole_shards(start_vectors, potential, bounds):
    vec_local, rows, columns = start_vectors.shape
    strips = lax.axis_size("strip")
    groups = lax.axis_size("vec")
    both = ("vec", "strip")
    total_vecs = vec_local * groups
    vecs = vec_local // strips
    slab_rows = rows // groups
    devices = strips * groups

    coeffs, center, spread = filter_terms(bounds)
    beta = 2.0 / spread
    odd = jnp.arange(DEGREE + 1) % 2 == 1
    terms = jnp.concatenate([jnp.where(odd, beta, 1.0) * coeffs, center[None], (beta * beta)[None]])
    me = lax.axis_index("strip").astype(jnp.int32)
    level = potential.astype(jnp.float32)

    def swap(value, bit):
        return lax.ppermute(value, "strip", [(i, i ^ bit) for i in range(strips)])

    inner = []

    def spread(vectors, chunk):
        part = vectors[chunk * strips : (chunk + 1) * strips]
        inner.append(lax.all_to_all(part, "strip", split_axis=0, concat_axis=0, tiled=True))

    spread(start_vectors, 0)
    beside = swap(level, 1)
    pieces = [swap(level, bit) for bit in range(2, strips, 2)]
    own_pots = jnp.stack(pieces)
    other_pots = swap(own_pots, 1)
    later, _ = lax.optimization_barrier((start_vectors, own_pots))
    for chunk in range(1, vecs):
        spread(later, chunk)

    parts = columns // LANES
    lattice = (rows, parts, strips, LANES)
    padded = (rows + 2, parts, strips, LANES)
    smem = pl.BlockSpec(memory_space=pltpu.SMEM)
    vmem = pl.BlockSpec(memory_space=pltpu.VMEM)
    hbm = pl.BlockSpec(memory_space=pl.ANY)
    slab_shape = jax.ShapeDtypeStruct((groups, strips, slab_rows, columns), jnp.float32)
    staging = [
        pltpu.VMEM((strips * rows // LANES, columns, LANES), jnp.float32),
        pltpu.VMEM((parts, strips * rows, LANES), jnp.float32),
    ]
    site = pl.pallas_call(
        site_kernel,
        in_specs=[smem, smem] + [hbm] * 4,
        out_specs=vmem,
        out_shape=jax.ShapeDtypeStruct(lattice, jnp.float32),
        scratch_shapes=[
            pltpu.VMEM((strips, rows, columns), jnp.float32),
            pltpu.SemaphoreType.DMA((strips,)),
        ]
        + staging,
        name="site",
    )(terms, me[None], level, beside, own_pots, other_pots)
    slabs = []
    holders = [p * groups + turned(s, p, groups) for p in range(strips) for s in range(groups)]
    ring = [(holders[(g + 1) % devices], holders[g]) for g in range(devices)]
    for chunk in range(vecs):
        done = pl.pallas_call(
            functools.partial(filter_kernel, slabs=groups),
            in_specs=[smem, vmem, vmem],
            out_specs=vmem,
            out_shape=slab_shape,
            scratch_shapes=staging
            + [
                pltpu.VMEM(lattice, jnp.float32),
                pltpu.VMEM(padded, jnp.float32),
                pltpu.VMEM(padded, jnp.float32),
            ],
            name="filter",
        )(terms, inner[chunk], site)
        slab = lax.all_to_all(done.reshape(devices, slab_rows, columns), both, split_axis=0, concat_axis=0, tiled=True)
        slabs.append(slab)

    place = lax.axis_index("vec").astype(jnp.int32)
    width = columns - columns // 4
    low_shape = jax.ShapeDtypeStruct((slab_rows, total_vecs, width), jnp.float32)
    high_shape = jax.ShapeDtypeStruct((slab_rows, total_vecs, columns - width), jnp.float32)
    sums_shape = jax.ShapeDtypeStruct((total_vecs, 2 * total_vecs), jnp.float32)
    sums, first_row, low, high = pl.pallas_call(
        functools.partial(gram_kernel, chunks=vecs),
        in_specs=[vmem] * vecs + [smem, vmem],
        out_specs=[vmem] * 4,
        out_shape=[
            sums_shape,
            jax.ShapeDtypeStruct((total_vecs, columns), jnp.float32),
            low_shape,
            high_shape,
        ],
        name="gram",
    )(*slabs, turned(place, me, groups)[None], level)
    next_row = lax.ppermute(first_row, ("strip", "vec"), ring)
    half = groups // 2
    middle = (half - 1, half)
    raw = lax.ppermute(high, "vec", [middle, middle[::-1]])
    last_low, last_high = (
        pl.BlockSpec((1, total_vecs, part.shape[2]), lambda i: (slab_rows - 1, 0, 0))
        for part in (low_shape, high_shape)
    )
    edge = pl.pallas_call(
        edge_kernel,
        grid=(1,),
        in_specs=[vmem, last_low, last_high],
        out_specs=vmem,
        out_shape=jax.ShapeDtypeStruct((total_vecs, total_vecs), jnp.float32),
        name="edge",
    )(next_row, low, high)

    def pairwise(value, order):
        rounds = [(axis, count, 1 << n) for axis, count in order for n in range(count.bit_length() - 1)]
        for number, (axis, count, bit) in enumerate(rounds):
            other = lax.ppermute(value, axis, [(i, i ^ bit) for i in range(count)])
            if number < len(rounds) - 1:
                value = value + other
        return value, other

    sums, pending = pairwise(sums, (("vec", groups), ("strip", strips)))
    mine, other = pairwise(edge, (("strip", strips),))
    edge = mine + other
    others = []
    for d in range(1, groups):
        others.append(lax.ppermute(edge, "vec", [(i, i ^ d) for i in range(groups)]))
    edge = edge + sum(others)

    static = dict(scale=math.sqrt(strips * rows * columns), half=half, vec_local=vec_local)
    far, near = tuple(range(half, groups)), tuple(range(half))
    piece = jax.ShapeDtypeStruct((vec_local, slab_rows, columns), jnp.float32)
    head = columns // 4
    head_piece = jax.ShapeDtypeStruct((vec_local, slab_rows, head), jnp.float32)
    tail_piece = jax.ShapeDtypeStruct((vec_local, slab_rows, width - head), jnp.float32)
    high_piece = jax.ShapeDtypeStruct((vec_local, slab_rows, columns - width), jnp.float32)
    products_scratch = [pltpu.VMEM((slab_rows, half * vec_local, width), jnp.float32)]
    inverse, gram_cross, *heads = pl.pallas_call(
        functools.partial(solve_kernel, targets=far, **static),
        in_specs=[smem] + [vmem] * 3,
        out_specs=[vmem] * (2 + half),
        out_shape=[jax.ShapeDtypeStruct((total_vecs, total_vecs), jnp.float32), sums_shape]
        + [head_piece] * half,
        scratch_shapes=products_scratch,
        name="solve",
    )(place[None], sums, pending, low)
    blocks = pl.pallas_call(
        functools.partial(rest_kernel, targets=far, **static),
        in_specs=[smem] + [vmem] * 3,
        out_specs=[vmem] * (2 * half),
        out_shape=[tail_piece] * half + [high_piece] * half,
        scratch_shapes=products_scratch,
        name="rest",
    )(place[None], inverse, low, high)
    own_block, beside_block = pl.pallas_call(
        functools.partial(near_kernel, targets=near, **static),
        in_specs=[smem] + [vmem] * 3,
        out_specs=[vmem] * half,
        out_shape=[piece] * half,
        scratch_shapes=products_scratch,
        name="near",
    )(place[None], inverse, low, high)
    own_extra, beside_extra = pl.pallas_call(
        functools.partial(extra_kernel, targets=near, **static),
        in_specs=[smem] + [vmem] * 2,
        out_specs=[vmem] * half,
        out_shape=[high_piece] * half,
        scratch_shapes=products_scratch,
        name="extra",
    )(place[None], inverse, raw)

    def across(block, d, sources=range(groups)):
        return lax.ppermute(block, "vec", [(i, i ^ d) for i in sources])

    outer_groups = [i for i in range(groups) if i not in middle]
    far_high = [across(block, d, outer_groups) for d, block in zip(far, blocks[half:])]
    far_head = [across(block, d) for d, block in zip(far, heads)]
    far_tail = [across(block, d) for d, block in zip(far, blocks[:half])]
    beside_block = across(beside_block, 1)
    beside_extra = across(beside_extra, 1, middle)
    far_high = [far_high[0] + beside_extra, far_high[1] + own_extra]

    ortho_basis = jnp.zeros((vec_local, rows, columns), jnp.float32)
    for d, block, at in (
        (0, own_block, 0),
        (1, beside_block, 0),
        (2, far_head[0], 0),
        (3, far_head[1], 0),
        (2, far_tail[0], head),
        (3, far_tail[1], head),
        (2, far_high[0], width),
        (3, far_high[1], width),
    ):
        start = turned(place ^ d, me, groups) * slab_rows
        ortho_basis = lax.dynamic_update_slice(ortho_basis, block, (0, start, at))

    cross_half = gram_cross[:, total_vecs:] + edge
    cross_sum = 0.5 * (cross_half + cross_half.T)
    half_done = jnp.dot(inverse, cross_sum, precision=lax.Precision.HIGHEST)
    ritz_matrix = float(rows) * jnp.dot(inverse, half_done.T, precision=lax.Precision.HIGHEST)
    return (ortho_basis, ritz_matrix)


def is_whole(vec_local, rows, columns, strips, groups):
    devices = strips * groups
    return (
        strips == SUBLANES
        and vec_local % strips == 0
        and rows % (groups * SUBLANES) == 0
        and columns % (LANES * SUBLANES) == 0
        and LANES % rows == 0
        and strips * rows % LANES == 0
        and groups == 4
        and devices & (devices - 1) == 0
        and vec_local % SUBLANES == 0
        and 2 * vec_local * groups == LANES
        and DEGREE % 2 == 0
    )


def solution(mesh):
    strips, groups = mesh.shape["strip"], mesh.shape["vec"]
    in_specs = (P("vec", "strip", None), P("strip", None), P())
    out_specs = (P("vec", "strip", None), P())

    def step(start_vectors, potential, bounds):
        total_vecs, total_rows, columns = start_vectors.shape
        vec_local, rows = total_vecs // groups, total_rows // strips
        whole = is_whole(vec_local, rows, columns, strips, groups)

        def form(*local):
            return (whole_shards if whole else halo_shards)(*local)

        sharded = jax.shard_map(form, mesh=mesh, in_specs=in_specs, out_specs=out_specs, check_vma=False)
        return sharded(start_vectors, potential, bounds)

    return step
```

```python
import functools
import math

import jax
import jax.numpy as jnp
from jax import lax
from jax.experimental import pallas as pl
from jax.experimental.pallas import tpu as pltpu
from jax.sharding import PartitionSpec as P

DEGREE = 32
DEPTH = 8
POT_LEVELS = 16
LANES = 128
SUBLANES = 8

grid_unit = 0.0625
disorder = 2.0


def filter_terms(bounds):
    edges = bounds.astype(jnp.float32) * grid_unit
    center = (edges[0] + edges[1]) * 0.5
    spread = (edges[1] - edges[0]) * 0.5
    theta_lo = jnp.arccos((edges[2] - center) / spread)
    theta_hi = jnp.arccos((edges[3] - center) / spread)
    orders = jnp.arange(1, DEGREE + 1).astype(jnp.float32)
    others = 2.0 * (jnp.sin(orders * theta_lo) - jnp.sin(orders * theta_hi)) / (orders * math.pi)
    first = jnp.reshape((theta_lo - theta_hi) / math.pi, (1,))
    return (jnp.concatenate([first, others]), center, spread)


def extended(value, sides, width):
    for axis, dim in sides:
        count, length = (lax.axis_size(axis), value.shape[dim])
        up = [(i, (i + 1) % count) for i in range(count)]
        down = [(j, i) for i, j in up]
        last = lax.slice_in_dim(value, length - width, length, axis=dim)
        leading = lax.slice_in_dim(value, 0, width, axis=dim)
        before = lax.ppermute(last, axis, up)
        after = lax.ppermute(leading, axis, down)
        value = jnp.concatenate([before, value, after], axis=dim)
    return value


def stencil(padded, pot_rows, center, spread):
    middle = padded[:, 1:-1]
    beside = padded[:, 2:] + padded[:, :-2] + jnp.roll(middle, 1, 2) + jnp.roll(middle, -1, 2)
    return ((pot_rows[None] - center) * middle - beside) / spread


def deep_filter(start_vectors, pot_padded, coeffs, center, spread):
    rows = start_vectors.shape[1]

    def one_round(rounds, carry):
        before, current, filtered = carry
        stacked = jnp.stack([before, current])
        padded = extended(stacked, (("strip", 2),), DEPTH)
        old_part = padded[0]
        new_part = padded[1]
        for inner in range(DEPTH):
            counter = rounds * DEPTH + inner
            factor = jnp.where(counter == 0, 1.0, 2.0).astype(jnp.float32)
            pot_rows = pot_padded[inner + 1 : rows + 2 * DEPTH - inner - 1]
            after = factor * stencil(new_part, pot_rows, center, spread) - old_part[:, 1:-1]
            offset = DEPTH - inner - 1
            filtered = filtered + coeffs[counter + 1] * after[:, offset : offset + rows]
            old_part = new_part[:, 1:-1]
            new_part = after
        return (old_part, new_part, filtered)

    initial = (jnp.zeros_like(start_vectors), start_vectors, coeffs[0] * start_vectors)
    return lax.fori_loop(0, DEGREE // DEPTH, one_round, initial)[2]


def halo_shards(start_vectors, potential, bounds):
    _, rows, columns = start_vectors.shape
    pot_field = disorder * (potential.astype(jnp.float32) / (POT_LEVELS - 1) - 0.5)
    coeffs, center, spread = filter_terms(bounds)
    pot_padded = extended(pot_field, (("strip", 0),), DEPTH)
    filtered = deep_filter(start_vectors, pot_padded, coeffs, center, spread)
    padded = extended(filtered, (("strip", 1),), 1)
    applied = stencil(padded, pot_field, 0.0, 1.0)
    slab_vecs, slab_applied = (
        lax.all_to_all(filtered, "vec", split_axis=1, concat_axis=0, tiled=True),
        lax.all_to_all(applied, "vec", split_axis=1, concat_axis=0, tiled=True),
    )
    total_vecs = slab_vecs.shape[0]
    y_rows = slab_vecs.reshape(total_vecs, -1)
    hy_rows = slab_applied.reshape(total_vecs, -1)
    gram_part = jnp.dot(
        y_rows, y_rows.T, precision=lax.Precision.HIGHEST, preferred_element_type=jnp.float32
    )
    cross_part = jnp.dot(
        y_rows, hy_rows.T, precision=lax.Precision.HIGHEST, preferred_element_type=jnp.float32
    )
    gram_sum, cross_sum = lax.psum((gram_part, cross_part), ("strip", "vec"))
    lower_factor = jnp.linalg.cholesky(gram_sum)
    site_count = lax.axis_size("strip") * rows * columns
    ortho = jax.scipy.linalg.solve_triangular(lower_factor, y_rows, lower=True)
    ortho_slab = (math.sqrt(site_count) * ortho).reshape(slab_vecs.shape)
    ortho_basis = lax.all_to_all(ortho_slab, "vec", split_axis=0, concat_axis=1, tiled=True)
    half_done = jax.scipy.linalg.solve_triangular(lower_factor, cross_sum, lower=True)
    ritz_matrix = float(rows) * jax.scipy.linalg.solve_triangular(
        lower_factor, half_done.T, lower=True
    )
    return (ortho_basis, ritz_matrix)


def turned(group, strip, groups):
    odd = strip % 2
    return group + odd * (groups - 1 - 2 * group)


def stage(read, flip, grid, target, change, rows, strips):
    parts, total_rows, lanes = grid.shape
    blocks = total_rows // lanes
    per_block = lanes // rows
    for part in range(parts):
        for block in range(blocks):
            tile = jnp.concatenate(
                [read(block * per_block + p, part * lanes) for p in range(per_block)], axis=0
            )
            flip[block, part * lanes : (part + 1) * lanes, :] = tile.T
    for part in range(parts):
        for block in range(blocks):
            tile = flip[block, pl.ds(part, lanes, stride=parts), :]
            grid[part, block * lanes : (block + 1) * lanes, :] = tile.T
    for j in range(rows):
        for part in range(parts):
            target(j, part, change(grid[part, pl.ds(j, strips, stride=rows), :]))


def site_kernel(coef_ref, me_ref, here_ref, beside_ref, own_ref, other_ref, site, pot_ref, sems, flip, grid):
    rows, _, strips, lanes = site.shape
    center = coef_ref[DEGREE + 1]
    me = me_ref[0]
    sources = [here_ref, beside_ref]
    for d in range(2, strips):
        sources.append((own_ref, other_ref)[d & 1].at[(d >> 1) - 1])
    copies = [pltpu.make_async_copy(sources[d], pot_ref.at[me ^ d], sems.at[d]) for d in range(strips)]
    for copy in copies:
        copy.start()
    for copy in copies:
        copy.wait()

    def put_site(j, part, value):
        site[j, part] = value

    stage(
        lambda p, start: pot_ref[p, :, start : start + lanes],
        flip,
        grid,
        put_site,
        lambda level: disorder * (level * (1.0 / (POT_LEVELS - 1)) - 0.5) - center,
        rows,
        strips,
    )


def filter_kernel(coef_ref, vec_ref, site, out_ref, flip, grid, field, state_a, state_b, *, slabs):
    rows, parts, strips, lanes = field.shape
    total_rows = rows * strips
    blocks = total_rows // lanes
    per_block = lanes // rows
    slab_rows = rows // slabs
    top = coef_ref[DEGREE]

    def put_field(j, part, value):
        field[j, part] = value
        state_a[j + 1, part] = top * value
        state_b[j + 1, part] = jnp.zeros_like(value)

    stage(
        lambda p, start: vec_ref[p, :, start : start + lanes],
        flip,
        grid,
        put_field,
        lambda value: value,
        rows,
        strips,
    )

    def wrap(state):
        for part in range(parts):
            state[0, part] = pltpu.roll(state[rows, part], 1, 0)
            state[rows + 1, part] = pltpu.roll(state[1, part], strips - 1, 0)

    def sweep(new, cur, weight, scale):
        def next_column(line):
            return line[1:] + [pltpu.roll(line[0], lanes - 1, 1)]

        def corner(here, below):
            sums = [a + b for a, b in zip(next_column(here), below)]
            return sums, [pltpu.roll(sums[-1], 1, 1)] + sums[:-1]

        def load(j):
            return [cur[j, part] for part in range(parts)]

        here = load(1)
        _, moved = corner(load(0), here)

        for j in range(rows):
            below = load(j + 2)
            sums, moved_next = corner(here, below)
            for part in range(parts):
                image = site[j, part] * here[part] - (sums[part] + moved[part])
                if scale is not None:
                    image = scale * image
                new[j + 1, part] = image + (weight * field[j, part] - new[j + 1, part])
            here, moved = below, moved_next

    square = coef_ref[DEGREE + 2]
    wrap(state_a)

    def two(step, carry):
        order = DEGREE - 1 - 2 * step
        sweep(state_b, state_a, coef_ref[order], square)
        wrap(state_b)
        sweep(state_a, state_b, coef_ref[order - 1], None)
        wrap(state_a)
        return carry

    lax.fori_loop(0, (DEGREE - 2) // 2, two, 0)
    sweep(state_b, state_a, coef_ref[1], square)
    wrap(state_b)
    sweep(state_a, state_b, coef_ref[0], 0.5)

    for j in range(rows):
        for part in range(parts):
            grid[part, pl.ds(j, strips, stride=rows), :] = state_a[j + 1, part]
    for part in range(parts):
        for block in range(blocks):
            flip[block, pl.ds(part, lanes, stride=parts), :] = grid[part, block * lanes : (block + 1) * lanes, :].T
    for part in range(parts):
        for block in range(blocks):
            tile = flip[block, part * lanes : (part + 1) * lanes, :].T
            for p in range(per_block):
                strip = block * per_block + p
                for slab in range(slabs):
                    start = p * rows + slab * slab_rows
                    group = turned(slab, strip, slabs)
                    out_ref[group, strip, :, part * lanes : (part + 1) * lanes] = tile[start : start + slab_rows]


def outer(left, right):
    return lax.dot_general(
        left,
        right,
        (((1,), (1,)), ((), ())),
        precision=lax.Precision.HIGHEST,
        preferred_element_type=jnp.float32,
    )


def gram_kernel(*refs, chunks):
    slab_refs = refs[:chunks]
    place_ref, pot_ref, out_ref, first_ref, low_ref, high_ref = refs[chunks:]
    slab_rows, total, width = low_ref.shape
    columns = slab_refs[0].shape[2]
    acc = jnp.zeros(out_ref.shape, jnp.float32)
    for chunk in range(chunks):
        for group in range(total // (chunks * SUBLANES)):
            here = slice(group * SUBLANES, (group + 1) * SUBLANES)
            start = (group * chunks + chunk) * SUBLANES
            there = slice(start, start + SUBLANES)
            value = jnp.swapaxes(slab_refs[chunk][here], 0, 1)
            low_ref[:, there, :] = value[:, :, :width]
            high_ref[:, there, :] = value[:, :, width:]
            first_ref[there, :] = value[0]

    def line(j):
        return jnp.concatenate([low_ref[j], high_ref[j]], axis=1)

    levels = pot_ref[pl.ds(pl.multiple_of(place_ref[0] * slab_rows, SUBLANES), slab_rows), :]
    for j in range(slab_rows):
        here = line(j)
        level = levels[j : j + 1, :]
        pot = disorder * (level * (1.0 / (POT_LEVELS - 1)) - 0.5)
        image = pot * here - (pltpu.roll(here, 1, 1) + pltpu.roll(here, columns - 1, 1))
        if j < slab_rows - 1:
            image = image - 2.0 * line(j + 1)
        acc = acc + outer(here, jnp.concatenate([here, image], axis=0))
    out_ref[...] = acc


def edge_kernel(next_ref, low_ref, high_ref, out_ref):
    last = jnp.concatenate([low_ref[0], high_ref[0]], axis=1)
    out_ref[...] = -2.0 * outer(last, next_ref[...])


def eliminate(sums):
    total, width = sums.shape
    blocks = total // SUBLANES
    lane = lax.broadcasted_iota(jnp.int32, (SUBLANES, width), 1)
    sublane = lax.broadcasted_iota(jnp.int32, (SUBLANES, width), 0)
    work = []
    for block in range(blocks):
        unit = (lane == sublane + (total + block * SUBLANES)).astype(jnp.float32)
        work.append(jnp.where(lane < total, sums[block * SUBLANES : (block + 1) * SUBLANES], unit))
    for k in range(0, total, 2):
        home, inside = k // SUBLANES, k % SUBLANES

        def column(k):
            return [
                jnp.broadcast_to(work[block][:, k : k + 1], (SUBLANES, width)) for block in range(home, blocks)
            ]

        one, two = column(k), column(k + 1)
        upper, lower = slice(inside, inside + 1), slice(inside + 1, inside + 2)
        inverse = 1.0 / one[0][upper]
        shared = two[0][upper] * inverse
        ratio = one[0][lower] * inverse
        row_one = work[home][upper]
        row_two = work[home][lower] - ratio * row_one
        row_two = row_two * (1.0 / (two[0][lower] - ratio * two[0][upper]))
        row_one = jnp.broadcast_to(row_one * inverse, (SUBLANES, width))
        row_two = jnp.broadcast_to(row_two, (SUBLANES, width))
        for block in range(home, blocks):
            first = one[block - home]
            second = two[block - home] - first * shared
            if block == home:
                first = jnp.where(sublane > inside, first, 0.0)
                second = jnp.where(sublane > inside + 1, second, 0.0)
            work[block] = work[block] - (first * row_one + second * row_two)
    result = []
    for block in range(blocks):
        pivots = jnp.sum(
            jnp.where(lane == sublane + block * SUBLANES, work[block], 0.0), axis=1, keepdims=True
        )
        result.append(work[block] / jnp.sqrt(pivots))
    return jnp.concatenate(result, axis=0)[:, total:]


def products(inv_ref, sources, done_ref, place, scale, targets, half, vec_local):
    first = ((place ^ targets[0]) // half) * half
    weights = scale * inv_ref[pl.ds(pl.multiple_of(first * vec_local, SUBLANES), half * vec_local), :]
    for lines_ref, begin, width, out_refs, at in sources:
        for j in range(lines_ref.shape[0]):
            done_ref[j, :, :width] = jnp.dot(
                weights,
                lines_ref[j, :, begin : begin + width],
                precision=lax.Precision.HIGHEST,
                preferred_element_type=jnp.float32,
            )
        for d, out_ref in zip(targets, out_refs):
            start = ((place ^ d) - first) * vec_local
            for vec in range(0, vec_local, SUBLANES):
                rows = pl.ds(pl.multiple_of(start + vec, SUBLANES), SUBLANES)
                out_ref[vec : vec + SUBLANES, :, at : at + width] = jnp.swapaxes(
                    done_ref[:, rows, :width], 0, 1
                )


def solve_kernel(place_ref, mine_ref, other_ref, low_ref, inv_ref, sums_ref, *rest, **static):
    sums = mine_ref[...] + other_ref[...]
    sums_ref[...] = sums
    inv_ref[...] = eliminate(sums)
    head = rest[0].shape[2]
    products(inv_ref, [(low_ref, 0, head, rest[:-1], 0)], rest[-1], place_ref[0], **static)


def rest_kernel(place_ref, inv_ref, low_ref, high_ref, *rest, **static):
    half, tail = static["half"], rest[0].shape[2]
    sources = [
        (low_ref, low_ref.shape[2] - tail, tail, rest[:half], 0),
        (high_ref, 0, high_ref.shape[2], rest[half : 2 * half], 0),
    ]
    products(inv_ref, sources, rest[-1], place_ref[0], **static)


def near_kernel(place_ref, inv_ref, low_ref, high_ref, *rest, **static):
    low, high = low_ref.shape[2], high_ref.shape[2]
    sources = [(low_ref, 0, low, rest[:-1], 0), (high_ref, 0, high, rest[:-1], low)]
    products(inv_ref, sources, rest[-1], place_ref[0], **static)


def extra_kernel(place_ref, inv_ref, lines_ref, *rest, **static):
    products(inv_ref, [(lines_ref, 0, lines_ref.shape[2], rest[:-1], 0)], rest[-1], place_ref[0], **static)


def held(value):
    return pltpu.with_memory_space_constraint(value, pltpu.VMEM)


def whole_shards(start_vectors, potential, bounds):
    vec_local, rows, columns = start_vectors.shape
    strips = lax.axis_size("strip")
    groups = lax.axis_size("vec")
    both = ("vec", "strip")
    total_vecs = vec_local * groups
    vecs = vec_local // strips
    slab_rows = rows // groups
    devices = strips * groups

    coeffs, center, spread = filter_terms(bounds)
    beta = 2.0 / spread
    odd = jnp.arange(DEGREE + 1) % 2 == 1
    terms = jnp.concatenate([jnp.where(odd, beta, 1.0) * coeffs, center[None], (beta * beta)[None]])
    me = lax.axis_index("strip").astype(jnp.int32)
    level = potential.astype(jnp.float32)

    def swap(value, bit):
        return lax.ppermute(value, "strip", [(i, i ^ bit) for i in range(strips)])

    inner = []

    def spread(vectors, chunk):
        part = vectors[chunk * strips : (chunk + 1) * strips]
        inner.append(lax.all_to_all(part, "strip", split_axis=0, concat_axis=0, tiled=True))

    spread(start_vectors, 0)
    beside = swap(level, 1)
    pieces = [swap(level, bit) for bit in range(2, strips, 2)]
    own_pots = jnp.stack(pieces)
    other_pots = swap(own_pots, 1)
    later, _ = lax.optimization_barrier((start_vectors, own_pots))
    for chunk in range(1, vecs):
        spread(later, chunk)

    parts = columns // LANES
    lattice = (rows, parts, strips, LANES)
    padded = (rows + 2, parts, strips, LANES)
    smem = pl.BlockSpec(memory_space=pltpu.SMEM)
    vmem = pl.BlockSpec(memory_space=pltpu.VMEM)
    hbm = pl.BlockSpec(memory_space=pl.ANY)
    slab_shape = jax.ShapeDtypeStruct((groups, strips, slab_rows, columns), jnp.float32)
    staging = [
        pltpu.VMEM((strips * rows // LANES, columns, LANES), jnp.float32),
        pltpu.VMEM((parts, strips * rows, LANES), jnp.float32),
    ]
    site = pl.pallas_call(
        site_kernel,
        in_specs=[smem, smem] + [hbm] * 4,
        out_specs=vmem,
        out_shape=jax.ShapeDtypeStruct(lattice, jnp.float32),
        scratch_shapes=[
            pltpu.VMEM((strips, rows, columns), jnp.float32),
            pltpu.SemaphoreType.DMA((strips,)),
        ]
        + staging,
        name="site",
    )(terms, me[None], level, beside, own_pots, other_pots)
    slabs = []
    holders = [p * groups + turned(s, p, groups) for p in range(strips) for s in range(groups)]
    ring = [(holders[(g + 1) % devices], holders[g]) for g in range(devices)]
    for chunk in range(vecs):
        done = pl.pallas_call(
            functools.partial(filter_kernel, slabs=groups),
            in_specs=[smem, vmem, vmem],
            out_specs=vmem,
            out_shape=slab_shape,
            scratch_shapes=staging
            + [
                pltpu.VMEM(lattice, jnp.float32),
                pltpu.VMEM(padded, jnp.float32),
                pltpu.VMEM(padded, jnp.float32),
            ],
            name="filter",
        )(terms, held(inner[chunk]), site)
        slab = lax.all_to_all(done.reshape(devices, slab_rows, columns), both, split_axis=0, concat_axis=0, tiled=True)
        slabs.append(slab)

    place = lax.axis_index("vec").astype(jnp.int32)
    width = columns - columns // 4
    low_shape = jax.ShapeDtypeStruct((slab_rows, total_vecs, width), jnp.float32)
    high_shape = jax.ShapeDtypeStruct((slab_rows, total_vecs, columns - width), jnp.float32)
    sums_shape = jax.ShapeDtypeStruct((total_vecs, 2 * total_vecs), jnp.float32)
    sums, first_row, low, high = pl.pallas_call(
        functools.partial(gram_kernel, chunks=vecs),
        in_specs=[vmem] * vecs + [smem, vmem],
        out_specs=[vmem] * 4,
        out_shape=[
            sums_shape,
            jax.ShapeDtypeStruct((total_vecs, columns), jnp.float32),
            low_shape,
            high_shape,
        ],
        name="gram",
    )(*map(held, slabs), turned(place, me, groups)[None], level)
    next_row = lax.ppermute(first_row, ("strip", "vec"), ring)
    half = groups // 2
    middle = (half - 1, half)
    raw = lax.ppermute(high, "vec", [middle, middle[::-1]])
    last_low, last_high = (
        pl.BlockSpec((1, total_vecs, part.shape[2]), lambda i: (slab_rows - 1, 0, 0))
        for part in (low_shape, high_shape)
    )
    edge = pl.pallas_call(
        edge_kernel,
        grid=(1,),
        in_specs=[vmem, last_low, last_high],
        out_specs=vmem,
        out_shape=jax.ShapeDtypeStruct((total_vecs, total_vecs), jnp.float32),
        name="edge",
    )(held(next_row), low, high)

    def pairwise(value, order):
        rounds = [(axis, count, 1 << n) for axis, count in order for n in range(count.bit_length() - 1)]
        for number, (axis, count, bit) in enumerate(rounds):
            other = lax.ppermute(value, axis, [(i, i ^ bit) for i in range(count)])
            if number < len(rounds) - 1:
                value = value + other
        return value, other

    sums, pending = pairwise(sums, (("vec", groups), ("strip", strips)))
    mine, other = pairwise(edge, (("strip", strips),))
    edge = mine + other
    others = []
    for d in range(1, groups):
        others.append(lax.ppermute(edge, "vec", [(i, i ^ d) for i in range(groups)]))
    edge = edge + sum(others)

    static = dict(scale=math.sqrt(strips * rows * columns), half=half, vec_local=vec_local)
    far, near = tuple(range(half, groups)), tuple(range(half))
    piece = jax.ShapeDtypeStruct((vec_local, slab_rows, columns), jnp.float32)
    head = columns // 4
    head_piece = jax.ShapeDtypeStruct((vec_local, slab_rows, head), jnp.float32)
    tail_piece = jax.ShapeDtypeStruct((vec_local, slab_rows, width - head), jnp.float32)
    high_piece = jax.ShapeDtypeStruct((vec_local, slab_rows, columns - width), jnp.float32)
    products_scratch = [pltpu.VMEM((slab_rows, half * vec_local, width), jnp.float32)]
    inverse, gram_cross, *heads = pl.pallas_call(
        functools.partial(solve_kernel, targets=far, **static),
        in_specs=[smem] + [vmem] * 3,
        out_specs=[vmem] * (2 + half),
        out_shape=[jax.ShapeDtypeStruct((total_vecs, total_vecs), jnp.float32), sums_shape]
        + [head_piece] * half,
        scratch_shapes=products_scratch,
        name="solve",
    )(place[None], sums, held(pending), low)
    blocks = pl.pallas_call(
        functools.partial(rest_kernel, targets=far, **static),
        in_specs=[smem] + [vmem] * 3,
        out_specs=[vmem] * (2 * half),
        out_shape=[tail_piece] * half + [high_piece] * half,
        scratch_shapes=products_scratch,
        name="rest",
    )(place[None], inverse, low, high)
    own_block, beside_block = pl.pallas_call(
        functools.partial(near_kernel, targets=near, **static),
        in_specs=[smem] + [vmem] * 3,
        out_specs=[vmem] * half,
        out_shape=[piece] * half,
        scratch_shapes=products_scratch,
        name="near",
    )(place[None], inverse, low, high)
    own_extra, beside_extra = pl.pallas_call(
        functools.partial(extra_kernel, targets=near, **static),
        in_specs=[smem] + [vmem] * 2,
        out_specs=[vmem] * half,
        out_shape=[high_piece] * half,
        scratch_shapes=products_scratch,
        name="extra",
    )(place[None], inverse, held(raw))

    def across(block, d, sources=range(groups)):
        return lax.ppermute(block, "vec", [(i, i ^ d) for i in sources])

    outer_groups = [i for i in range(groups) if i not in middle]
    far_high = [across(block, d, outer_groups) for d, block in zip(far, blocks[half:])]
    far_head = [across(block, d) for d, block in zip(far, heads)]
    far_tail = [across(block, d) for d, block in zip(far, blocks[:half])]
    beside_block = across(beside_block, 1)
    beside_extra = across(beside_extra, 1, middle)
    far_high = [far_high[0] + beside_extra, far_high[1] + own_extra]

    ortho_basis = jnp.zeros((vec_local, rows, columns), jnp.float32)
    for d, block, at in (
        (0, own_block, 0),
        (2, far_head[0], 0),
        (3, far_head[1], 0),
        (2, far_tail[0], head),
        (3, far_tail[1], head),
        (3, far_high[1], width),
        (1, beside_block, 0),
        (2, far_high[0], width),
    ):
        start = turned(place ^ d, me, groups) * slab_rows
        ortho_basis = lax.dynamic_update_slice(ortho_basis, block, (0, start, at))

    cross_half = gram_cross[:, total_vecs:] + edge
    cross_sum = 0.5 * (cross_half + cross_half.T)
    half_done = jnp.dot(inverse, cross_sum, precision=lax.Precision.HIGHEST)
    ritz_matrix = float(rows) * jnp.dot(inverse, half_done.T, precision=lax.Precision.HIGHEST)
    return (ortho_basis, ritz_matrix)


def is_whole(vec_local, rows, columns, strips, groups):
    devices = strips * groups
    return (
        strips == SUBLANES
        and vec_local % strips == 0
        and rows % (groups * SUBLANES) == 0
        and columns % (LANES * SUBLANES) == 0
        and LANES % rows == 0
        and strips * rows % LANES == 0
        and groups == 4
        and devices & (devices - 1) == 0
        and vec_local % SUBLANES == 0
        and 2 * vec_local * groups == LANES
        and DEGREE % 2 == 0
    )


def solution(mesh):
    strips, groups = mesh.shape["strip"], mesh.shape["vec"]
    in_specs = (P("vec", "strip", None), P("strip", None), P())
    out_specs = (P("vec", "strip", None), P())

    def step(start_vectors, potential, bounds):
        total_vecs, total_rows, columns = start_vectors.shape
        vec_local, rows = total_vecs // groups, total_rows // strips
        whole = is_whole(vec_local, rows, columns, strips, groups)

        def form(*local):
            return (whole_shards if whole else halo_shards)(*local)

        sharded = jax.shard_map(form, mesh=mesh, in_specs=in_specs, out_specs=out_specs, check_vma=False)
        return sharded(start_vectors, potential, bounds)

    return step
```

```python
import functools
import math

import jax
import jax.numpy as jnp
from jax import lax
from jax.experimental import pallas as pl
from jax.experimental.pallas import tpu as pltpu
from jax.sharding import PartitionSpec as P

DEGREE = 32
DEPTH = 8
POT_LEVELS = 16
LANES = 128
SUBLANES = 8

grid_unit = 0.0625
disorder = 2.0


def filter_terms(bounds):
    edges = bounds.astype(jnp.float32) * grid_unit
    center = (edges[0] + edges[1]) * 0.5
    spread = (edges[1] - edges[0]) * 0.5
    theta_lo = jnp.arccos((edges[2] - center) / spread)
    theta_hi = jnp.arccos((edges[3] - center) / spread)
    orders = jnp.arange(1, DEGREE + 1).astype(jnp.float32)
    others = 2.0 * (jnp.sin(orders * theta_lo) - jnp.sin(orders * theta_hi)) / (orders * math.pi)
    first = jnp.reshape((theta_lo - theta_hi) / math.pi, (1,))
    return (jnp.concatenate([first, others]), center, spread)


def extended(value, sides, width):
    for axis, dim in sides:
        count, length = (lax.axis_size(axis), value.shape[dim])
        up = [(i, (i + 1) % count) for i in range(count)]
        down = [(j, i) for i, j in up]
        last = lax.slice_in_dim(value, length - width, length, axis=dim)
        leading = lax.slice_in_dim(value, 0, width, axis=dim)
        before = lax.ppermute(last, axis, up)
        after = lax.ppermute(leading, axis, down)
        value = jnp.concatenate([before, value, after], axis=dim)
    return value


def stencil(padded, pot_rows, center, spread):
    middle = padded[:, 1:-1]
    beside = padded[:, 2:] + padded[:, :-2] + jnp.roll(middle, 1, 2) + jnp.roll(middle, -1, 2)
    return ((pot_rows[None] - center) * middle - beside) / spread


def deep_filter(start_vectors, pot_padded, coeffs, center, spread):
    rows = start_vectors.shape[1]

    def one_round(rounds, carry):
        before, current, filtered = carry
        stacked = jnp.stack([before, current])
        padded = extended(stacked, (("strip", 2),), DEPTH)
        old_part = padded[0]
        new_part = padded[1]
        for inner in range(DEPTH):
            counter = rounds * DEPTH + inner
            factor = jnp.where(counter == 0, 1.0, 2.0).astype(jnp.float32)
            pot_rows = pot_padded[inner + 1 : rows + 2 * DEPTH - inner - 1]
            after = factor * stencil(new_part, pot_rows, center, spread) - old_part[:, 1:-1]
            offset = DEPTH - inner - 1
            filtered = filtered + coeffs[counter + 1] * after[:, offset : offset + rows]
            old_part = new_part[:, 1:-1]
            new_part = after
        return (old_part, new_part, filtered)

    initial = (jnp.zeros_like(start_vectors), start_vectors, coeffs[0] * start_vectors)
    return lax.fori_loop(0, DEGREE // DEPTH, one_round, initial)[2]


def halo_shards(start_vectors, potential, bounds):
    _, rows, columns = start_vectors.shape
    pot_field = disorder * (potential.astype(jnp.float32) / (POT_LEVELS - 1) - 0.5)
    coeffs, center, spread = filter_terms(bounds)
    pot_padded = extended(pot_field, (("strip", 0),), DEPTH)
    filtered = deep_filter(start_vectors, pot_padded, coeffs, center, spread)
    padded = extended(filtered, (("strip", 1),), 1)
    applied = stencil(padded, pot_field, 0.0, 1.0)
    slab_vecs, slab_applied = (
        lax.all_to_all(filtered, "vec", split_axis=1, concat_axis=0, tiled=True),
        lax.all_to_all(applied, "vec", split_axis=1, concat_axis=0, tiled=True),
    )
    total_vecs = slab_vecs.shape[0]
    y_rows = slab_vecs.reshape(total_vecs, -1)
    hy_rows = slab_applied.reshape(total_vecs, -1)
    gram_part = jnp.dot(
        y_rows, y_rows.T, precision=lax.Precision.HIGHEST, preferred_element_type=jnp.float32
    )
    cross_part = jnp.dot(
        y_rows, hy_rows.T, precision=lax.Precision.HIGHEST, preferred_element_type=jnp.float32
    )
    gram_sum, cross_sum = lax.psum((gram_part, cross_part), ("strip", "vec"))
    lower_factor = jnp.linalg.cholesky(gram_sum)
    site_count = lax.axis_size("strip") * rows * columns
    ortho = jax.scipy.linalg.solve_triangular(lower_factor, y_rows, lower=True)
    ortho_slab = (math.sqrt(site_count) * ortho).reshape(slab_vecs.shape)
    ortho_basis = lax.all_to_all(ortho_slab, "vec", split_axis=0, concat_axis=1, tiled=True)
    half_done = jax.scipy.linalg.solve_triangular(lower_factor, cross_sum, lower=True)
    ritz_matrix = float(rows) * jax.scipy.linalg.solve_triangular(
        lower_factor, half_done.T, lower=True
    )
    return (ortho_basis, ritz_matrix)


def turned(group, strip, groups):
    odd = strip % 2
    return group + odd * (groups - 1 - 2 * group)


def stage(read, flip, grid, target, change, rows, strips):
    parts, total_rows, lanes = grid.shape
    blocks = total_rows // lanes
    per_block = lanes // rows
    for part in range(parts):
        for block in range(blocks):
            tile = jnp.concatenate(
                [read(block * per_block + p, part * lanes) for p in range(per_block)], axis=0
            )
            flip[block, part * lanes : (part + 1) * lanes, :] = tile.T
    for part in range(parts):
        for block in range(blocks):
            tile = flip[block, pl.ds(part, lanes, stride=parts), :]
            grid[part, block * lanes : (block + 1) * lanes, :] = tile.T
    for j in range(rows):
        for part in range(parts):
            target(j, part, change(grid[part, pl.ds(j, strips, stride=rows), :]))


def site_kernel(coef_ref, me_ref, here_ref, beside_ref, own_ref, other_ref, site, pot_ref, sems, flip, grid):
    rows, _, strips, lanes = site.shape
    center = coef_ref[DEGREE + 1]
    me = me_ref[0]
    sources = [here_ref, beside_ref]
    for d in range(2, strips):
        sources.append((own_ref, other_ref)[d & 1].at[(d >> 1) - 1])
    copies = [pltpu.make_async_copy(sources[d], pot_ref.at[me ^ d], sems.at[d]) for d in range(strips)]
    for copy in copies:
        copy.start()
    for copy in copies:
        copy.wait()

    def put_site(j, part, value):
        site[j, part] = value

    stage(
        lambda p, start: pot_ref[p, :, start : start + lanes],
        flip,
        grid,
        put_site,
        lambda level: disorder * (level * (1.0 / (POT_LEVELS - 1)) - 0.5) - center,
        rows,
        strips,
    )


def filter_kernel(coef_ref, vec_ref, site, out_ref, flip, grid, field, state_a, state_b, *, slabs):
    rows, parts, strips, lanes = field.shape
    total_rows = rows * strips
    blocks = total_rows // lanes
    per_block = lanes // rows
    slab_rows = rows // slabs
    top = coef_ref[DEGREE]

    def put_field(j, part, value):
        field[j, part] = value
        state_a[j + 1, part] = top * value
        state_b[j + 1, part] = jnp.zeros_like(value)

    stage(
        lambda p, start: vec_ref[p, :, start : start + lanes],
        flip,
        grid,
        put_field,
        lambda value: value,
        rows,
        strips,
    )

    def wrap(state):
        for part in range(parts):
            state[0, part] = pltpu.roll(state[rows, part], 1, 0)
            state[rows + 1, part] = pltpu.roll(state[1, part], strips - 1, 0)

    def sweep(new, cur, weight, scale):
        def next_column(line):
            return line[1:] + [pltpu.roll(line[0], lanes - 1, 1)]

        def corner(here, below):
            sums = [a + b for a, b in zip(next_column(here), below)]
            return sums, [pltpu.roll(sums[-1], 1, 1)] + sums[:-1]

        def load(j):
            return [cur[j, part] for part in range(parts)]

        here = load(1)
        _, moved = corner(load(0), here)

        for j in range(rows):
            below = load(j + 2)
            sums, moved_next = corner(here, below)
            for part in range(parts):
                image = site[j, part] * here[part] - (sums[part] + moved[part])
                if scale is not None:
                    image = scale * image
                new[j + 1, part] = image + (weight * field[j, part] - new[j + 1, part])
            here, moved = below, moved_next

    square = coef_ref[DEGREE + 2]
    wrap(state_a)

    def two(step, carry):
        order = DEGREE - 1 - 2 * step
        sweep(state_b, state_a, coef_ref[order], square)
        wrap(state_b)
        sweep(state_a, state_b, coef_ref[order - 1], None)
        wrap(state_a)
        return carry

    lax.fori_loop(0, (DEGREE - 2) // 2, two, 0)
    sweep(state_b, state_a, coef_ref[1], square)
    wrap(state_b)
    sweep(state_a, state_b, coef_ref[0], 0.5)

    for j in range(rows):
        for part in range(parts):
            grid[part, pl.ds(j, strips, stride=rows), :] = state_a[j + 1, part]
    for part in range(parts):
        for block in range(blocks):
            flip[block, pl.ds(part, lanes, stride=parts), :] = grid[part, block * lanes : (block + 1) * lanes, :].T
    for part in range(parts):
        for block in range(blocks):
            tile = flip[block, part * lanes : (part + 1) * lanes, :].T
            for p in range(per_block):
                strip = block * per_block + p
                for slab in range(slabs):
                    start = p * rows + slab * slab_rows
                    group = turned(slab, strip, slabs)
                    out_ref[group, strip, :, part * lanes : (part + 1) * lanes] = tile[start : start + slab_rows]


def outer(left, right):
    return lax.dot_general(
        left,
        right,
        (((1,), (1,)), ((), ())),
        precision=lax.Precision.HIGHEST,
        preferred_element_type=jnp.float32,
    )


def gram_kernel(*refs, chunks):
    slab_refs = refs[:chunks]
    place_ref, pot_ref, out_ref, first_ref, low_ref, high_ref = refs[chunks:]
    slab_rows, total, width = low_ref.shape
    columns = slab_refs[0].shape[2]
    acc = jnp.zeros(out_ref.shape, jnp.float32)
    for chunk in range(chunks):
        for group in range(total // (chunks * SUBLANES)):
            here = slice(group * SUBLANES, (group + 1) * SUBLANES)
            start = (group * chunks + chunk) * SUBLANES
            there = slice(start, start + SUBLANES)
            value = jnp.swapaxes(slab_refs[chunk][here], 0, 1)
            low_ref[:, there, :] = value[:, :, :width]
            high_ref[:, there, :] = value[:, :, width:]
            first_ref[there, :] = value[0]

    def line(j):
        return jnp.concatenate([low_ref[j], high_ref[j]], axis=1)

    levels = pot_ref[pl.ds(pl.multiple_of(place_ref[0] * slab_rows, SUBLANES), slab_rows), :]
    for j in range(slab_rows):
        here = line(j)
        level = levels[j : j + 1, :]
        pot = disorder * (level * (1.0 / (POT_LEVELS - 1)) - 0.5)
        image = pot * here - (pltpu.roll(here, 1, 1) + pltpu.roll(here, columns - 1, 1))
        if j < slab_rows - 1:
            image = image - 2.0 * line(j + 1)
        acc = acc + outer(here, jnp.concatenate([here, image], axis=0))
    out_ref[...] = acc


def edge_kernel(next_ref, low_ref, high_ref, out_ref):
    last = jnp.concatenate([low_ref[0], high_ref[0]], axis=1)
    out_ref[...] = -2.0 * outer(last, next_ref[...])


def eliminate(sums):
    total, width = sums.shape
    blocks = total // SUBLANES
    lane = lax.broadcasted_iota(jnp.int32, (SUBLANES, width), 1)
    sublane = lax.broadcasted_iota(jnp.int32, (SUBLANES, width), 0)
    work = []
    for block in range(blocks):
        unit = (lane == sublane + (total + block * SUBLANES)).astype(jnp.float32)
        work.append(jnp.where(lane < total, sums[block * SUBLANES : (block + 1) * SUBLANES], unit))
    for k in range(0, total, 2):
        home, inside = k // SUBLANES, k % SUBLANES

        def column(k):
            return [
                jnp.broadcast_to(work[block][:, k : k + 1], (SUBLANES, width)) for block in range(home, blocks)
            ]

        one, two = column(k), column(k + 1)
        upper, lower = slice(inside, inside + 1), slice(inside + 1, inside + 2)
        inverse = 1.0 / one[0][upper]
        shared = two[0][upper] * inverse
        ratio = one[0][lower] * inverse
        row_one = work[home][upper]
        row_two = work[home][lower] - ratio * row_one
        row_two = row_two * (1.0 / (two[0][lower] - ratio * two[0][upper]))
        row_one = jnp.broadcast_to(row_one * inverse, (SUBLANES, width))
        row_two = jnp.broadcast_to(row_two, (SUBLANES, width))
        for block in range(home, blocks):
            first = one[block - home]
            second = two[block - home] - first * shared
            if block == home:
                first = jnp.where(sublane > inside, first, 0.0)
                second = jnp.where(sublane > inside + 1, second, 0.0)
            work[block] = work[block] - (first * row_one + second * row_two)
    result = []
    for block in range(blocks):
        pivots = jnp.sum(
            jnp.where(lane == sublane + block * SUBLANES, work[block], 0.0), axis=1, keepdims=True
        )
        result.append(work[block] / jnp.sqrt(pivots))
    return jnp.concatenate(result, axis=0)[:, total:]


def products(inv_ref, sources, done_ref, place, scale, targets, half, vec_local):
    first = ((place ^ targets[0]) // half) * half
    weights = scale * inv_ref[pl.ds(pl.multiple_of(first * vec_local, SUBLANES), half * vec_local), :]
    for lines_ref, begin, width, out_refs, at in sources:
        for j in range(lines_ref.shape[0]):
            done_ref[j, :, :width] = jnp.dot(
                weights,
                lines_ref[j, :, begin : begin + width],
                precision=lax.Precision.HIGHEST,
                preferred_element_type=jnp.float32,
            )
        for d, out_ref in zip(targets, out_refs):
            start = ((place ^ d) - first) * vec_local
            for vec in range(0, vec_local, SUBLANES):
                rows = pl.ds(pl.multiple_of(start + vec, SUBLANES), SUBLANES)
                out_ref[vec : vec + SUBLANES, :, at : at + width] = jnp.swapaxes(
                    done_ref[:, rows, :width], 0, 1
                )


def solve_kernel(place_ref, mine_ref, other_ref, low_ref, inv_ref, sums_ref, *rest, **static):
    sums = mine_ref[...] + other_ref[...]
    sums_ref[...] = sums
    inv_ref[...] = eliminate(sums)
    head = rest[0].shape[2]
    products(inv_ref, [(low_ref, 0, head, rest[:-1], 0)], rest[-1], place_ref[0], **static)


def rest_kernel(place_ref, inv_ref, low_ref, high_ref, *rest, **static):
    half, tail = static["half"], rest[0].shape[2]
    sources = [
        (low_ref, low_ref.shape[2] - tail, tail, rest[:half], 0),
        (high_ref, 0, high_ref.shape[2], rest[half : 2 * half], 0),
    ]
    products(inv_ref, sources, rest[-1], place_ref[0], **static)


def near_kernel(place_ref, inv_ref, low_ref, high_ref, *rest, **static):
    low, high = low_ref.shape[2], high_ref.shape[2]
    sources = [(low_ref, 0, low, rest[:-1], 0), (high_ref, 0, high, rest[:-1], low)]
    products(inv_ref, sources, rest[-1], place_ref[0], **static)


def extra_kernel(place_ref, inv_ref, lines_ref, *rest, **static):
    products(inv_ref, [(lines_ref, 0, lines_ref.shape[2], rest[:-1], 0)], rest[-1], place_ref[0], **static)


def held(value):
    return pltpu.with_memory_space_constraint(value, pltpu.VMEM)


def whole_shards(start_vectors, potential, bounds):
    vec_local, rows, columns = start_vectors.shape
    strips = lax.axis_size("strip")
    groups = lax.axis_size("vec")
    both = ("vec", "strip")
    total_vecs = vec_local * groups
    vecs = vec_local // strips
    slab_rows = rows // groups
    devices = strips * groups

    coeffs, center, spread = filter_terms(bounds)
    beta = 2.0 / spread
    odd = jnp.arange(DEGREE + 1) % 2 == 1
    terms = jnp.concatenate([jnp.where(odd, beta, 1.0) * coeffs, center[None], (beta * beta)[None]])
    me = lax.axis_index("strip").astype(jnp.int32)
    level = potential.astype(jnp.float32)

    def swap(value, bit):
        return lax.ppermute(value, "strip", [(i, i ^ bit) for i in range(strips)])

    inner = []

    def spread(vectors, chunk):
        part = vectors[chunk * strips : (chunk + 1) * strips]
        inner.append(lax.all_to_all(part, "strip", split_axis=0, concat_axis=0, tiled=True))

    spread(start_vectors, 0)
    beside = swap(level, 1)
    pieces = [swap(level, bit) for bit in range(2, strips, 2)]
    own_pots = jnp.stack(pieces)
    other_pots = swap(own_pots, 1)
    later, _ = lax.optimization_barrier((start_vectors, own_pots))
    for chunk in range(1, vecs):
        spread(later, chunk)

    parts = columns // LANES
    lattice = (rows, parts, strips, LANES)
    padded = (rows + 2, parts, strips, LANES)
    smem = pl.BlockSpec(memory_space=pltpu.SMEM)
    vmem = pl.BlockSpec(memory_space=pltpu.VMEM)
    hbm = pl.BlockSpec(memory_space=pl.ANY)
    slab_shape = jax.ShapeDtypeStruct((groups, strips, slab_rows, columns), jnp.float32)
    staging = [
        pltpu.VMEM((strips * rows // LANES, columns, LANES), jnp.float32),
        pltpu.VMEM((parts, strips * rows, LANES), jnp.float32),
    ]
    site = pl.pallas_call(
        site_kernel,
        in_specs=[smem, smem] + [hbm] * 4,
        out_specs=vmem,
        out_shape=jax.ShapeDtypeStruct(lattice, jnp.float32),
        scratch_shapes=[
            pltpu.VMEM((strips, rows, columns), jnp.float32),
            pltpu.SemaphoreType.DMA((strips,)),
        ]
        + staging,
        name="site",
    )(terms, me[None], level, beside, own_pots, other_pots)
    slabs = []
    holders = [p * groups + turned(s, p, groups) for p in range(strips) for s in range(groups)]
    ring = [(holders[(g + 1) % devices], holders[g]) for g in range(devices)]
    for chunk in range(vecs):
        done = pl.pallas_call(
            functools.partial(filter_kernel, slabs=groups),
            in_specs=[smem, vmem, vmem],
            out_specs=vmem,
            out_shape=slab_shape,
            scratch_shapes=staging
            + [
                pltpu.VMEM(lattice, jnp.float32),
                pltpu.VMEM(padded, jnp.float32),
                pltpu.VMEM(padded, jnp.float32),
            ],
            name="filter",
        )(terms, held(inner[chunk]), site)
        slab = lax.all_to_all(done.reshape(devices, slab_rows, columns), both, split_axis=0, concat_axis=0, tiled=True)
        slabs.append(slab)

    place = lax.axis_index("vec").astype(jnp.int32)
    width = columns - columns // 4
    low_shape = jax.ShapeDtypeStruct((slab_rows, total_vecs, width), jnp.float32)
    high_shape = jax.ShapeDtypeStruct((slab_rows, total_vecs, columns - width), jnp.float32)
    sums_shape = jax.ShapeDtypeStruct((total_vecs, 2 * total_vecs), jnp.float32)
    sums, first_row, low, high = pl.pallas_call(
        functools.partial(gram_kernel, chunks=vecs),
        in_specs=[vmem] * vecs + [smem, vmem],
        out_specs=[vmem] * 4,
        out_shape=[
            sums_shape,
            jax.ShapeDtypeStruct((total_vecs, columns), jnp.float32),
            low_shape,
            high_shape,
        ],
        name="gram",
    )(*map(held, slabs), turned(place, me, groups)[None], level)
    next_row = lax.ppermute(first_row, ("strip", "vec"), ring)
    half = groups // 2
    middle = (half - 1, half)
    raw = lax.ppermute(high, "vec", [middle, middle[::-1]])
    last_low, last_high = (
        pl.BlockSpec((1, total_vecs, part.shape[2]), lambda i: (slab_rows - 1, 0, 0))
        for part in (low_shape, high_shape)
    )
    edge = pl.pallas_call(
        edge_kernel,
        grid=(1,),
        in_specs=[vmem, last_low, last_high],
        out_specs=vmem,
        out_shape=jax.ShapeDtypeStruct((total_vecs, total_vecs), jnp.float32),
        name="edge",
    )(held(next_row), low, high)

    def pairwise(value, order):
        rounds = [(axis, count, 1 << n) for axis, count in order for n in range(count.bit_length() - 1)]
        for number, (axis, count, bit) in enumerate(rounds):
            other = lax.ppermute(value, axis, [(i, i ^ bit) for i in range(count)])
            if number < len(rounds) - 1:
                value = value + other
        return value, other

    sums, pending = pairwise(sums, (("vec", groups), ("strip", strips)))
    mine, other = pairwise(edge, (("strip", strips),))
    edge = mine + other
    others = []
    for d in range(1, groups):
        others.append(lax.ppermute(edge, "vec", [(i, i ^ d) for i in range(groups)]))
    edge = edge + sum(others)

    static = dict(scale=math.sqrt(strips * rows * columns), half=half, vec_local=vec_local)
    far, near = tuple(range(half, groups)), tuple(range(half))
    piece = jax.ShapeDtypeStruct((vec_local, slab_rows, columns), jnp.float32)
    head = columns // 4
    head_piece = jax.ShapeDtypeStruct((vec_local, slab_rows, head), jnp.float32)
    tail_piece = jax.ShapeDtypeStruct((vec_local, slab_rows, width - head), jnp.float32)
    high_piece = jax.ShapeDtypeStruct((vec_local, slab_rows, columns - width), jnp.float32)
    products_scratch = [pltpu.VMEM((slab_rows, half * vec_local, width), jnp.float32)]
    inverse, gram_cross, *heads = pl.pallas_call(
        functools.partial(solve_kernel, targets=far, **static),
        in_specs=[smem] + [vmem] * 3,
        out_specs=[vmem] * (2 + half),
        out_shape=[jax.ShapeDtypeStruct((total_vecs, total_vecs), jnp.float32), sums_shape]
        + [head_piece] * half,
        scratch_shapes=products_scratch,
        name="solve",
    )(place[None], sums, held(pending), held(low))
    blocks = pl.pallas_call(
        functools.partial(rest_kernel, targets=far, **static),
        in_specs=[smem] + [vmem] * 3,
        out_specs=[vmem] * (2 * half),
        out_shape=[tail_piece] * half + [high_piece] * half,
        scratch_shapes=products_scratch,
        name="rest",
    )(place[None], inverse, held(low), held(high))
    own_block, beside_block = pl.pallas_call(
        functools.partial(near_kernel, targets=near, **static),
        in_specs=[smem] + [vmem] * 3,
        out_specs=[vmem] * half,
        out_shape=[piece] * half,
        scratch_shapes=products_scratch,
        name="near",
    )(place[None], inverse, held(low), held(high))
    own_extra, beside_extra = pl.pallas_call(
        functools.partial(extra_kernel, targets=near, **static),
        in_specs=[smem] + [vmem] * 2,
        out_specs=[vmem] * half,
        out_shape=[high_piece] * half,
        scratch_shapes=products_scratch,
        name="extra",
    )(place[None], inverse, held(raw))

    def across(block, d, sources=range(groups)):
        return lax.ppermute(block, "vec", [(i, i ^ d) for i in sources])

    outer_groups = [i for i in range(groups) if i not in middle]
    far_high = [across(block, d, outer_groups) for d, block in zip(far, blocks[half:])]
    far_head = [across(block, d) for d, block in zip(far, heads)]
    far_tail = [across(block, d) for d, block in zip(far, blocks[:half])]
    beside_block = across(beside_block, 1)
    beside_extra = across(beside_extra, 1, middle)
    far_high = [far_high[0] + beside_extra, far_high[1] + own_extra]

    ortho_basis = jnp.zeros((vec_local, rows, columns), jnp.float32)
    for d, block, at in (
        (0, own_block, 0),
        (2, far_head[0], 0),
        (3, far_head[1], 0),
        (2, far_tail[0], head),
        (3, far_tail[1], head),
        (3, far_high[1], width),
        (1, beside_block, 0),
        (2, far_high[0], width),
    ):
        start = turned(place ^ d, me, groups) * slab_rows
        ortho_basis = lax.dynamic_update_slice(ortho_basis, block, (0, start, at))

    cross_half = gram_cross[:, total_vecs:] + edge
    cross_sum = 0.5 * (cross_half + cross_half.T)
    half_done = jnp.dot(inverse, cross_sum, precision=lax.Precision.HIGHEST)
    ritz_matrix = float(rows) * jnp.dot(inverse, half_done.T, precision=lax.Precision.HIGHEST)
    return (ortho_basis, ritz_matrix)


def is_whole(vec_local, rows, columns, strips, groups):
    devices = strips * groups
    return (
        strips == SUBLANES
        and vec_local % strips == 0
        and rows % (groups * SUBLANES) == 0
        and columns % (LANES * SUBLANES) == 0
        and LANES % rows == 0
        and strips * rows % LANES == 0
        and groups == 4
        and devices & (devices - 1) == 0
        and vec_local % SUBLANES == 0
        and 2 * vec_local * groups == LANES
        and DEGREE % 2 == 0
    )


def solution(mesh):
    strips, groups = mesh.shape["strip"], mesh.shape["vec"]
    in_specs = (P("vec", "strip", None), P("strip", None), P())
    out_specs = (P("vec", "strip", None), P())

    def step(start_vectors, potential, bounds):
        total_vecs, total_rows, columns = start_vectors.shape
        vec_local, rows = total_vecs // groups, total_rows // strips
        whole = is_whole(vec_local, rows, columns, strips, groups)

        def form(*local):
            return (whole_shards if whole else halo_shards)(*local)

        sharded = jax.shard_map(form, mesh=mesh, in_specs=in_specs, out_specs=out_specs, check_vma=False)
        return sharded(start_vectors, potential, bounds)

    return step
```
